32 devices in a mesh: domain: 8 (over y, x, core), band: 4 (over z).
Axes of the slice: x: 2, y: 2, z: 4, core: 2. Of those that a mesh axis runs over, the one named last changes fastest.
Arguments:
- psi: float32 [4, 48, 32, 128], P('band', 'domain'), may hold values from -6 to 6
- potential: float32 [48, 32, 128], P('domain', 'band'), may hold values from -2 to 2
- projectors: float32 [8, 8, 2, 8, 1024], P('domain'), may hold values from -0.1875 to 0.1875
- offsets: int32 [8, 8, 2], P('domain'), may hold values from 0 to 184
- intersection: int32 [8, 8, 2], P('domain'), may hold values from -1 to 31, as said below
- dmat: float32 [256, 8, 8], P('domain'), may hold values from -9 to 9
Outputs:
- filtered: float32 [4, 48, 32, 128], P('band', 'domain')
The draws below stay inside these ranges and needn't reach their ends.
Inputs may be any that keep to these rules, and one draw needn't show every extreme that they name: intersection[s, d, k] is -1 for an empty slot, else the index among the 32 atoms owned by domain device d of an atom whose projector reaches into domain device s's block; in every draw some owner d receives all 2 slots live from every source s. `offsets`: footprints are whole runs of 8 tiles inside the source block and may intersection one another.
All inputs are finite; a program needn't handle non-finite values.
Results may differ from the reference program's by a relative error of at most 0.00022.
Values sent between devices are 32-bit elements; how exact they have to be, the bound alone decides.
No kernel may reach another device: no remote copies, remote signals or barrier semaphores. Data moves between devices by JAX's collectives and lax.ppermute only.
A program may use at most 64 MiB of HBM per device.

```python
import jax
import jax.numpy as jnp
from jax import lax

CX = 6
NY = 32
NZ = 128
NPROJ = 8
FOOT = 8
CAP = 2
ATOM_DEV = 32
DEGREE = 4
NX = 48
STATES = 4
ATOMS = 256
N_DOMAIN = 8


def draw_intersection(key, part):
    key_atoms, key_live, key_full = jax.random.split(jax.random.fold_in(key, 7), 3)
    atoms = jax.random.randint(key_atoms, (N_DOMAIN, N_DOMAIN, CAP), 0, ATOM_DEV)
    live_slots = jax.random.randint(key_live, (N_DOMAIN, N_DOMAIN, CAP), 0, 2)
    full_owner = jax.random.randint(key_full, (), 0, N_DOMAIN)
    owners = jnp.arange(N_DOMAIN)[None, :, None]
    live_slots = jnp.where(owners == full_owner, 1, live_slots)
    return jnp.where(live_slots == 1, atoms, -1).astype(jnp.int32)


def place_ends(array, own_key, low, high):
    spot = [jax.random.randint(jax.random.fold_in(own_key, axis), (), 0, length) for axis, length in enumerate(array.shape)]
    main_axis = array.shape.index(max(array.shape))
    beside = spot[:main_axis] + [(spot[main_axis] + 1) % array.shape[main_axis]] + spot[main_axis + 1:]
    return array.at[tuple(spot)].set(low).at[tuple(beside)].set(high)


def steps_of(rng, shape, cuts, low, high):
    def one(position, shards_of):
        draws = jax.random.uniform(jax.random.fold_in(jax.random.fold_in(rng, 6), position), (shards_of,), jnp.float32, low / len(cuts), high / len(cuts))
        return jnp.repeat(jnp.exp(draws), shape[position] // shards_of).reshape((-1,) + (1,) * (len(shape) - position - 1))

    level = one(*cuts[0])
    for cut in cuts[1:]:
        level = level * one(*cut)
    return level


def scatter_about(key, dims, deviation, limit, pieces=(), kind=jnp.bfloat16):
    factor_of = steps_of(key, dims, pieces, -0.22, 0.18) if pieces else 1.0
    entries = jax.random.normal(key, dims, jnp.float32) * deviation * factor_of
    return jnp.minimum(jnp.maximum(entries, -limit), limit).astype(kind)


def setup_inputs(seed: int = 0) -> dict:
    key_list = jax.random.split(jax.random.key(seed), 7)
    return {
        "psi": scatter_about(key_list[0], (STATES, NX, NY, NZ), 1.0, 6.0, ((0, 4), (1, 8)), jnp.float32),
        "potential": jnp.clip(jax.random.uniform(key_list[1], (NX, NY, NZ), jnp.float32, -2.0, 2.0) * steps_of(key_list[1], (NX, NY, NZ), ((0, 8), (1, 4)), -0.4, 0.0), -2.0, 2.0),
        "projectors": scatter_about(key_list[2], (N_DOMAIN, N_DOMAIN, CAP, NPROJ, FOOT * 128), (FOOT * 128) ** -0.5, 0.1875, ((0, 8),), jnp.float32),
        "offsets": place_ends(jax.random.randint(key_list[3], (N_DOMAIN, N_DOMAIN, CAP), 0, CX * NY * NZ // 128 - FOOT + 1), jax.random.fold_in(key_list[3], 1), 0, (CX * NY * NZ // 128 - FOOT + 1) - 1).astype(jnp.int32),
        "intersection": draw_intersection(jax.random.fold_in(key_list[6], 71), 0),
        "dmat": scatter_about(key_list[5], (ATOMS, NPROJ, NPROJ), 1.5, 9.0, ((0, 8),), jnp.float32),
    }


stencil_weights = (-5369.0 / 1800.0, 12.0 / 7.0, -15.0 / 56.0, 10.0 / 189.0, -1.0 / 112.0, 2.0 / 1925.0, -1.0 / 16632.0)
filter_center = 6.0
filter_half_width = 4.0
highest = lax.Precision.HIGHEST


def kinetic(grid_field):
    reach_cells = len(stencil_weights) - 1
    planes = grid_field.shape[0]
    padded = jnp.pad(grid_field, ((reach_cells, reach_cells), (0, 0), (0, 0)))
    summed = 3.0 * stencil_weights[0] * grid_field
    for distance in range(1, reach_cells + 1):
        beside_all = padded[reach_cells + distance:reach_cells + distance + planes] + padded[reach_cells - distance:reach_cells - distance + planes]
        beside_all = beside_all + jnp.roll(grid_field, distance, 1) + jnp.roll(grid_field, -distance, 1)
        beside_all = beside_all + jnp.roll(grid_field, distance, 2) + jnp.roll(grid_field, -distance, 2)
        summed = summed + stencil_weights[distance] * beside_all
    return -0.5 * summed


def nonlocal_part(grid_field, projectors, offsets, intersection, dmat):
    tiles_all = grid_field.reshape(N_DOMAIN, -1, 128)
    tile_index = offsets[..., None] + jnp.arange(FOOT, dtype=jnp.int32)
    gathered = jax.vmap(lambda tiles, where_at: tiles[where_at])(tiles_all, tile_index)
    gathered = gathered.reshape(N_DOMAIN, N_DOMAIN, CAP, FOOT * 128)
    live_slots = (intersection >= 0).astype(jnp.float32)
    partial_value = jnp.einsum('sdkil,sdkl->sdki', projectors, gathered, precision=highest) * live_slots[..., None]
    one_hot = (intersection[..., None] == jnp.arange(ATOM_DEV, dtype=jnp.int32)).astype(jnp.float32)
    coefficient = jnp.einsum('sdka,sdki->dai', one_hot, partial_value, precision=highest)
    coupling = dmat.reshape(N_DOMAIN, ATOM_DEV, NPROJ, NPROJ)
    applied = jnp.einsum('daij,daj->dai', coupling, coefficient, precision=highest)
    returned = jnp.einsum('sdka,dai->sdki', one_hot, applied, precision=highest)
    contrib = jnp.einsum('sdkil,sdki->sdkl', projectors, returned, precision=highest)
    contrib = contrib.reshape(N_DOMAIN, N_DOMAIN * CAP * FOOT, 128)
    flat_index = tile_index.reshape(N_DOMAIN, -1)
    added = jax.vmap(lambda tiles, where_at, extra: tiles.at[where_at].add(extra))(jnp.zeros_like(tiles_all), flat_index, contrib)
    return added.reshape(grid_field.shape)


def reference(psi, potential, projectors, offsets, intersection, dmat):
    def hamiltonian(grid_field):
        return kinetic(grid_field) + potential * grid_field + nonlocal_part(grid_field, projectors, offsets, intersection, dmat)

    def one_state(state):
        previous = state
        current = (hamiltonian(state) - filter_center * state) / filter_half_width
        for degree in range(1, DEGREE):
            following = 2.0 * (hamiltonian(current) - filter_center * current) / filter_half_width - previous
            previous, current = current, following
        return current

    return lax.map(one_state, psi)
```

```python
import functools

import jax
import jax.numpy as jnp
from jax import lax
from jax.experimental import pallas as pl
from jax.experimental.pallas import tpu as pltpu
from jax.sharding import PartitionSpec as P

DEGREE = 4

stencil_weights = (
    -5369.0 / 1800.0,
    12.0 / 7.0,
    -15.0 / 56.0,
    10.0 / 189.0,
    -1.0 / 112.0,
    2.0 / 1925.0,
    -1.0 / 16632.0,
)
reach = len(stencil_weights) - 1
filter_center = 6.0
filter_half_width = 4.0
highest = lax.Precision.HIGHEST
f32 = jnp.float32
VMEM = pl.BlockSpec(memory_space=pltpu.VMEM)
SMEM = pl.BlockSpec(memory_space=pltpu.SMEM)


def iota(shape, dim):
    return lax.broadcasted_iota(jnp.int32, shape, dim)


def partials(y_ref, p_ref, off_ref, r_ref, dims):
    n, cap, nproj, foot, chunk = dims
    for slot in range(n * cap):
        start = off_ref[slot % cap, slot // cap]
        rows = pl.ds(slot * nproj, nproj)
        total = None
        for tile in range(foot):
            cells = jnp.broadcast_to(y_ref[pl.ds(start + tile, 1), :], (nproj, 128))
            term = p_ref[rows, tile * 128 : (tile + 1) * 128] * cells
            total = term if total is None else total + term
        r_ref[rows, :] = total
    return lax.dot_general(
        jnp.ones((8, 128), f32),
        r_ref[...],
        (((1,), (1,)), ((), ())),
        precision=highest,
        preferred_element_type=f32,
    )


def by_owner(rows, n, chunk):
    lanes = n * chunk
    shape = (n, lanes)
    ahead = (iota(shape, 1) // chunk - iota(shape, 0) + n) % n
    out = rows
    for step in range(1, n):
        moved = pltpu.roll(rows, n - step, 0)
        moved = pltpu.roll(moved, step * chunk, 1)
        out = jnp.where(ahead == step, moved, out)
    return out


def start_kernel(dims, y_ref, p_ref, off_ref, atom_ref, dmat_ref, out_ref, r_ref):
    n, cap, nproj, foot, chunk = dims
    lanes = n * chunk
    out_ref[:, 0, :] = jnp.broadcast_to(
        partials(y_ref, p_ref, off_ref, r_ref, dims)[0:1], (n, lanes)
    )
    lane = iota((1, lanes), 1) // nproj
    atoms = jnp.zeros((1, lanes), f32)
    for slot in range(n * cap):
        value = atom_ref[slot % cap, slot // cap].astype(f32)
        atoms = jnp.where(lane == slot, value, atoms)
    out_ref[:, 1, :] = jnp.broadcast_to(atoms, (n, lanes))
    count = dmat_ref.shape[1]
    for group in range(128 // count):
        block = dmat_ref[group * 2 * nproj : (group + 1) * 2 * nproj, :]
        for peer in range(n):
            out_ref[peer, 8:, group * count : (group + 1) * count] = block


def step_kernel(dims, nband, first, last, *refs):
    n, cap, nproj, foot, chunk = dims
    refs = list(refs)
    take = lambda: refs.pop(0)
    info_ref, off_ref = take(), take()
    y_ref, a_ref, b_ref, got_ref, p_ref = take(), take(), take(), take(), take()
    if first:
        atom_ref = take()
        v_pieces = [take() for _ in range(nband)]
        prev_ref = None
    else:
        prev_ref, v_ref, w_ref = take(), take(), take()
    out_ref = take()
    if not last:
        c_ref = take()
    if first:
        v_ref, w_ref = take(), take()
    pad_ref, lo_ref, hi_ref, r_ref = take(), take(), take(), take()
    cells = y_ref.shape[0]
    ny = 32
    planes = cells // ny
    lanes = n * chunk
    weights = stencil_weights

    if first:
        if nband > 1:
            piece_rows = ny // nband
            for back, piece in enumerate(v_pieces):
                at = lax.rem(info_ref[1] - back + nband, nband) * piece_rows
                for plane in range(planes):
                    spot = pl.multiple_of(plane * ny + at, 8)
                    v_ref[pl.ds(spot, piece_rows), :] = piece[
                        plane * piece_rows : (plane + 1) * piece_rows, :
                    ]
        else:
            v_ref[...] = v_pieces[0][...]
        atoms = by_owner(got_ref[:, 1, :], n, chunk)
        row = iota((chunk, 128), 0)
        column = iota((chunk, 128), 1)
        count = 128 // (nproj // 2)
        parity = (iota((chunk, 2 * nproj), 1) // nproj) == (iota((chunk, 2 * nproj), 0) % 2)
        spread = (iota((2 * nproj, lanes), 1) % nproj == iota((2 * nproj, lanes), 0) % nproj)
        spread = spread.astype(f32)
        for owner in range(n):
            mine = jnp.zeros((chunk, 128), jnp.int32)
            for k in range(cap):
                mine = jnp.where(row // nproj == k, atom_ref[k, owner], mine)
            pick = (column == (row % nproj) // 2 * count + mine) & (mine >= 0)
            entries = lax.dot_general(
                pick.astype(f32),
                got_ref[owner, 8:, 0:128],
                (((1,), (1,)), ((), ())),
                precision=highest,
                preferred_element_type=f32,
            )
            entries = jnp.where(parity, entries, 0.0)
            block = jnp.dot(entries, spread, precision=highest, preferred_element_type=f32)
            mine_row = jnp.zeros((chunk, lanes), f32)
            row_wide = iota((chunk, lanes), 0) // nproj
            for k in range(cap):
                mine_row = jnp.where(row_wide == k, atom_ref[k, owner].astype(f32), mine_row)
            same = (atoms[owner : owner + 1, :] == mine_row) & (mine_row >= 0.0)
            w_ref[pl.ds(owner * chunk, chunk), :] = jnp.where(same, block, 0.0)
        coefficients = by_owner(got_ref[:, 0, :], n, chunk)
    else:
        coefficients = by_owner(got_ref[...], n, chunk)

    odd = jnp.full((cells, 128), info_ref[0], jnp.int32) == 1
    from_a, from_b = a_ref[...], b_ref[...]
    lo_ref[...] = jnp.where(odd, from_a, from_b)
    hi_ref[...] = jnp.where(odd, from_b, from_a)
    tall = ny + 16
    for plane in range(planes):
        own = y_ref[plane * ny : (plane + 1) * ny, :]
        base = plane * tall
        pad_ref[base + 8 : base + 8 + ny, :] = own
        pad_ref[base : base + 8, :] = own[ny - 8 :, :]
        pad_ref[base + 8 + ny : base + tall, :] = own[0:8, :]

    apart = iota((128, 128), 0) - iota((128, 128), 1)
    apart = jnp.abs(apart)
    apart = jnp.minimum(apart, 128 - apart)
    circulant = jnp.full((128, 128), 3.0 * weights[0], f32)
    circulant = jnp.where(apart > reach, 0.0, circulant)
    for distance in range(1, reach + 1):
        circulant = jnp.where(apart == distance, weights[distance], circulant)
    along_z = jnp.dot(y_ref[...], circulant, precision=highest, preferred_element_type=f32)

    scale = (1.0 if first else 2.0) / filter_half_width

    def plane_of(index):
        if index < 0:
            ref, index = lo_ref, index + planes
        elif index >= planes:
            ref, index = hi_ref, index - planes
        else:
            ref = y_ref
        return ref[index * ny : (index + 1) * ny, :]

    for plane in range(planes):
        rows = slice(plane * ny, (plane + 1) * ny)
        base = plane * tall + 8
        own = y_ref[rows, :]
        lap = along_z[rows, :]
        for distance in range(1, reach + 1):
            beside = plane_of(plane + distance) + plane_of(plane - distance)
            beside = beside + pad_ref[base + distance : base + distance + ny, :]
            beside = beside + pad_ref[base - distance : base - distance + ny, :]
            lap = lap + weights[distance] * beside
        value = scale * ((v_ref[rows, :] - filter_center) * own - 0.5 * lap)
        if prev_ref is not None:
            value = value - prev_ref[rows, :]
        out_ref[rows, :] = value

    sublane = iota((foot, 128), 0)
    for slot in range(n * cap):
        owner = slot // cap
        rows = slice(slot * nproj, (slot + 1) * nproj)
        returned = jnp.sum(
            w_ref[rows, :] * coefficients[owner : owner + 1, :], axis=1, keepdims=True
        )
        returned = jnp.broadcast_to(returned * scale, (nproj, 128))
        contrib = jnp.zeros((foot, 128), f32)
        for tile in range(foot):
            term = jnp.sum(
                p_ref[rows, tile * 128 : (tile + 1) * 128] * returned, axis=0, keepdims=True
            )
            contrib = jnp.where(sublane == tile, term, contrib)
        start = off_ref[slot % cap, slot // cap]
        out_ref[pl.ds(start, foot), :] = out_ref[pl.ds(start, foot), :] + contrib

    if not last:
        c_ref[...] = jnp.broadcast_to(
            partials(out_ref, p_ref, off_ref, r_ref, dims)[0:1], (n, lanes)
        )


def beside_slabs(y, n):
    pairs = [(i, i ^ 1) for i in range(n) if i ^ 1 < n]
    cross = [(i, i + 1) for i in range(1, n - 1, 2)] + [(i + 1, i) for i in range(1, n - 1, 2)]
    return lax.ppermute(y, "domain", pairs), lax.ppermute(y, "domain", cross)


def shards(psi, potential, projectors, offsets, intersection, dmat):
    n = lax.axis_size("domain")
    nband = lax.axis_size("band")
    cap, nproj = projectors.shape[2], projectors.shape[3]
    foot = projectors.shape[4] // 128
    chunk = cap * nproj
    lanes = n * chunk
    dims = (n, cap, nproj, foot, chunk)
    cells = psi.shape[1] * psi.shape[2]
    y = psi.reshape(cells, 128)
    p = projectors.reshape(lanes, foot * 128)
    off = offsets[0].T
    atom = intersection[0].T
    couplings = dmat.transpose(1, 2, 0).reshape(nproj * nproj, dmat.shape[0])
    info = jnp.stack([lax.axis_index("domain") % 2, lax.axis_index("band")]).astype(jnp.int32)
    params = pltpu.CompilerParams(vmem_limit_bytes=40 * 1024 * 1024)

    start = pl.pallas_call(
        functools.partial(start_kernel, dims),
        out_shape=jax.ShapeDtypeStruct((n, 24, lanes), f32),
        in_specs=[VMEM, VMEM, SMEM, SMEM, VMEM],
        out_specs=VMEM,
        scratch_shapes=[pltpu.VMEM((lanes, 128), f32)],
        compiler_params=params,
        name="first_partials",
    )
    got = lax.all_to_all(
        start(y, p, off, atom, couplings), "domain", split_axis=0, concat_axis=0, tiled=True
    )
    if potential.shape[1] % 8 == 0 and nband <= 8:
        pieces = [potential.reshape(-1, 128)]
        for back in range(1, nband):
            ring = [(i, (i + back) % nband) for i in range(nband)]
            pieces.append(lax.ppermute(pieces[0], "band", ring))
    else:
        pieces = [lax.all_gather(potential, "band", axis=1, tiled=True).reshape(cells, 128)]

    y_shape = jax.ShapeDtypeStruct((cells, 128), f32)
    c_shape = jax.ShapeDtypeStruct((n, lanes), f32)
    scratch = [
        pltpu.VMEM((cells // 32 * 48, 128), f32),
        pltpu.VMEM((cells, 128), f32),
        pltpu.VMEM((cells, 128), f32),
        pltpu.VMEM((lanes, 128), f32),
    ]
    from_a, from_b = beside_slabs(y, n)
    previous = y
    y, c, v, w = pl.pallas_call(
        functools.partial(step_kernel, dims, len(pieces), True, False),
        out_shape=(y_shape, c_shape, y_shape, jax.ShapeDtypeStruct((lanes, lanes), f32)),
        in_specs=[SMEM, SMEM] + [VMEM] * 5 + [SMEM] + [VMEM] * len(pieces),
        out_specs=(VMEM,) * 4,
        scratch_shapes=scratch,
        compiler_params=params,
        name="first_step",
    )(info, off, y, from_a, from_b, got, p, atom, *pieces)
    for degree in range(1, DEGREE):
        last = degree == DEGREE - 1
        got = lax.all_to_all(c, "domain", split_axis=0, concat_axis=0, tiled=True)
        from_a, from_b = beside_slabs(y, n)
        out = pl.pallas_call(
            functools.partial(step_kernel, dims, len(pieces), False, last),
            out_shape=(y_shape,) if last else (y_shape, c_shape),
            in_specs=[SMEM, SMEM] + [VMEM] * 8,
            out_specs=(VMEM,) if last else (VMEM, VMEM),
            scratch_shapes=scratch,
            compiler_params=params,
            name="last_step" if last else "next_step",
        )(info, off, y, from_a, from_b, got, p, previous, v, w)
        previous, y = y, out[0]
        if not last:
            c = out[1]
    return y.reshape(psi.shape)


def solution(mesh):
    return jax.shard_map(
        shards,
        mesh=mesh,
        in_specs=(
            P("band", "domain", None, None),
            P("domain", "band", None),
            P("domain", None, None, None, None),
            P("domain", None, None),
            P("domain", None, None),
            P("domain", None, None),
        ),
        out_specs=P("band", "domain", None, None),
        check_vma=False,
    )
```

```python
import functools

import jax
import jax.numpy as jnp
from jax import lax
from jax.experimental import pallas as pl
from jax.experimental.pallas import tpu as pltpu
from jax.sharding import PartitionSpec as P

DEGREE = 4
BIG = 100000

stencil_weights = (
    -5369.0 / 1800.0,
    12.0 / 7.0,
    -15.0 / 56.0,
    10.0 / 189.0,
    -1.0 / 112.0,
    2.0 / 1925.0,
    -1.0 / 16632.0,
)
reach = len(stencil_weights) - 1
filter_center = 6.0
filter_half_width = 4.0
highest = lax.Precision.HIGHEST
f32 = jnp.float32
VMEM = pl.BlockSpec(memory_space=pltpu.VMEM)
SMEM = pl.BlockSpec(memory_space=pltpu.SMEM)


def iota(shape, dim):
    return lax.broadcasted_iota(jnp.int32, shape, dim)


def partials(y_ref, p_ref, off_ref, r_ref, dims):
    n, cap, nproj, foot, chunk = dims
    for slot in range(n * cap):
        start = off_ref[slot % cap, slot // cap]
        rows = pl.ds(slot * nproj, nproj)
        total = None
        for tile in range(foot):
            cells = jnp.broadcast_to(y_ref[pl.ds(start + tile, 1), :], (nproj, 128))
            term = p_ref[rows, tile * 128 : (tile + 1) * 128] * cells
            total = term if total is None else total + term
        r_ref[rows, :] = total
    return lax.dot_general(
        jnp.ones((8, 128), f32),
        r_ref[...],
        (((1,), (1,)), ((), ())),
        precision=highest,
        preferred_element_type=f32,
    )


def by_owner(rows, n, chunk):
    lanes = n * chunk
    shape = (n, lanes)
    ahead = (iota(shape, 1) // chunk - iota(shape, 0) + n) % n
    out = rows
    for step in range(1, n):
        moved = pltpu.roll(rows, n - step, 0)
        moved = pltpu.roll(moved, step * chunk, 1)
        out = jnp.where(ahead == step, moved, out)
    return out


def start_kernel(dims, *refs):
    n, cap, nproj, foot, chunk = dims
    sources, (out_ref, y_ref, p_ref, v_ref) = refs[:6], refs[6:10]
    off_ref, atom_ref, dmat_ref, r_ref, sems = refs[10:]
    lanes = n * chunk
    targets = (y_ref, p_ref, off_ref, atom_ref, dmat_ref, v_ref)
    copies = [
        pltpu.make_async_copy(source, target, sems.at[index])
        for index, (source, target) in enumerate(zip(sources, targets))
    ]
    for copy in copies:
        copy.start()
    copies[3].wait()
    copies[4].wait()
    lane = iota((1, lanes), 1) // nproj
    atoms = jnp.zeros((1, lanes), f32)
    for slot in range(n * cap):
        value = atom_ref[slot % cap, slot // cap].astype(f32)
        atoms = jnp.where(lane == slot, value, atoms)
    out_ref[:, 1, :] = jnp.broadcast_to(atoms, (n, lanes))
    count = dmat_ref.shape[1]
    for group in range(128 // count):
        block = dmat_ref[group * 2 * nproj : (group + 1) * 2 * nproj, :]
        for peer in range(n):
            out_ref[peer, 8:, group * count : (group + 1) * count] = block
    for copy in copies[:3] + copies[5:]:
        copy.wait()
    out_ref[:, 0, :] = jnp.broadcast_to(
        partials(y_ref, p_ref, off_ref, r_ref, dims)[0:1], (n, lanes)
    )


def local_kernel(first, *refs):
    if first:
        y_ref, part_ref, pad_ref = refs
    else:
        y_ref, v_ref, prev_ref, part_ref, pad_ref = refs
    weights = stencil_weights
    ny = 32
    planes = y_ref.shape[0] // ny
    tall = ny + 16
    for plane in range(planes):
        own = y_ref[plane * ny : (plane + 1) * ny, :]
        base = plane * tall
        pad_ref[base + 8 : base + 8 + ny, :] = own
        pad_ref[base : base + 8, :] = own[ny - 8 :, :]
        pad_ref[base + 8 + ny : base + tall, :] = own[0:8, :]
    apart = jnp.abs(iota((128, 128), 0) - iota((128, 128), 1))
    apart = jnp.minimum(apart, 128 - apart)
    circulant = jnp.full((128, 128), 3.0 * weights[0], f32)
    circulant = jnp.where(apart > reach, 0.0, circulant)
    for distance in range(1, reach + 1):
        circulant = jnp.where(apart == distance, weights[distance], circulant)
    along_z = jnp.dot(y_ref[...], circulant, precision=highest, preferred_element_type=f32)
    scale = (1.0 if first else 2.0) / filter_half_width
    for plane in range(planes):
        rows = slice(plane * ny, (plane + 1) * ny)
        base = plane * tall + 8
        own = y_ref[rows, :]
        lap = along_z[rows, :]
        for distance in range(1, reach + 1):
            beside = pad_ref[base + distance : base + distance + ny, :]
            beside = beside + pad_ref[base - distance : base - distance + ny, :]
            for index in (plane - distance, plane + distance):
                if 0 <= index < planes:
                    beside = beside + y_ref[index * ny : (index + 1) * ny, :]
            lap = lap + weights[distance] * beside
        if first:
            value = scale * (-filter_center * own - 0.5 * lap)
        else:
            value = scale * ((v_ref[rows, :] - filter_center) * own - 0.5 * lap)
            value = value - prev_ref[rows, :]
        part_ref[rows, :] = value


def couple_kernel(dims, first, *refs):
    n, cap, nproj, foot, chunk = dims
    if first:
        off_ref, atom_ref, got_ref, part_ref, p_ref, out_ref, w_ref = refs
    else:
        off_ref, got_ref, part_ref, p_ref, w_ref, out_ref = refs
    lanes = n * chunk
    if first:
        atoms = by_owner(got_ref[:, 1, :], n, chunk)
        row = iota((chunk, 128), 0)
        column = iota((chunk, 128), 1)
        count = 128 // (nproj // 2)
        parity = (iota((chunk, 2 * nproj), 1) // nproj) == (iota((chunk, 2 * nproj), 0) % 2)
        spread = iota((2 * nproj, lanes), 1) % nproj == iota((2 * nproj, lanes), 0) % nproj
        spread = spread.astype(f32)
        row_wide = iota((chunk, lanes), 0) // nproj
        for owner in range(n):
            mine = jnp.zeros((chunk, 128), jnp.int32)
            mine_wide = jnp.zeros((chunk, lanes), f32)
            for k in range(cap):
                atom = atom_ref[k, owner]
                mine = jnp.where(row // nproj == k, atom, mine)
                mine_wide = jnp.where(row_wide == k, atom.astype(f32), mine_wide)
            pick = (column == (row % nproj) // 2 * count + mine) & (mine >= 0)
            entries = lax.dot_general(
                pick.astype(f32),
                got_ref[owner, 8:, 0:128],
                (((1,), (1,)), ((), ())),
                precision=highest,
                preferred_element_type=f32,
            )
            entries = jnp.where(parity, entries, 0.0)
            block = jnp.dot(entries, spread, precision=highest, preferred_element_type=f32)
            same = (atoms[owner : owner + 1, :] == mine_wide) & (mine_wide >= 0.0)
            w_ref[pl.ds(owner * chunk, chunk), :] = jnp.where(same, block, 0.0)
        coefficients = by_owner(got_ref[:, 0, :], n, chunk)
    else:
        coefficients = by_owner(got_ref[...], n, chunk)
    scale = (1.0 if first else 2.0) / filter_half_width
    out_ref[...] = part_ref[...]
    sublane = iota((foot, 128), 0)
    for slot in range(n * cap):
        owner = slot // cap
        rows = slice(slot * nproj, (slot + 1) * nproj)
        returned = jnp.sum(
            w_ref[rows, :] * coefficients[owner : owner + 1, :], axis=1, keepdims=True
        )
        returned = jnp.broadcast_to(returned * scale, (nproj, 128))
        contrib = jnp.zeros((foot, 128), f32)
        for tile in range(foot):
            term = jnp.sum(
                p_ref[rows, tile * 128 : (tile + 1) * 128] * returned, axis=0, keepdims=True
            )
            contrib = jnp.where(sublane == tile, term, contrib)
        start = off_ref[slot % cap, slot // cap]
        out_ref[pl.ds(start, foot), :] = out_ref[pl.ds(start, foot), :] + contrib


def step_kernel(dims, nband, first, last, *refs):
    n, cap, nproj, foot, chunk = dims
    refs = list(refs)
    take = lambda: refs.pop(0)
    info_ref, part_ref, a_ref, b_ref = take(), take(), take(), take()
    if first:
        y_ref = take()
        v_pieces = [take() for _ in range(nband)]
    if not last:
        off_ref, p_ref = take(), take()
    out_ref = take()
    if not last:
        c_ref = take()
    if first:
        v_ref = take()
    lo_ref, hi_ref = take(), take()
    cells = part_ref.shape[0]
    ny = 32
    planes = cells // ny
    lanes = n * chunk
    weights = stencil_weights
    if first and nband > 1:
        piece_rows = ny // nband
        for back, piece in enumerate(v_pieces):
            at = lax.rem(info_ref[1] - back + nband, nband) * piece_rows
            for plane in range(planes):
                spot = pl.multiple_of(plane * ny + at, 8)
                v_ref[pl.ds(spot, piece_rows), :] = piece[
                    plane * piece_rows : (plane + 1) * piece_rows, :
                ]
    elif first:
        v_ref[...] = v_pieces[0][...]
    odd = jnp.full((cells, 128), info_ref[0], jnp.int32) == 1
    from_a, from_b = a_ref[...], b_ref[...]
    lo_ref[...] = jnp.where(odd, from_a, from_b)
    hi_ref[...] = jnp.where(odd, from_b, from_a)
    scale = (1.0 if first else 2.0) / filter_half_width
    for plane in range(planes):
        rows = slice(plane * ny, (plane + 1) * ny)
        value = part_ref[rows, :]
        for distance in range(1, reach + 1):
            for index in (plane - distance, plane + distance):
                if index < 0:
                    beside = lo_ref[(index + planes) * ny : (index + planes + 1) * ny, :]
                elif index >= planes:
                    beside = hi_ref[(index - planes) * ny : (index - planes + 1) * ny, :]
                else:
                    continue
                value = value + (-0.5 * scale * weights[distance]) * beside
        if first:
            value = value + (scale * v_ref[rows, :]) * y_ref[rows, :]
        out_ref[rows, :] = value
    if not last:
        r_ref = take()
        c_ref[...] = jnp.broadcast_to(
            partials(out_ref, p_ref, off_ref, r_ref, dims)[0:1], (n, lanes)
        )


def beside_slabs(y, n):
    pairs = [(i, i ^ 1) for i in range(n) if i ^ 1 < n]
    cross = [(i, i + 1) for i in range(1, n - 1, 2)] + [(i + 1, i) for i in range(1, n - 1, 2)]
    return lax.ppermute(y, "domain", pairs), lax.ppermute(y, "domain", cross)


def shards(psi, potential, projectors, offsets, intersection, dmat):
    n = lax.axis_size("domain")
    nband = lax.axis_size("band")
    cap, nproj = projectors.shape[2], projectors.shape[3]
    foot = projectors.shape[4] // 128
    chunk = cap * nproj
    lanes = n * chunk
    dims = (n, cap, nproj, foot, chunk)
    cells = psi.shape[1] * psi.shape[2]
    y = psi.reshape(cells, 128)
    p = projectors.reshape(lanes, foot * 128)
    off = offsets[0].T
    atom = intersection[0].T
    couplings = dmat.transpose(1, 2, 0).reshape(nproj * nproj, dmat.shape[0])
    info = jnp.stack([lax.axis_index("domain") % 2, lax.axis_index("band")]).astype(jnp.int32)
    v_piece = potential.reshape(-1, 128)
    params = pltpu.CompilerParams(vmem_limit_bytes=40 * 1024 * 1024)
    y_shape = jax.ShapeDtypeStruct((cells, 128), f32)
    c_shape = jax.ShapeDtypeStruct((n, lanes), f32)
    row_scratch = pltpu.VMEM((lanes, 128), f32)

    def call(kernel, name, outs, ins, scratch=(), flops=40, smem=()):
        return pl.pallas_call(
            kernel,
            out_shape=outs,
            in_specs=[SMEM if index in smem else VMEM for index in range(len(ins))],
            out_specs=(VMEM,) * len(outs),
            scratch_shapes=scratch,
            compiler_params=params,
            cost_estimate=pl.CostEstimate(
                flops=flops * cells * 128, bytes_accessed=16 * cells * 128, transcendentals=0
            ),
            name=name,
        )(*ins)

    sources = (y, p, off, atom, couplings, v_piece)
    sources = [pltpu.with_memory_space_constraint(x, pltpu.HBM) for x in sources]
    payload, y, p, v_piece = pl.pallas_call(
        functools.partial(start_kernel, dims),
        out_shape=(
            jax.ShapeDtypeStruct((n, 24, lanes), f32),
            y_shape,
            jax.ShapeDtypeStruct(p.shape, f32),
            jax.ShapeDtypeStruct(v_piece.shape, f32),
        ),
        in_specs=[pl.BlockSpec(memory_space=pltpu.HBM)] * 6,
        out_specs=(VMEM,) * 4,
        scratch_shapes=[
            pltpu.SMEM(off.shape, jnp.int32),
            pltpu.SMEM(off.shape, jnp.int32),
            pltpu.VMEM(couplings.shape, f32),
            row_scratch,
            pltpu.SemaphoreType.DMA((6,)),
        ],
        compiler_params=params,
        name="first_partials",
    )(*sources)
    got = lax.all_to_all(payload, "domain", split_axis=0, concat_axis=0, tiled=True)
    if potential.shape[1] % 8 == 0 and nband <= 8:
        pieces = [v_piece]
        for back in range(1, nband):
            ring = [(i, (i + back) % nband) for i in range(nband)]
            pieces.append(lax.ppermute(v_piece, "band", ring))
    else:
        whole = v_piece.reshape(potential.shape)
        pieces = [lax.all_gather(whole, "band", axis=1, tiled=True).reshape(cells, 128)]

    slabs = [pltpu.VMEM((cells, 128), f32)] * 2
    padded = [pltpu.VMEM((cells // 32 * 48, 128), f32)]
    v = w = previous = None
    for degree in range(DEGREE):
        first, last = degree == 0, degree == DEGREE - 1
        if not first:
            got = lax.all_to_all(c, "domain", split_axis=0, concat_axis=0, tiled=True)
        from_a, from_b = beside_slabs(y, n)
        ins = (y,) if first else (y, v, previous)
        (part,) = call(functools.partial(local_kernel, first), "local", (y_shape,), ins, padded)
        couple = functools.partial(couple_kernel, dims, first)
        if first:
            outs = (y_shape, jax.ShapeDtypeStruct((lanes, lanes), f32))
            ins = (off, atom, got, part, p)
            part, w = call(couple, "first_couple", outs, ins, flops=BIG, smem=(0, 1))
        else:
            (part,) = call(couple, "couple", (y_shape,), (off, got, part, p, w), flops=BIG, smem=(0,))
        ins = (info, part, from_a, from_b)
        outs = (y_shape,)
        smem = (0,)
        if first:
            ins += (y, *pieces)
        if not last:
            smem += (len(ins),)
            ins += (off, p)
            outs += (c_shape,)
        if first:
            outs += (y_shape,)
        step = functools.partial(step_kernel, dims, len(pieces), first, last)
        scratch = slabs if last else slabs + [row_scratch]
        out = call(step, "last_step" if last else "step", outs, ins, scratch, smem=smem)
        previous, y = y, out[0]
        if not last:
            c = out[1]
        if first:
            v = out[2]
    return y.reshape(psi.shape)


def solution(mesh):
    return jax.shard_map(
        shards,
        mesh=mesh,
        in_specs=(
            P("band", "domain", None, None),
            P("domain", "band", None),
            P("domain", None, None, None, None),
            P("domain", None, None),
            P("domain", None, None),
            P("domain", None, None),
        ),
        out_specs=P("band", "domain", None, None),
        check_vma=False,
    )
```

```python
import functools

import jax
import jax.numpy as jnp
import numpy as np
from jax import lax
from jax.experimental import pallas as pl
from jax.experimental.pallas import tpu as pltpu
from jax.sharding import PartitionSpec as P

DEGREE = 4

stencil_weights = (
    -5369.0 / 1800.0,
    12.0 / 7.0,
    -15.0 / 56.0,
    10.0 / 189.0,
    -1.0 / 112.0,
    2.0 / 1925.0,
    -1.0 / 16632.0,
)
reach = len(stencil_weights) - 1
filter_center = 6.0
filter_half_width = 4.0
highest = lax.Precision.HIGHEST
f32 = jnp.float32
VMEM = pl.BlockSpec(memory_space=pltpu.VMEM)
SMEM = pl.BlockSpec(memory_space=pltpu.SMEM)


def iota(shape, dim):
    return lax.broadcasted_iota(jnp.int32, shape, dim)


def partials(y_ref, p_ref, off_ref, r_ref, dims):
    n, cap, nproj, foot, chunk = dims
    for slot in range(n * cap):
        start = off_ref[slot % cap, slot // cap]
        rows = pl.ds(slot * nproj, nproj)
        total = None
        for tile in range(foot):
            cells = jnp.broadcast_to(y_ref[pl.ds(start + tile, 1), :], (nproj, 128))
            term = p_ref[rows, tile * 128 : (tile + 1) * 128] * cells
            total = term if total is None else total + term
        r_ref[rows, :] = total
    return lax.dot_general(
        jnp.ones((8, 128), f32),
        r_ref[...],
        (((1,), (1,)), ((), ())),
        precision=highest,
        preferred_element_type=f32,
    )


def by_owner(rows, n, chunk):
    lanes = n * chunk
    shape = (n, lanes)
    ahead = (iota(shape, 1) // chunk - iota(shape, 0) + n) % n
    out = rows
    for step in range(1, n):
        moved = pltpu.roll(rows, n - step, 0)
        moved = pltpu.roll(moved, step * chunk, 1)
        out = jnp.where(ahead == step, moved, out)
    return out


def start_kernel(dims, y_ref, p_ref, off_ref, atom_ref, dmat_ref, out_ref, r_ref):
    n, cap, nproj, foot, chunk = dims
    lanes = n * chunk
    out_ref[:, 0, :] = jnp.broadcast_to(
        partials(y_ref, p_ref, off_ref, r_ref, dims)[0:1], (n, lanes)
    )
    lane = iota((1, lanes), 1) // nproj
    atoms = jnp.zeros((1, lanes), f32)
    for slot in range(n * cap):
        value = atom_ref[slot % cap, slot // cap].astype(f32)
        atoms = jnp.where(lane == slot, value, atoms)
    out_ref[:, 1, :] = jnp.broadcast_to(atoms, (n, lanes))
    count = dmat_ref.shape[1]
    for group in range(128 // count):
        block = dmat_ref[group * 2 * nproj : (group + 1) * 2 * nproj, :]
        for peer in range(n):
            out_ref[peer, 8:, group * count : (group + 1) * count] = block


def step_kernel(dims, nband, first, last, *refs):
    n, cap, nproj, foot, chunk = dims
    refs = list(refs)
    take = lambda: refs.pop(0)
    info_ref, off_ref = take(), take()
    y_ref, a_ref, b_ref, got_ref, p_ref = take(), take(), take(), take(), take()
    if first:
        atom_ref = take()
        v_pieces = [take() for _ in range(nband)]
        prev_ref = None
    else:
        prev_ref, v_ref, w_ref = take(), take(), take()
    out_ref = take()
    if not last:
        c_ref = take()
    if first:
        v_ref, w_ref = take(), take()
    pad_ref, lo_ref, hi_ref, r_ref = take(), take(), take(), take()
    cells = y_ref.shape[0]
    ny = 32
    planes = cells // ny
    lanes = n * chunk
    weights = stencil_weights

    if first:
        if nband > 1:
            piece_rows = ny // nband
            for back, piece in enumerate(v_pieces):
                at = lax.rem(info_ref[1] - back + nband, nband) * piece_rows
                for plane in range(planes):
                    spot = pl.multiple_of(plane * ny + at, 8)
                    v_ref[pl.ds(spot, piece_rows), :] = piece[
                        plane * piece_rows : (plane + 1) * piece_rows, :
                    ]
        else:
            v_ref[...] = v_pieces[0][...]
        atoms = by_owner(got_ref[:, 1, :], n, chunk)
        row = iota((chunk, 128), 0)
        column = iota((chunk, 128), 1)
        count = 128 // (nproj // 2)
        parity = (iota((chunk, 2 * nproj), 1) // nproj) == (iota((chunk, 2 * nproj), 0) % 2)
        spread = (iota((2 * nproj, lanes), 1) % nproj == iota((2 * nproj, lanes), 0) % nproj)
        spread = spread.astype(f32)
        for owner in range(n):
            mine = jnp.zeros((chunk, 128), jnp.int32)
            for k in range(cap):
                mine = jnp.where(row // nproj == k, atom_ref[k, owner], mine)
            pick = (column == (row % nproj) // 2 * count + mine) & (mine >= 0)
            entries = lax.dot_general(
                pick.astype(f32),
                got_ref[owner, 8:, 0:128],
                (((1,), (1,)), ((), ())),
                precision=highest,
                preferred_element_type=f32,
            )
            entries = jnp.where(parity, entries, 0.0)
            block = jnp.dot(entries, spread, precision=highest, preferred_element_type=f32)
            mine_row = jnp.zeros((chunk, lanes), f32)
            row_wide = iota((chunk, lanes), 0) // nproj
            for k in range(cap):
                mine_row = jnp.where(row_wide == k, atom_ref[k, owner].astype(f32), mine_row)
            same = (atoms[owner : owner + 1, :] == mine_row) & (mine_row >= 0.0)
            w_ref[pl.ds(owner * chunk, chunk), :] = jnp.where(same, block, 0.0)
        coefficients = by_owner(got_ref[:, 0, :], n, chunk)
    else:
        coefficients = by_owner(got_ref[...], n, chunk)

    odd = jnp.full((cells, 128), info_ref[0], jnp.int32) == 1
    from_a, from_b = a_ref[...], b_ref[...]
    lo_ref[...] = jnp.where(odd, from_a, from_b)
    hi_ref[...] = jnp.where(odd, from_b, from_a)
    tall = ny + 16
    for plane in range(planes):
        own = y_ref[plane * ny : (plane + 1) * ny, :]
        base = plane * tall
        pad_ref[base + 8 : base + 8 + ny, :] = own
        pad_ref[base : base + 8, :] = own[ny - 8 :, :]
        pad_ref[base + 8 + ny : base + tall, :] = own[0:8, :]

    apart = iota((128, 128), 0) - iota((128, 128), 1)
    apart = jnp.abs(apart)
    apart = jnp.minimum(apart, 128 - apart)
    circulant = jnp.full((128, 128), 3.0 * weights[0], f32)
    circulant = jnp.where(apart > reach, 0.0, circulant)
    for distance in range(1, reach + 1):
        circulant = jnp.where(apart == distance, weights[distance], circulant)
    along_z = jnp.dot(y_ref[...], circulant, precision=highest, preferred_element_type=f32)

    scale = (1.0 if first else 2.0) / filter_half_width

    def plane_of(index):
        if index < 0:
            ref, index = lo_ref, index + planes
        elif index >= planes:
            ref, index = hi_ref, index - planes
        else:
            ref = y_ref
        return ref[index * ny : (index + 1) * ny, :]

    for plane in range(planes):
        rows = slice(plane * ny, (plane + 1) * ny)
        base = plane * tall + 8
        own = y_ref[rows, :]
        lap = along_z[rows, :]
        for distance in range(1, reach + 1):
            beside = plane_of(plane + distance) + plane_of(plane - distance)
            beside = beside + pad_ref[base + distance : base + distance + ny, :]
            beside = beside + pad_ref[base - distance : base - distance + ny, :]
            lap = lap + weights[distance] * beside
        value = scale * ((v_ref[rows, :] - filter_center) * own - 0.5 * lap)
        if prev_ref is not None:
            value = value - prev_ref[rows, :]
        out_ref[rows, :] = value

    sublane = iota((foot, 128), 0)
    for slot in range(n * cap):
        owner = slot // cap
        rows = slice(slot * nproj, (slot + 1) * nproj)
        returned = jnp.sum(
            w_ref[rows, :] * coefficients[owner : owner + 1, :], axis=1, keepdims=True
        )
        returned = jnp.broadcast_to(returned * scale, (nproj, 128))
        contrib = jnp.zeros((foot, 128), f32)
        for tile in range(foot):
            term = jnp.sum(
                p_ref[rows, tile * 128 : (tile + 1) * 128] * returned, axis=0, keepdims=True
            )
            contrib = jnp.where(sublane == tile, term, contrib)
        start = off_ref[slot % cap, slot // cap]
        out_ref[pl.ds(start, foot), :] = out_ref[pl.ds(start, foot), :] + contrib

    if not last:
        c_ref[...] = jnp.broadcast_to(
            partials(out_ref, p_ref, off_ref, r_ref, dims)[0:1], (n, lanes)
        )


def beside_slabs(y, n):
    pairs = [(i, i ^ 1) for i in range(n) if i ^ 1 < n]
    cross = [(i, i + 1) for i in range(1, n - 1, 2)] + [(i + 1, i) for i in range(1, n - 1, 2)]
    return lax.ppermute(y, "domain", pairs), lax.ppermute(y, "domain", cross)


def slab_form(psi, potential, projectors, offsets, intersection, dmat):
    n = lax.axis_size("domain")
    nband = lax.axis_size("band")
    cap, nproj = projectors.shape[2], projectors.shape[3]
    foot = projectors.shape[4] // 128
    chunk = cap * nproj
    lanes = n * chunk
    dims = (n, cap, nproj, foot, chunk)
    cells = psi.shape[1] * psi.shape[2]
    y = psi.reshape(cells, 128)
    p = projectors.reshape(lanes, foot * 128)
    off = offsets[0].T
    atom = intersection[0].T
    couplings = dmat.transpose(1, 2, 0).reshape(nproj * nproj, dmat.shape[0])
    info = jnp.stack([lax.axis_index("domain") % 2, lax.axis_index("band")]).astype(jnp.int32)
    params = pltpu.CompilerParams(vmem_limit_bytes=40 * 1024 * 1024)

    start = pl.pallas_call(
        functools.partial(start_kernel, dims),
        out_shape=jax.ShapeDtypeStruct((n, 24, lanes), f32),
        in_specs=[VMEM, VMEM, SMEM, SMEM, VMEM],
        out_specs=VMEM,
        scratch_shapes=[pltpu.VMEM((lanes, 128), f32)],
        compiler_params=params,
        name="first_partials",
    )
    got = lax.all_to_all(
        start(y, p, off, atom, couplings), "domain", split_axis=0, concat_axis=0, tiled=True
    )
    if potential.shape[1] % 8 == 0 and nband <= 8:
        pieces = [potential.reshape(-1, 128)]
        for back in range(1, nband):
            ring = [(i, (i + back) % nband) for i in range(nband)]
            pieces.append(lax.ppermute(pieces[0], "band", ring))
    else:
        pieces = [lax.all_gather(potential, "band", axis=1, tiled=True).reshape(cells, 128)]

    y_shape = jax.ShapeDtypeStruct((cells, 128), f32)
    c_shape = jax.ShapeDtypeStruct((n, lanes), f32)
    scratch = [
        pltpu.VMEM((cells // 32 * 48, 128), f32),
        pltpu.VMEM((cells, 128), f32),
        pltpu.VMEM((cells, 128), f32),
        pltpu.VMEM((lanes, 128), f32),
    ]
    from_a, from_b = beside_slabs(y, n)
    previous = y
    y, c, v, w = pl.pallas_call(
        functools.partial(step_kernel, dims, len(pieces), True, False),
        out_shape=(y_shape, c_shape, y_shape, jax.ShapeDtypeStruct((lanes, lanes), f32)),
        in_specs=[SMEM, SMEM] + [VMEM] * 5 + [SMEM] + [VMEM] * len(pieces),
        out_specs=(VMEM,) * 4,
        scratch_shapes=scratch,
        compiler_params=params,
        name="first_step",
    )(info, off, y, from_a, from_b, got, p, atom, *pieces)
    for degree in range(1, DEGREE):
        last = degree == DEGREE - 1
        got = lax.all_to_all(c, "domain", split_axis=0, concat_axis=0, tiled=True)
        from_a, from_b = beside_slabs(y, n)
        out = pl.pallas_call(
            functools.partial(step_kernel, dims, len(pieces), False, last),
            out_shape=(y_shape,) if last else (y_shape, c_shape),
            in_specs=[SMEM, SMEM] + [VMEM] * 8,
            out_specs=(VMEM,) if last else (VMEM, VMEM),
            scratch_shapes=scratch,
            compiler_params=params,
            name="last_step" if last else "next_step",
        )(info, off, y, from_a, from_b, got, p, previous, v, w)
        previous, y = y, out[0]
        if not last:
            c = out[1]
    return y.reshape(psi.shape)


NY = 32
SLAB = 6 * NY
PACK = 2 * SLAB + 24


def circulant_z():
    apart = jnp.abs(iota((128, 128), 0) - iota((128, 128), 1))
    apart = jnp.minimum(apart, 128 - apart)
    out = jnp.full((128, 128), 3.0 * stencil_weights[0], f32)
    out = jnp.where(apart > reach, 0.0, out)
    for distance in range(1, reach + 1):
        out = jnp.where(apart == distance, stencil_weights[distance], out)
    return out


def stencil(y_ref, other_ref, v_ref, prev_ref, out_ref, pad_ref, slabs, scale, bases):
    tall = NY + 16
    for plane in range(6 * slabs):
        own = y_ref[plane * NY : (plane + 1) * NY, :]
        base = plane * tall
        pad_ref[base + 8 : base + 8 + NY, :] = own
        pad_ref[base : base + 8, :] = own[NY - 8 :, :]
        pad_ref[base + 8 + NY : base + tall, :] = own[0:8, :]
    along_z = jnp.dot(
        y_ref[0 : slabs * SLAB, :],
        circulant_z(),
        precision=highest,
        preferred_element_type=f32,
    )
    below, above = bases()
    for slab in range(slabs):
        for plane in range(6):
            at = (slab * 6 + plane) * NY
            rows = slice(at, at + NY)
            base = (slab * 6 + plane) * tall + 8
            own = y_ref[rows, :]
            lap = along_z[rows, :]
            for distance in range(1, reach + 1):
                beside = pad_ref[base + distance : base + distance + NY, :]
                beside = beside + pad_ref[base - distance : base - distance + NY, :]
                for index in (plane - distance, plane + distance):
                    if index < 0:
                        spot = pl.multiple_of(below[slab] + (index + 6) * NY, 8)
                        beside = beside + other_ref[pl.ds(spot, NY), :]
                    elif index >= 6:
                        spot = pl.multiple_of(above[slab] + (index - 6) * NY, 8)
                        beside = beside + other_ref[pl.ds(spot, NY), :]
                    else:
                        spot = (slab * 6 + index) * NY
                        beside = beside + y_ref[spot : spot + NY, :]
                lap = lap + stencil_weights[distance] * beside
            value = scale * ((v_ref[rows, :] - filter_center) * own - 0.5 * lap)
            if prev_ref is not None:
                value = value - prev_ref[rows, :]
            out_ref[rows, :] = value


def pack_kernel(dims, *refs):
    n, cap, nproj, foot, chunk = dims
    lanes = n * chunk
    sources, pack_ref, scratch = refs[:5], refs[5], refs[6:]
    p_ref, off_ref, atom_ref, dmat_ref, r_ref, sems = scratch
    y_ref = pack_ref.at[0:SLAB, :]
    targets = (y_ref, p_ref, off_ref, atom_ref, dmat_ref)
    copies = [
        pltpu.make_async_copy(source, target, sems.at[index])
        for index, (source, target) in enumerate(zip(sources, targets))
    ]
    for copy in copies:
        copy.start()
    for copy in copies[2:]:
        copy.wait()
    lane = iota((1, lanes), 1) // nproj
    atoms = jnp.zeros((1, lanes), f32)
    starts = jnp.zeros((1, lanes), f32)
    for slot in range(n * cap):
        here = lane == slot
        atoms = jnp.where(here, atom_ref[slot % cap, slot // cap].astype(f32), atoms)
        starts = jnp.where(here, off_ref[slot % cap, slot // cap].astype(f32), starts)
    small = 2 * SLAB
    pack_ref[small + 1 : small + 2, :] = atoms
    pack_ref[small + 2 : small + 3, :] = starts
    count = dmat_ref.shape[1]
    for group in range(128 // count):
        block = dmat_ref[group * 2 * nproj : (group + 1) * 2 * nproj, :]
        pack_ref[small + 8 :, group * count : (group + 1) * count] = block
    copies[0].wait()
    copies[1].wait()
    pack_ref[small : small + 1, :] = partials(pack_ref, p_ref, off_ref, r_ref, dims)[0:1]


def fill_kernel(pack_ref, *refs):
    pieces, out_ref = refs[:-1], refs[-1]
    out_ref[0:SLAB, :] = pack_ref[0:SLAB, :]
    out_ref[2 * SLAB :, :] = pack_ref[2 * SLAB :, :]
    rows = pieces[0].shape[0]
    for back, piece in enumerate(pieces):
        out_ref[SLAB + back * rows : SLAB + (back + 1) * rows, :] = piece[...]


def begin_kernel(dims, nband, info_ref, got_ref, part_ref, y_ref, v_ref, w_ref, c_ref, int_ref, other_ref, pad_ref):
    n, cap, nproj, foot, chunk = dims
    half = n // 2
    lanes = n * chunk
    small = 2 * SLAB
    piece = NY // nband
    c_rows, atom_rows, start_rows = [], [], []
    for local in range(half):
        mine, theirs = info_ref[local], info_ref[half + local]
        rows = slice(local * SLAB, (local + 1) * SLAB)
        y_ref[rows, :] = got_ref[mine, 0:SLAB, :]
        other_ref[rows, :] = got_ref[theirs, 0:SLAB, :]
        for back in range(nband):
            at = lax.rem(info_ref[4 * half] - back + nband, nband) * piece
            for plane in range(6):
                spot = pl.multiple_of(local * SLAB + plane * NY + at, 8)
                source = SLAB + back * 6 * piece + plane * piece
                v_ref[pl.ds(spot, piece), :] = got_ref[mine, source : source + piece, :]
    other_ref[half * SLAB :, :] = jnp.zeros((SLAB, 128), f32)
    for group in (0, half):
        for local in range(half):
            slab = info_ref[group + local]
            c_rows.append(got_ref[slab, small : small + 1, :])
            atom_rows.append(got_ref[slab, small + 1 : small + 2, :])
            if group == 0:
                start_rows.append(got_ref[slab, small + 2 : small + 3, :])
    c_ref[...] = by_owner(jnp.concatenate(c_rows, 0), n, chunk)
    atoms = by_owner(jnp.concatenate(atom_rows, 0), n, chunk)
    lane = iota((1, 128), 1)
    table = jnp.zeros((1, 128), jnp.int32)
    for local in range(half):
        int_ref[local : local + 1, :] = start_rows[local].astype(jnp.int32)
        for side in range(2):
            value = info_ref[(2 + side) * half + local]
            table = jnp.where(lane == side * half + local, value, table)
    int_ref[half : half + 1, :] = table
    int_ref[half + 1 :, :] = jnp.zeros((8 - half - 1, 128), jnp.int32)

    def bases():
        return (
            [info_ref[2 * half + local] for local in range(half)],
            [info_ref[3 * half + local] for local in range(half)],
        )

    stencil(
        y_ref, other_ref, v_ref, None, part_ref, pad_ref, half, 1.0 / filter_half_width, bases
    )
    square = (lanes, 128)
    diagonal = iota(square, 0) == iota(square, 1)
    ones = jnp.ones((128, 128), f32)
    column = iota(square, 1).astype(f32)
    count = 128 // (nproj // 2)
    shift = (iota(square, 0) % nproj // 2 * count).astype(f32)
    wide, picks = [], []
    for local in range(half):
        held = jnp.where(diagonal, atom_rows[local], 0.0)
        mine = jnp.dot(held, ones, precision=highest, preferred_element_type=f32)
        mine = jnp.round(mine)
        wide.append(mine)
        picks.append(jnp.where((column == shift + mine) & (mine >= 0.0), 1.0, 0.0))
    tall = half * chunk
    parity = iota((tall, 2 * nproj), 1) // nproj == iota((tall, 2 * nproj), 0) % 2
    spread = iota((2 * nproj, 128), 1) % nproj == iota((2 * nproj, 128), 0) % nproj
    spread = jnp.where(spread, 1.0, 0.0)
    for owner in range(n):
        rows = slice(owner * chunk, (owner + 1) * chunk)
        pick = jnp.concatenate([p[rows, :] for p in picks], 0)
        mine = jnp.concatenate([m[rows, :] for m in wide], 0)
        entries = lax.dot_general(
            pick,
            got_ref[owner, small + 8 :, :],
            (((1,), (1,)), ((), ())),
            precision=highest,
            preferred_element_type=f32,
        )
        entries = jnp.where(parity, entries, 0.0)
        block = jnp.dot(entries, spread, precision=highest, preferred_element_type=f32)
        same = (atoms[owner : owner + 1, :] == mine) & (mine >= 0.0)
        w_ref[owner * tall : (owner + 1) * tall, :] = jnp.where(same, block, 0.0)


def couple(dims, slabs, half, coefficients, w_ref, p_refs, start_of, out_ref, scale):
    n, cap, nproj, foot, chunk = dims
    sublane = iota((foot, 128), 0)
    for slab in range(slabs):
        for slot in range(n * cap):
            owner, k = slot // cap, slot % cap
            at = (owner * half + slab) * chunk + k * nproj
            returned = jnp.sum(
                w_ref[at : at + nproj, :] * coefficients[owner : owner + 1, :],
                axis=1,
                keepdims=True,
            )
            returned = jnp.broadcast_to(returned * scale, (nproj, 128))
            contrib = jnp.zeros((foot, 128), f32)
            rows = slice(slot * nproj, (slot + 1) * nproj)
            for tile in range(foot):
                term = jnp.sum(
                    p_refs[slab][rows, tile * 128 : (tile + 1) * 128] * returned,
                    axis=0,
                    keepdims=True,
                )
                contrib = jnp.where(sublane == tile, term, contrib)
            spot = pl.ds(start_of(slab, slot), foot)
            out_ref[spot, :] = out_ref[spot, :] + contrib


def next_partials(dims, half, send_ref, p_refs, start_of, r_ref):
    n, cap, nproj, foot, chunk = dims
    lanes = n * chunk
    for slab in range(half):
        for slot in range(n * cap):
            start = start_of(slab, slot)
            rows = slice(slot * nproj, (slot + 1) * nproj)
            total = None
            for tile in range(foot):
                cells = jnp.broadcast_to(send_ref[pl.ds(start + tile, 1), :], (nproj, 128))
                term = p_refs[slab][rows, tile * 128 : (tile + 1) * 128] * cells
                total = term if total is None else total + term
            r_ref[slab * lanes + slot * nproj : slab * lanes + (slot + 1) * nproj, :] = total
    row = lax.dot_general(
        jnp.ones((8, 128), f32),
        r_ref[...],
        (((1,), (1,)), ((), ())),
        precision=highest,
        preferred_element_type=f32,
    )
    for slab in range(half):
        send_ref[half * SLAB + slab : half * SLAB + slab + 1, :] = row[
            0:1, slab * lanes : (slab + 1) * lanes
        ]
    send_ref[half * SLAB + half :, :] = jnp.zeros((8 - half, 128), f32)


def starts_from(int_s, nproj):
    return lambda slab, slot: slab * SLAB + int_s[slab, slot * nproj]


def first_kernel(dims, *refs):
    n, cap, nproj, foot, chunk = dims
    half = n // 2
    int_ref, part_ref, w_ref, c_ref = refs[:4]
    p_refs, (send_ref, r_ref, int_s, sem) = refs[4 : 4 + half], refs[4 + half :]
    copy = pltpu.make_async_copy(int_ref, int_s, sem)
    copy.start()
    send_ref[0 : half * SLAB, :] = part_ref[...]
    copy.wait()
    start_of = starts_from(int_s, nproj)
    scale = 1.0 / filter_half_width
    couple(dims, half, half, c_ref[...], w_ref, p_refs, start_of, send_ref, scale)
    next_partials(dims, half, send_ref, p_refs, start_of, r_ref)


def chip_kernel(dims, last, *refs):
    n, cap, nproj, foot, chunk = dims
    half = n // 2
    int_ref, y_ref, got_ref, prev_ref, v_ref, w_ref = refs[:6]
    p_refs = refs[6 : 6 + half]
    out_ref, other_ref, pad_ref, int_s, sem = refs[6 + half : 11 + half]
    copy = pltpu.make_async_copy(int_ref, int_s, sem)
    copy.start()
    other_ref[0 : half * SLAB, :] = got_ref[0 : half * SLAB, :]
    other_ref[half * SLAB :, :] = jnp.zeros((SLAB, 128), f32)
    slabs = 1 if last else half
    scale = 2.0 / filter_half_width

    def bases():
        copy.wait()
        return (
            [int_s[half, local] for local in range(half)],
            [int_s[half, half + local] for local in range(half)],
        )

    stencil(y_ref, other_ref, v_ref, prev_ref, out_ref, pad_ref, slabs, scale, bases)
    below = slice(half * SLAB, half * SLAB + half)
    rows = jnp.concatenate([y_ref[below, :], got_ref[below, :]], 0)
    coefficients = by_owner(rows, n, chunk)
    start_of = starts_from(int_s, nproj)
    couple(dims, slabs, half, coefficients, w_ref, p_refs, start_of, out_ref, scale)
    if not last:
        next_partials(dims, half, out_ref, p_refs, start_of, refs[11 + half])


def chip_table(n):
    half = n // 2
    table = np.zeros((n, 4 * half), np.int32)
    for device in range(n):
        chip, core = device // 2, device % 2
        for local in range(half):
            there = chip ^ local
            table[device, local] = 2 * there + core
            table[device, half + local] = 2 * there + 1 - core
            same = local * SLAB
            far = there + (1 if core else -1)
            cross = (far ^ chip) * SLAB if 0 <= far < half else half * SLAB
            table[device, 2 * half + local] = same if core else cross
            table[device, 3 * half + local] = cross if core else same
    return table


def chip_form(psi, potential, projectors, offsets, intersection, dmat):
    n = lax.axis_size("domain")
    nband = lax.axis_size("band")
    cap, nproj = projectors.shape[2], projectors.shape[3]
    foot = projectors.shape[4] // 128
    chunk = cap * nproj
    lanes = n * chunk
    half = n // 2
    dims = (n, cap, nproj, foot, chunk)
    p = projectors.reshape(lanes, foot * 128)
    v_piece = potential.reshape(-1, 128)
    couplings = dmat.transpose(1, 2, 0).reshape(nproj * nproj, dmat.shape[0])
    domain = lax.axis_index("domain")
    info = jnp.concatenate(
        [
            lax.dynamic_slice_in_dim(jnp.asarray(chip_table(n)), domain, 1, 0)[0],
            lax.axis_index("band").astype(jnp.int32)[None],
        ]
    )
    params = pltpu.CompilerParams(vmem_limit_bytes=40 * 1024 * 1024)
    HBM = pl.BlockSpec(memory_space=pltpu.HBM)
    small = pl.CostEstimate(flops=1, bytes_accessed=1, transcendentals=0)

    def shape(rows, dtype=f32):
        return jax.ShapeDtypeStruct((rows, 128), dtype)

    def swap(x, step):
        return lax.ppermute(x, "domain", [(i, i ^ step) for i in range(n)])

    all_p = [p] + [swap(p, 2 * local) for local in range(1, half)]
    pieces = [v_piece]
    for back in range(1, nband):
        ring = [(i, (i + back) % nband) for i in range(nband)]
        pieces.append(lax.ppermute(v_piece, "band", ring))
    sources = (psi.reshape(SLAB, 128), p, offsets[0].T, intersection[0].T, couplings)
    sources = [pltpu.with_memory_space_constraint(x, pltpu.HBM) for x in sources]
    pack = pl.pallas_call(
        functools.partial(pack_kernel, dims),
        out_shape=shape(PACK),
        in_specs=[HBM] * 5,
        out_specs=VMEM,
        scratch_shapes=[
            pltpu.VMEM(p.shape, f32),
            pltpu.SMEM((cap, n), jnp.int32),
            pltpu.SMEM((cap, n), jnp.int32),
            pltpu.VMEM(couplings.shape, f32),
            pltpu.VMEM((lanes, 128), f32),
            pltpu.SemaphoreType.DMA((5,)),
        ],
        compiler_params=params,
        cost_estimate=small,
        name="pack",
    )(*sources)
    pack = pl.pallas_call(
        fill_kernel,
        out_shape=shape(PACK),
        in_specs=[VMEM] * (1 + nband),
        out_specs=VMEM,
        compiler_params=params,
        cost_estimate=small,
        name="fill",
    )(pack, *pieces)
    got = lax.all_gather(pack, "domain", axis=0)
    other = pltpu.VMEM(((half + 1) * SLAB, 128), f32)
    padded = pltpu.VMEM((half * 6 * (NY + 16), 128), f32)
    row_scratch = pltpu.VMEM((half * lanes, 128), f32)
    ints = [pltpu.SMEM((8, 128), jnp.int32), pltpu.SemaphoreType.DMA(())]
    part, previous, v, w, c, table = pl.pallas_call(
        functools.partial(begin_kernel, dims, nband),
        out_shape=(
            shape(half * SLAB),
            shape(half * SLAB),
            shape(half * SLAB),
            shape(half * lanes),
            shape(n),
            shape(8, jnp.int32),
        ),
        in_specs=[SMEM, VMEM],
        out_specs=(VMEM,) * 6,
        scratch_shapes=[other, padded],
        compiler_params=params,
        cost_estimate=small,
        name="begin",
    )(info, got)
    sent = shape(half * SLAB + 8)
    y = pl.pallas_call(
        functools.partial(first_kernel, dims),
        out_shape=sent,
        in_specs=[VMEM] * (4 + half),
        out_specs=VMEM,
        scratch_shapes=[row_scratch] + ints,
        compiler_params=params,
        name="first",
    )(table, part, w, c, *all_p)
    for degree in range(1, DEGREE):
        last = degree == DEGREE - 1
        following = pl.pallas_call(
            functools.partial(chip_kernel, dims, last),
            out_shape=shape(SLAB) if last else sent,
            in_specs=[VMEM] * (6 + half),
            out_specs=VMEM,
            scratch_shapes=[other, padded] + ints + ([] if last else [row_scratch]),
            compiler_params=params,
            name="last" if last else "next",
        )(table, y, swap(y, 1), previous, v, w, *all_p)
        previous, y = y, following
    return y.reshape(psi.shape)


def shards(psi, potential, projectors, offsets, intersection, dmat):
    n = lax.axis_size("domain")
    nband = lax.axis_size("band")
    pairs = n % 2 == 0 and (n // 2) & (n // 2 - 1) == 0
    fits = 4 <= n <= 8 and potential.shape[1] % 8 == 0 and nband <= 8
    form = chip_form if pairs and fits else slab_form
    return form(psi, potential, projectors, offsets, intersection, dmat)


def solution(mesh):
    return jax.shard_map(
        shards,
        mesh=mesh,
        in_specs=(
            P("band", "domain", None, None),
            P("domain", "band", None),
            P("domain", None, None, None, None),
            P("domain", None, None),
            P("domain", None, None),
            P("domain", None, None),
        ),
        out_specs=P("band", "domain", None, None),
        check_vma=False,
    )
```

```python
import functools

import jax
import jax.numpy as jnp
import numpy as np
from jax import lax
from jax.experimental import pallas as pl
from jax.experimental.pallas import tpu as pltpu
from jax.sharding import PartitionSpec as P

DEGREE = 4

stencil_weights = (
    -5369.0 / 1800.0,
    12.0 / 7.0,
    -15.0 / 56.0,
    10.0 / 189.0,
    -1.0 / 112.0,
    2.0 / 1925.0,
    -1.0 / 16632.0,
)
reach = len(stencil_weights) - 1
filter_center = 6.0
filter_half_width = 4.0
highest = lax.Precision.HIGHEST
f32 = jnp.float32
VMEM = pl.BlockSpec(memory_space=pltpu.VMEM)
SMEM = pl.BlockSpec(memory_space=pltpu.SMEM)


def iota(shape, dim):
    return lax.broadcasted_iota(jnp.int32, shape, dim)


def partials(y_ref, p_ref, off_ref, r_ref, dims):
    n, cap, nproj, foot, chunk = dims
    for slot in range(n * cap):
        start = off_ref[slot % cap, slot // cap]
        rows = pl.ds(slot * nproj, nproj)
        total = None
        for tile in range(foot):
            cells = jnp.broadcast_to(y_ref[pl.ds(start + tile, 1), :], (nproj, 128))
            term = p_ref[rows, tile * 128 : (tile + 1) * 128] * cells
            total = term if total is None else total + term
        r_ref[rows, :] = total
    return lax.dot_general(
        jnp.ones((8, 128), f32),
        r_ref[...],
        (((1,), (1,)), ((), ())),
        precision=highest,
        preferred_element_type=f32,
    )


def by_owner(rows, n, chunk):
    lanes = n * chunk
    shape = (n, lanes)
    ahead = (iota(shape, 1) // chunk - iota(shape, 0) + n) % n
    out = rows
    for step in range(1, n):
        moved = pltpu.roll(rows, n - step, 0)
        moved = pltpu.roll(moved, step * chunk, 1)
        out = jnp.where(ahead == step, moved, out)
    return out


def start_kernel(dims, y_ref, p_ref, off_ref, atom_ref, dmat_ref, out_ref, r_ref):
    n, cap, nproj, foot, chunk = dims
    lanes = n * chunk
    out_ref[:, 0, :] = jnp.broadcast_to(
        partials(y_ref, p_ref, off_ref, r_ref, dims)[0:1], (n, lanes)
    )
    lane = iota((1, lanes), 1) // nproj
    atoms = jnp.zeros((1, lanes), f32)
    for slot in range(n * cap):
        value = atom_ref[slot % cap, slot // cap].astype(f32)
        atoms = jnp.where(lane == slot, value, atoms)
    out_ref[:, 1, :] = jnp.broadcast_to(atoms, (n, lanes))
    count = dmat_ref.shape[1]
    for group in range(128 // count):
        block = dmat_ref[group * 2 * nproj : (group + 1) * 2 * nproj, :]
        for peer in range(n):
            out_ref[peer, 8:, group * count : (group + 1) * count] = block


def step_kernel(dims, nband, first, last, *refs):
    n, cap, nproj, foot, chunk = dims
    refs = list(refs)
    take = lambda: refs.pop(0)
    info_ref, off_ref = take(), take()
    y_ref, a_ref, b_ref, got_ref, p_ref = take(), take(), take(), take(), take()
    if first:
        atom_ref = take()
        v_pieces = [take() for _ in range(nband)]
        prev_ref = None
    else:
        prev_ref, v_ref, w_ref = take(), take(), take()
    out_ref = take()
    if not last:
        c_ref = take()
    if first:
        v_ref, w_ref = take(), take()
    pad_ref, lo_ref, hi_ref, r_ref = take(), take(), take(), take()
    cells = y_ref.shape[0]
    ny = 32
    planes = cells // ny
    lanes = n * chunk
    weights = stencil_weights

    if first:
        if nband > 1:
            piece_rows = ny // nband
            for back, piece in enumerate(v_pieces):
                at = lax.rem(info_ref[1] - back + nband, nband) * piece_rows
                for plane in range(planes):
                    spot = pl.multiple_of(plane * ny + at, 8)
                    v_ref[pl.ds(spot, piece_rows), :] = piece[
                        plane * piece_rows : (plane + 1) * piece_rows, :
                    ]
        else:
            v_ref[...] = v_pieces[0][...]
        atoms = by_owner(got_ref[:, 1, :], n, chunk)
        row = iota((chunk, 128), 0)
        column = iota((chunk, 128), 1)
        count = 128 // (nproj // 2)
        parity = (iota((chunk, 2 * nproj), 1) // nproj) == (iota((chunk, 2 * nproj), 0) % 2)
        spread = (iota((2 * nproj, lanes), 1) % nproj == iota((2 * nproj, lanes), 0) % nproj)
        spread = spread.astype(f32)
        for owner in range(n):
            mine = jnp.zeros((chunk, 128), jnp.int32)
            for k in range(cap):
                mine = jnp.where(row // nproj == k, atom_ref[k, owner], mine)
            pick = (column == (row % nproj) // 2 * count + mine) & (mine >= 0)
            entries = lax.dot_general(
                pick.astype(f32),
                got_ref[owner, 8:, 0:128],
                (((1,), (1,)), ((), ())),
                precision=highest,
                preferred_element_type=f32,
            )
            entries = jnp.where(parity, entries, 0.0)
            block = jnp.dot(entries, spread, precision=highest, preferred_element_type=f32)
            mine_row = jnp.zeros((chunk, lanes), f32)
            row_wide = iota((chunk, lanes), 0) // nproj
            for k in range(cap):
                mine_row = jnp.where(row_wide == k, atom_ref[k, owner].astype(f32), mine_row)
            same = (atoms[owner : owner + 1, :] == mine_row) & (mine_row >= 0.0)
            w_ref[pl.ds(owner * chunk, chunk), :] = jnp.where(same, block, 0.0)
        coefficients = by_owner(got_ref[:, 0, :], n, chunk)
    else:
        coefficients = by_owner(got_ref[...], n, chunk)

    odd = jnp.full((cells, 128), info_ref[0], jnp.int32) == 1
    from_a, from_b = a_ref[...], b_ref[...]
    lo_ref[...] = jnp.where(odd, from_a, from_b)
    hi_ref[...] = jnp.where(odd, from_b, from_a)
    tall = ny + 16
    for plane in range(planes):
        own = y_ref[plane * ny : (plane + 1) * ny, :]
        base = plane * tall
        pad_ref[base + 8 : base + 8 + ny, :] = own
        pad_ref[base : base + 8, :] = own[ny - 8 :, :]
        pad_ref[base + 8 + ny : base + tall, :] = own[0:8, :]

    apart = iota((128, 128), 0) - iota((128, 128), 1)
    apart = jnp.abs(apart)
    apart = jnp.minimum(apart, 128 - apart)
    circulant = jnp.full((128, 128), 3.0 * weights[0], f32)
    circulant = jnp.where(apart > reach, 0.0, circulant)
    for distance in range(1, reach + 1):
        circulant = jnp.where(apart == distance, weights[distance], circulant)
    along_z = jnp.dot(y_ref[...], circulant, precision=highest, preferred_element_type=f32)

    scale = (1.0 if first else 2.0) / filter_half_width

    def plane_of(index):
        if index < 0:
            ref, index = lo_ref, index + planes
        elif index >= planes:
            ref, index = hi_ref, index - planes
        else:
            ref = y_ref
        return ref[index * ny : (index + 1) * ny, :]

    for plane in range(planes):
        rows = slice(plane * ny, (plane + 1) * ny)
        base = plane * tall + 8
        own = y_ref[rows, :]
        lap = along_z[rows, :]
        for distance in range(1, reach + 1):
            beside = plane_of(plane + distance) + plane_of(plane - distance)
            beside = beside + pad_ref[base + distance : base + distance + ny, :]
            beside = beside + pad_ref[base - distance : base - distance + ny, :]
            lap = lap + weights[distance] * beside
        value = scale * ((v_ref[rows, :] - filter_center) * own - 0.5 * lap)
        if prev_ref is not None:
            value = value - prev_ref[rows, :]
        out_ref[rows, :] = value

    sublane = iota((foot, 128), 0)
    for slot in range(n * cap):
        owner = slot // cap
        rows = slice(slot * nproj, (slot + 1) * nproj)
        returned = jnp.sum(
            w_ref[rows, :] * coefficients[owner : owner + 1, :], axis=1, keepdims=True
        )
        returned = jnp.broadcast_to(returned * scale, (nproj, 128))
        contrib = jnp.zeros((foot, 128), f32)
        for tile in range(foot):
            term = jnp.sum(
                p_ref[rows, tile * 128 : (tile + 1) * 128] * returned, axis=0, keepdims=True
            )
            contrib = jnp.where(sublane == tile, term, contrib)
        start = off_ref[slot % cap, slot // cap]
        out_ref[pl.ds(start, foot), :] = out_ref[pl.ds(start, foot), :] + contrib

    if not last:
        c_ref[...] = jnp.broadcast_to(
            partials(out_ref, p_ref, off_ref, r_ref, dims)[0:1], (n, lanes)
        )


def beside_slabs(y, n):
    pairs = [(i, i ^ 1) for i in range(n) if i ^ 1 < n]
    cross = [(i, i + 1) for i in range(1, n - 1, 2)] + [(i + 1, i) for i in range(1, n - 1, 2)]
    return lax.ppermute(y, "domain", pairs), lax.ppermute(y, "domain", cross)


def slab_form(psi, potential, projectors, offsets, intersection, dmat):
    n = lax.axis_size("domain")
    nband = lax.axis_size("band")
    cap, nproj = projectors.shape[2], projectors.shape[3]
    foot = projectors.shape[4] // 128
    chunk = cap * nproj
    lanes = n * chunk
    dims = (n, cap, nproj, foot, chunk)
    cells = psi.shape[1] * psi.shape[2]
    y = psi.reshape(cells, 128)
    p = projectors.reshape(lanes, foot * 128)
    off = offsets[0].T
    atom = intersection[0].T
    couplings = dmat.transpose(1, 2, 0).reshape(nproj * nproj, dmat.shape[0])
    info = jnp.stack([lax.axis_index("domain") % 2, lax.axis_index("band")]).astype(jnp.int32)
    params = pltpu.CompilerParams(vmem_limit_bytes=40 * 1024 * 1024)

    start = pl.pallas_call(
        functools.partial(start_kernel, dims),
        out_shape=jax.ShapeDtypeStruct((n, 24, lanes), f32),
        in_specs=[VMEM, VMEM, SMEM, SMEM, VMEM],
        out_specs=VMEM,
        scratch_shapes=[pltpu.VMEM((lanes, 128), f32)],
        compiler_params=params,
        name="first_partials",
    )
    got = lax.all_to_all(
        start(y, p, off, atom, couplings), "domain", split_axis=0, concat_axis=0, tiled=True
    )
    if potential.shape[1] % 8 == 0 and nband <= 8:
        pieces = [potential.reshape(-1, 128)]
        for back in range(1, nband):
            ring = [(i, (i + back) % nband) for i in range(nband)]
            pieces.append(lax.ppermute(pieces[0], "band", ring))
    else:
        pieces = [lax.all_gather(potential, "band", axis=1, tiled=True).reshape(cells, 128)]

    y_shape = jax.ShapeDtypeStruct((cells, 128), f32)
    c_shape = jax.ShapeDtypeStruct((n, lanes), f32)
    scratch = [
        pltpu.VMEM((cells // 32 * 48, 128), f32),
        pltpu.VMEM((cells, 128), f32),
        pltpu.VMEM((cells, 128), f32),
        pltpu.VMEM((lanes, 128), f32),
    ]
    from_a, from_b = beside_slabs(y, n)
    previous = y
    y, c, v, w = pl.pallas_call(
        functools.partial(step_kernel, dims, len(pieces), True, False),
        out_shape=(y_shape, c_shape, y_shape, jax.ShapeDtypeStruct((lanes, lanes), f32)),
        in_specs=[SMEM, SMEM] + [VMEM] * 5 + [SMEM] + [VMEM] * len(pieces),
        out_specs=(VMEM,) * 4,
        scratch_shapes=scratch,
        compiler_params=params,
        name="first_step",
    )(info, off, y, from_a, from_b, got, p, atom, *pieces)
    for degree in range(1, DEGREE):
        last = degree == DEGREE - 1
        got = lax.all_to_all(c, "domain", split_axis=0, concat_axis=0, tiled=True)
        from_a, from_b = beside_slabs(y, n)
        out = pl.pallas_call(
            functools.partial(step_kernel, dims, len(pieces), False, last),
            out_shape=(y_shape,) if last else (y_shape, c_shape),
            in_specs=[SMEM, SMEM] + [VMEM] * 8,
            out_specs=(VMEM,) if last else (VMEM, VMEM),
            scratch_shapes=scratch,
            compiler_params=params,
            name="last_step" if last else "next_step",
        )(info, off, y, from_a, from_b, got, p, previous, v, w)
        previous, y = y, out[0]
        if not last:
            c = out[1]
    return y.reshape(psi.shape)


NY = 32
SLAB = 6 * NY
SMALL = 24


def circulant_z():
    apart = jnp.abs(iota((128, 128), 0) - iota((128, 128), 1))
    apart = jnp.minimum(apart, 128 - apart)
    out = jnp.full((128, 128), 3.0 * stencil_weights[0], f32)
    out = jnp.where(apart > reach, 0.0, out)
    for distance in range(1, reach + 1):
        out = jnp.where(apart == distance, stencil_weights[distance], out)
    return out


def stencil(y_ref, other_ref, v_ref, prev_ref, out_ref, pad_ref, slabs, scale, bases):
    tall = NY + 16
    for plane in range(6 * slabs):
        own = y_ref[plane * NY : (plane + 1) * NY, :]
        base = plane * tall
        pad_ref[base + 8 : base + 8 + NY, :] = own
        pad_ref[base : base + 8, :] = own[NY - 8 :, :]
        pad_ref[base + 8 + NY : base + tall, :] = own[0:8, :]
    along_z = jnp.dot(
        y_ref[0 : slabs * SLAB, :],
        circulant_z(),
        precision=highest,
        preferred_element_type=f32,
    )
    below, above = bases()
    for slab in range(slabs):
        for plane in range(6):
            at = (slab * 6 + plane) * NY
            rows = slice(at, at + NY)
            base = (slab * 6 + plane) * tall + 8
            own = y_ref[rows, :]
            lap = along_z[rows, :]
            for distance in range(1, reach + 1):
                beside = pad_ref[base + distance : base + distance + NY, :]
                beside = beside + pad_ref[base - distance : base - distance + NY, :]
                for index in (plane - distance, plane + distance):
                    if index < 0:
                        spot = pl.multiple_of(below[slab] + (index + 6) * NY, 8)
                        beside = beside + other_ref[pl.ds(spot, NY), :]
                    elif index >= 6:
                        spot = pl.multiple_of(above[slab] + (index - 6) * NY, 8)
                        beside = beside + other_ref[pl.ds(spot, NY), :]
                    else:
                        spot = (slab * 6 + index) * NY
                        beside = beside + y_ref[spot : spot + NY, :]
                lap = lap + stencil_weights[distance] * beside
            value = scale * ((v_ref[rows, :] - filter_center) * own - 0.5 * lap)
            if prev_ref is not None:
                value = value - prev_ref[rows, :]
            out_ref[rows, :] = value


def pack_kernel(dims, *refs):
    n, cap, nproj, foot, chunk = dims
    lanes = n * chunk
    sources, pack_ref, scratch = refs[:6], refs[6], refs[7:]
    p_ref, off_ref, atom_ref, dmat_ref, r_ref, sems = scratch
    small = pack_ref.shape[0] - SMALL
    targets = (
        pack_ref.at[0:SLAB, :],
        p_ref,
        off_ref,
        atom_ref,
        dmat_ref,
        pack_ref.at[SLAB:small, :],
    )
    copies = [
        pltpu.make_async_copy(source, target, sems.at[index])
        for index, (source, target) in enumerate(zip(sources, targets))
    ]
    for copy in copies:
        copy.start()
    for copy in copies[2:]:
        copy.wait()
    lane = iota((1, lanes), 1) // nproj
    atoms = jnp.zeros((1, lanes), f32)
    starts = jnp.zeros((1, lanes), f32)
    for slot in range(n * cap):
        here = lane == slot
        atoms = jnp.where(here, atom_ref[slot % cap, slot // cap].astype(f32), atoms)
        starts = jnp.where(here, off_ref[slot % cap, slot // cap].astype(f32), starts)
    pack_ref[small + 1 : small + 2, :] = atoms
    pack_ref[small + 2 : small + 3, :] = starts
    pack_ref[small + 3 : small + 8, :] = jnp.zeros((5, 128), f32)
    count = dmat_ref.shape[1]
    for group in range(128 // count):
        block = dmat_ref[group * 2 * nproj : (group + 1) * 2 * nproj, :]
        pack_ref[small + 8 :, group * count : (group + 1) * count] = block
    copies[0].wait()
    copies[1].wait()
    pack_ref[small : small + 1, :] = partials(pack_ref, p_ref, off_ref, r_ref, dims)[0:1]


def sort_kernel(*refs):
    packs, (pair_ref, v_ref) = refs[:-2], refs[-2:]
    small = packs[0].shape[0] - SMALL
    size = SLAB + SMALL
    for local, pack in enumerate(packs):
        pair_ref[local * size : local * size + SLAB, :] = pack[0:SLAB, :]
        pair_ref[local * size + SLAB : (local + 1) * size, :] = pack[small:, :]
        v_ref[local * (small - SLAB) : (local + 1) * (small - SLAB), :] = pack[SLAB:small, :]


def relay_kernel(x_ref, y_ref, top_ref, bottom_ref):
    rows = top_ref.shape[0]
    top_ref[...] = x_ref[0:rows, :]
    bottom_ref[...] = y_ref[rows:, :]


def begin_kernel(dims, nband, info_ref, own_ref, got_ref, *refs):
    n, cap, nproj, foot, chunk = dims
    half = n // 2
    v_pieces, refs = refs[:nband], refs[nband:]
    part_ref, y_ref, v_ref, w_ref, c_ref, int_ref, other_ref, pad_ref, dmat_ref = refs
    lanes = n * chunk
    size = SLAB + SMALL
    piece = NY // nband
    for back in range(nband):
        at = lax.rem(info_ref[4 * half + n] - back + nband, nband) * piece
        for plane in range(6 * half):
            spot = pl.multiple_of(plane * NY + at, 8)
            v_ref[pl.ds(spot, piece), :] = v_pieces[back][plane * piece : (plane + 1) * piece, :]
    c_rows, atom_rows, start_rows = [], [], []
    for group, source in enumerate((own_ref, got_ref)):
        for local in range(half):
            slab = local * size
            rows = slice(local * SLAB, (local + 1) * SLAB)
            target = other_ref if group else y_ref
            target[rows, :] = source[slab : slab + SLAB, :]
            small = slab + SLAB
            c_rows.append(source[small : small + 1, :])
            atom_rows.append(source[small + 1 : small + 2, :])
            if group == 0:
                start_rows.append(source[small + 2 : small + 3, :])
            dmat_ref[group * half + local] = source[small + 8 : small + SMALL, :]
    other_ref[half * SLAB :, :] = jnp.zeros((SLAB, 128), f32)
    c_ref[...] = by_owner(jnp.concatenate(c_rows, 0), n, chunk)
    atoms = by_owner(jnp.concatenate(atom_rows, 0), n, chunk)
    lane = iota((1, 128), 1)
    table = jnp.zeros((1, 128), jnp.int32)
    for local in range(half):
        int_ref[local : local + 1, :] = start_rows[local].astype(jnp.int32)
        for side in range(2):
            value = info_ref[(2 + side) * half + local]
            table = jnp.where(lane == side * half + local, value, table)
    int_ref[half : half + 1, :] = table
    int_ref[half + 1 :, :] = jnp.zeros((8 - half - 1, 128), jnp.int32)

    def bases():
        return (
            [info_ref[2 * half + local] for local in range(half)],
            [info_ref[3 * half + local] for local in range(half)],
        )

    stencil(
        y_ref, other_ref, v_ref, None, part_ref, pad_ref, half, 1.0 / filter_half_width, bases
    )
    square = (lanes, 128)
    diagonal = iota(square, 0) == iota(square, 1)
    ones = jnp.ones((128, 128), f32)
    column = iota(square, 1).astype(f32)
    count = 128 // (nproj // 2)
    shift = (iota(square, 0) % nproj // 2 * count).astype(f32)
    wide, picks = [], []
    for local in range(half):
        held = jnp.where(diagonal, atom_rows[local], 0.0)
        mine = jnp.dot(held, ones, precision=highest, preferred_element_type=f32)
        mine = jnp.round(mine)
        wide.append(mine)
        picks.append(jnp.where((column == shift + mine) & (mine >= 0.0), 1.0, 0.0))
    tall = half * chunk
    parity = iota((tall, 2 * nproj), 1) // nproj == iota((tall, 2 * nproj), 0) % 2
    spread = iota((2 * nproj, 128), 1) % nproj == iota((2 * nproj, 128), 0) % nproj
    spread = jnp.where(spread, 1.0, 0.0)
    for owner in range(n):
        rows = slice(owner * chunk, (owner + 1) * chunk)
        pick = jnp.concatenate([p[rows, :] for p in picks], 0)
        mine = jnp.concatenate([m[rows, :] for m in wide], 0)
        entries = lax.dot_general(
            pick,
            dmat_ref[info_ref[4 * half + owner]],
            (((1,), (1,)), ((), ())),
            precision=highest,
            preferred_element_type=f32,
        )
        entries = jnp.where(parity, entries, 0.0)
        block = jnp.dot(entries, spread, precision=highest, preferred_element_type=f32)
        same = (atoms[owner : owner + 1, :] == mine) & (mine >= 0.0)
        w_ref[owner * tall : (owner + 1) * tall, :] = jnp.where(same, block, 0.0)


def p_rows(p_refs, slab, slot, nproj, tile):
    ref, at = p_refs[slab], slot * nproj
    if at >= ref.shape[0]:
        ref, at = p_refs[slab + 1], at - ref.shape[0]
    return ref[at : at + nproj, tile * 128 : (tile + 1) * 128]


def couple(dims, slabs, half, coefficients, w_ref, p_refs, start_of, out_ref, scale):
    n, cap, nproj, foot, chunk = dims
    sublane = iota((foot, 128), 0)
    for slab in range(slabs):
        for slot in range(n * cap):
            owner, k = slot // cap, slot % cap
            at = (owner * half + slab) * chunk + k * nproj
            returned = jnp.sum(
                w_ref[at : at + nproj, :] * coefficients[owner : owner + 1, :],
                axis=1,
                keepdims=True,
            )
            returned = jnp.broadcast_to(returned * scale, (nproj, 128))
            contrib = jnp.zeros((foot, 128), f32)
            for tile in range(foot):
                term = jnp.sum(
                    p_rows(p_refs, slab, slot, nproj, tile) * returned,
                    axis=0,
                    keepdims=True,
                )
                contrib = jnp.where(sublane == tile, term, contrib)
            spot = pl.ds(start_of(slab, slot), foot)
            out_ref[spot, :] = out_ref[spot, :] + contrib


def next_partials(dims, half, send_ref, p_refs, start_of, r_ref):
    n, cap, nproj, foot, chunk = dims
    lanes = n * chunk
    for slab in range(half):
        for slot in range(n * cap):
            start = start_of(slab, slot)
            total = None
            for tile in range(foot):
                cells = jnp.broadcast_to(send_ref[pl.ds(start + tile, 1), :], (nproj, 128))
                term = p_rows(p_refs, slab, slot, nproj, tile) * cells
                total = term if total is None else total + term
            r_ref[slab * lanes + slot * nproj : slab * lanes + (slot + 1) * nproj, :] = total
    row = lax.dot_general(
        jnp.ones((8, 128), f32),
        r_ref[...],
        (((1,), (1,)), ((), ())),
        precision=highest,
        preferred_element_type=f32,
    )
    for slab in range(half):
        send_ref[half * SLAB + slab : half * SLAB + slab + 1, :] = row[
            0:1, slab * lanes : (slab + 1) * lanes
        ]
    send_ref[half * SLAB + half :, :] = jnp.zeros((8 - half, 128), f32)


def starts_from(int_s, nproj):
    return lambda slab, slot: slab * SLAB + int_s[slab, slot * nproj]


def first_kernel(dims, *refs):
    n, cap, nproj, foot, chunk = dims
    half = n // 2
    int_ref, part_ref, w_ref, c_ref = refs[:4]
    p_refs, (send_ref, r_ref, int_s, sem) = refs[4 : 5 + half], refs[5 + half :]
    copy = pltpu.make_async_copy(int_ref, int_s, sem)
    copy.start()
    send_ref[0 : half * SLAB, :] = part_ref[...]
    copy.wait()
    start_of = starts_from(int_s, nproj)
    scale = 1.0 / filter_half_width
    couple(dims, half, half, c_ref[...], w_ref, p_refs, start_of, send_ref, scale)
    next_partials(dims, half, send_ref, p_refs, start_of, r_ref)


def chip_kernel(dims, last, *refs):
    n, cap, nproj, foot, chunk = dims
    half = n // 2
    int_ref, y_ref, got_ref, prev_ref, v_ref, w_ref = refs[:6]
    p_refs = refs[6 : 7 + half]
    out_ref, other_ref, pad_ref, int_s, sem = refs[7 + half : 12 + half]
    copy = pltpu.make_async_copy(int_ref, int_s, sem)
    copy.start()
    other_ref[0 : half * SLAB, :] = got_ref[0 : half * SLAB, :]
    other_ref[half * SLAB :, :] = jnp.zeros((SLAB, 128), f32)
    slabs = 1 if last else half
    scale = 2.0 / filter_half_width

    def bases():
        copy.wait()
        return (
            [int_s[half, local] for local in range(half)],
            [int_s[half, half + local] for local in range(half)],
        )

    stencil(y_ref, other_ref, v_ref, prev_ref, out_ref, pad_ref, slabs, scale, bases)
    below = slice(half * SLAB, half * SLAB + half)
    rows = jnp.concatenate([y_ref[below, :], got_ref[below, :]], 0)
    coefficients = by_owner(rows, n, chunk)
    start_of = starts_from(int_s, nproj)
    couple(dims, slabs, half, coefficients, w_ref, p_refs, start_of, out_ref, scale)
    if not last:
        next_partials(dims, half, out_ref, p_refs, start_of, refs[12 + half])


def chip_table(n):
    half = n // 2
    table = np.zeros((n, 4 * half + n), np.int32)
    for device in range(n):
        chip, core = device // 2, device % 2
        for local in range(half):
            there = chip ^ local
            same = local * SLAB
            far = there + (1 if core else -1)
            cross = (far ^ chip) * SLAB if 0 <= far < half else half * SLAB
            table[device, 2 * half + local] = same if core else cross
            table[device, 3 * half + local] = cross if core else same
        for owner in range(n):
            table[device, 4 * half + owner] = owner % 2 * half if core == 0 else (1 - owner % 2) * half
            table[device, 4 * half + owner] += owner // 2 ^ chip
    return table


def chip_form(psi, potential, projectors, offsets, intersection, dmat):
    n = lax.axis_size("domain")
    nband = lax.axis_size("band")
    cap, nproj = projectors.shape[2], projectors.shape[3]
    foot = projectors.shape[4] // 128
    chunk = cap * nproj
    lanes = n * chunk
    half = n // 2
    dims = (n, cap, nproj, foot, chunk)
    p = projectors.reshape(lanes, foot * 128)
    v_piece = potential.reshape(-1, 128)
    couplings = dmat.transpose(1, 2, 0).reshape(nproj * nproj, dmat.shape[0])
    domain = lax.axis_index("domain")
    info = jnp.concatenate(
        [
            lax.dynamic_slice_in_dim(jnp.asarray(chip_table(n)), domain, 1, 0)[0],
            lax.axis_index("band").astype(jnp.int32)[None],
        ]
    )
    params = pltpu.CompilerParams(vmem_limit_bytes=40 * 1024 * 1024)
    HBM = pl.BlockSpec(memory_space=pltpu.HBM)
    small = pl.CostEstimate(flops=1, bytes_accessed=1, transcendentals=0)
    large = pl.CostEstimate(flops=10**10, bytes_accessed=1, transcendentals=0)

    def shape(rows, dtype=f32):
        return jax.ShapeDtypeStruct((rows, 128), dtype)

    def swap(x, step):
        return lax.ppermute(x, "domain", [(i, i ^ step) for i in range(n)])

    sources = (psi.reshape(SLAB, 128), p, offsets[0].T, intersection[0].T, couplings, v_piece)
    sources = [pltpu.with_memory_space_constraint(x, pltpu.HBM) for x in sources]
    pack = pl.pallas_call(
        functools.partial(pack_kernel, dims),
        out_shape=shape(SLAB + v_piece.shape[0] + SMALL),
        in_specs=[HBM] * 6,
        out_specs=VMEM,
        scratch_shapes=[
            pltpu.VMEM(p.shape, f32),
            pltpu.SMEM((cap, n), jnp.int32),
            pltpu.SMEM((cap, n), jnp.int32),
            pltpu.VMEM(couplings.shape, f32),
            pltpu.VMEM((lanes, 128), f32),
            pltpu.SemaphoreType.DMA((6,)),
        ],
        compiler_params=params,
        cost_estimate=small,
        name="pack",
    )(*sources)
    packs = [pack] + [swap(pack, 2 * local) for local in range(1, half)]
    own, v_piece = pl.pallas_call(
        sort_kernel,
        out_shape=(shape(half * (SLAB + SMALL)), shape(half * v_piece.shape[0])),
        in_specs=[VMEM] * half,
        out_specs=(VMEM, VMEM),
        compiler_params=params,
        cost_estimate=small,
        name="sort",
    )(*packs)
    got = swap(own, 1)
    pieces = [v_piece]
    for back in range(1, nband):
        ring = [(i, (i + back) % nband) for i in range(nband)]
        pieces.append(lax.ppermute(v_piece, "band", ring))
    p_x, p_y = swap(p, 2), swap(p, 4)
    halves = (jax.ShapeDtypeStruct((lanes // 2, foot * 128), f32),) * 2
    top, bottom = pl.pallas_call(
        relay_kernel,
        out_shape=halves,
        in_specs=[VMEM] * 2,
        out_specs=(VMEM, VMEM),
        compiler_params=params,
        cost_estimate=large,
        name="relay",
    )(p_x, p_y)
    all_p = [p, p_x, p_y, swap(top, 4), swap(bottom, 2)]
    other = pltpu.VMEM(((half + 1) * SLAB, 128), f32)
    padded = pltpu.VMEM((half * 6 * (NY + 16), 128), f32)
    row_scratch = pltpu.VMEM((half * lanes, 128), f32)
    ints = [pltpu.SMEM((8, 128), jnp.int32), pltpu.SemaphoreType.DMA(())]
    part, previous, v, w, c, table = pl.pallas_call(
        functools.partial(begin_kernel, dims, nband),
        out_shape=(
            shape(half * SLAB),
            shape(half * SLAB),
            shape(half * SLAB),
            shape(half * lanes),
            shape(n),
            shape(8, jnp.int32),
        ),
        in_specs=[SMEM] + [VMEM] * (2 + nband),
        out_specs=(VMEM,) * 6,
        scratch_shapes=[other, padded, pltpu.VMEM((n, 2 * nproj, 128), f32)],
        compiler_params=params,
        cost_estimate=small,
        name="begin",
    )(info, own, got, *pieces)
    sent = shape(half * SLAB + 8)
    y = pl.pallas_call(
        functools.partial(first_kernel, dims),
        out_shape=sent,
        in_specs=[VMEM] * (5 + half),
        out_specs=VMEM,
        scratch_shapes=[row_scratch] + ints,
        compiler_params=params,
        name="first",
    )(table, part, w, c, *all_p)
    for degree in range(1, DEGREE):
        last = degree == DEGREE - 1
        following = pl.pallas_call(
            functools.partial(chip_kernel, dims, last),
            out_shape=shape(SLAB) if last else sent,
            in_specs=[VMEM] * (7 + half),
            out_specs=VMEM,
            scratch_shapes=[other, padded] + ints + ([] if last else [row_scratch]),
            compiler_params=params,
            name="last" if last else "next",
        )(table, y, swap(y, 1), previous, v, w, *all_p)
        previous, y = y, following
    return y.reshape(psi.shape)


def shards(psi, potential, projectors, offsets, intersection, dmat):
    n = lax.axis_size("domain")
    nband = lax.axis_size("band")
    fits = n == 8 and potential.shape[1] % 8 == 0 and nband <= 8
    form = chip_form if fits else slab_form
    return form(psi, potential, projectors, offsets, intersection, dmat)


def solution(mesh):
    return jax.shard_map(
        shards,
        mesh=mesh,
        in_specs=(
            P("band", "domain", None, None),
            P("domain", "band", None),
            P("domain", None, None, None, None),
            P("domain", None, None),
            P("domain", None, None),
            P("domain", None, None),
        ),
        out_specs=P("band", "domain", None, None),
        check_vma=False,
    )
```

```python
import functools

import jax
import jax.numpy as jnp
import numpy as np
from jax import lax
from jax.experimental import pallas as pl
from jax.experimental.pallas import tpu as pltpu
from jax.sharding import PartitionSpec as P

DEGREE = 4

stencil_weights = (
    -5369.0 / 1800.0,
    12.0 / 7.0,
    -15.0 / 56.0,
    10.0 / 189.0,
    -1.0 / 112.0,
    2.0 / 1925.0,
    -1.0 / 16632.0,
)
reach = len(stencil_weights) - 1
filter_center = 6.0
filter_half_width = 4.0
highest = lax.Precision.HIGHEST
f32 = jnp.float32
VMEM = pl.BlockSpec(memory_space=pltpu.VMEM)
SMEM = pl.BlockSpec(memory_space=pltpu.SMEM)


def iota(shape, dim):
    return lax.broadcasted_iota(jnp.int32, shape, dim)


def partials(y_ref, p_ref, off_ref, r_ref, dims):
    n, cap, nproj, foot, chunk = dims
    for slot in range(n * cap):
        start = off_ref[slot % cap, slot // cap]
        rows = pl.ds(slot * nproj, nproj)
        total = None
        for tile in range(foot):
            cells = jnp.broadcast_to(y_ref[pl.ds(start + tile, 1), :], (nproj, 128))
            term = p_ref[rows, tile * 128 : (tile + 1) * 128] * cells
            total = term if total is None else total + term
        r_ref[rows, :] = total
    return lax.dot_general(
        jnp.ones((8, 128), f32),
        r_ref[...],
        (((1,), (1,)), ((), ())),
        precision=highest,
        preferred_element_type=f32,
    )


def by_owner(rows, n, chunk):
    lanes = n * chunk
    shape = (n, lanes)
    ahead = (iota(shape, 1) // chunk - iota(shape, 0) + n) % n
    out = rows
    for step in range(1, n):
        moved = pltpu.roll(rows, n - step, 0)
        moved = pltpu.roll(moved, step * chunk, 1)
        out = jnp.where(ahead == step, moved, out)
    return out


def start_kernel(dims, y_ref, p_ref, off_ref, atom_ref, dmat_ref, out_ref, r_ref):
    n, cap, nproj, foot, chunk = dims
    lanes = n * chunk
    out_ref[:, 0, :] = jnp.broadcast_to(
        partials(y_ref, p_ref, off_ref, r_ref, dims)[0:1], (n, lanes)
    )
    lane = iota((1, lanes), 1) // nproj
    atoms = jnp.zeros((1, lanes), f32)
    for slot in range(n * cap):
        value = atom_ref[slot % cap, slot // cap].astype(f32)
        atoms = jnp.where(lane == slot, value, atoms)
    out_ref[:, 1, :] = jnp.broadcast_to(atoms, (n, lanes))
    count = dmat_ref.shape[1]
    for group in range(128 // count):
        block = dmat_ref[group * 2 * nproj : (group + 1) * 2 * nproj, :]
        for peer in range(n):
            out_ref[peer, 8:, group * count : (group + 1) * count] = block


def step_kernel(dims, nband, first, last, *refs):
    n, cap, nproj, foot, chunk = dims
    refs = list(refs)
    take = lambda: refs.pop(0)
    info_ref, off_ref = take(), take()
    y_ref, a_ref, b_ref, got_ref, p_ref = take(), take(), take(), take(), take()
    if first:
        atom_ref = take()
        v_pieces = [take() for _ in range(nband)]
        prev_ref = None
    else:
        prev_ref, v_ref, w_ref = take(), take(), take()
    out_ref = take()
    if not last:
        c_ref = take()
    if first:
        v_ref, w_ref = take(), take()
    pad_ref, lo_ref, hi_ref, r_ref = take(), take(), take(), take()
    cells = y_ref.shape[0]
    ny = 32
    planes = cells // ny
    lanes = n * chunk
    weights = stencil_weights

    if first:
        if nband > 1:
            piece_rows = ny // nband
            for back, piece in enumerate(v_pieces):
                at = lax.rem(info_ref[1] - back + nband, nband) * piece_rows
                for plane in range(planes):
                    spot = pl.multiple_of(plane * ny + at, 8)
                    v_ref[pl.ds(spot, piece_rows), :] = piece[
                        plane * piece_rows : (plane + 1) * piece_rows, :
                    ]
        else:
            v_ref[...] = v_pieces[0][...]
        atoms = by_owner(got_ref[:, 1, :], n, chunk)
        row = iota((chunk, 128), 0)
        column = iota((chunk, 128), 1)
        count = 128 // (nproj // 2)
        parity = (iota((chunk, 2 * nproj), 1) // nproj) == (iota((chunk, 2 * nproj), 0) % 2)
        spread = (iota((2 * nproj, lanes), 1) % nproj == iota((2 * nproj, lanes), 0) % nproj)
        spread = spread.astype(f32)
        for owner in range(n):
            mine = jnp.zeros((chunk, 128), jnp.int32)
            for k in range(cap):
                mine = jnp.where(row // nproj == k, atom_ref[k, owner], mine)
            pick = (column == (row % nproj) // 2 * count + mine) & (mine >= 0)
            entries = lax.dot_general(
                pick.astype(f32),
                got_ref[owner, 8:, 0:128],
                (((1,), (1,)), ((), ())),
                precision=highest,
                preferred_element_type=f32,
            )
            entries = jnp.where(parity, entries, 0.0)
            block = jnp.dot(entries, spread, precision=highest, preferred_element_type=f32)
            mine_row = jnp.zeros((chunk, lanes), f32)
            row_wide = iota((chunk, lanes), 0) // nproj
            for k in range(cap):
                mine_row = jnp.where(row_wide == k, atom_ref[k, owner].astype(f32), mine_row)
            same = (atoms[owner : owner + 1, :] == mine_row) & (mine_row >= 0.0)
            w_ref[pl.ds(owner * chunk, chunk), :] = jnp.where(same, block, 0.0)
        coefficients = by_owner(got_ref[:, 0, :], n, chunk)
    else:
        coefficients = by_owner(got_ref[...], n, chunk)

    odd = jnp.full((cells, 128), info_ref[0], jnp.int32) == 1
    from_a, from_b = a_ref[...], b_ref[...]
    lo_ref[...] = jnp.where(odd, from_a, from_b)
    hi_ref[...] = jnp.where(odd, from_b, from_a)
    tall = ny + 16
    for plane in range(planes):
        own = y_ref[plane * ny : (plane + 1) * ny, :]
        base = plane * tall
        pad_ref[base + 8 : base + 8 + ny, :] = own
        pad_ref[base : base + 8, :] = own[ny - 8 :, :]
        pad_ref[base + 8 + ny : base + tall, :] = own[0:8, :]

    apart = iota((128, 128), 0) - iota((128, 128), 1)
    apart = jnp.abs(apart)
    apart = jnp.minimum(apart, 128 - apart)
    circulant = jnp.full((128, 128), 3.0 * weights[0], f32)
    circulant = jnp.where(apart > reach, 0.0, circulant)
    for distance in range(1, reach + 1):
        circulant = jnp.where(apart == distance, weights[distance], circulant)
    along_z = jnp.dot(y_ref[...], circulant, precision=highest, preferred_element_type=f32)

    scale = (1.0 if first else 2.0) / filter_half_width

    def plane_of(index):
        if index < 0:
            ref, index = lo_ref, index + planes
        elif index >= planes:
            ref, index = hi_ref, index - planes
        else:
            ref = y_ref
        return ref[index * ny : (index + 1) * ny, :]

    for plane in range(planes):
        rows = slice(plane * ny, (plane + 1) * ny)
        base = plane * tall + 8
        own = y_ref[rows, :]
        lap = along_z[rows, :]
        for distance in range(1, reach + 1):
            beside = plane_of(plane + distance) + plane_of(plane - distance)
            beside = beside + pad_ref[base + distance : base + distance + ny, :]
            beside = beside + pad_ref[base - distance : base - distance + ny, :]
            lap = lap + weights[distance] * beside
        value = scale * ((v_ref[rows, :] - filter_center) * own - 0.5 * lap)
        if prev_ref is not None:
            value = value - prev_ref[rows, :]
        out_ref[rows, :] = value

    sublane = iota((foot, 128), 0)
    for slot in range(n * cap):
        owner = slot // cap
        rows = slice(slot * nproj, (slot + 1) * nproj)
        returned = jnp.sum(
            w_ref[rows, :] * coefficients[owner : owner + 1, :], axis=1, keepdims=True
        )
        returned = jnp.broadcast_to(returned * scale, (nproj, 128))
        contrib = jnp.zeros((foot, 128), f32)
        for tile in range(foot):
            term = jnp.sum(
                p_ref[rows, tile * 128 : (tile + 1) * 128] * returned, axis=0, keepdims=True
            )
            contrib = jnp.where(sublane == tile, term, contrib)
        start = off_ref[slot % cap, slot // cap]
        out_ref[pl.ds(start, foot), :] = out_ref[pl.ds(start, foot), :] + contrib

    if not last:
        c_ref[...] = jnp.broadcast_to(
            partials(out_ref, p_ref, off_ref, r_ref, dims)[0:1], (n, lanes)
        )


def beside_slabs(y, n):
    pairs = [(i, i ^ 1) for i in range(n) if i ^ 1 < n]
    cross = [(i, i + 1) for i in range(1, n - 1, 2)] + [(i + 1, i) for i in range(1, n - 1, 2)]
    return lax.ppermute(y, "domain", pairs), lax.ppermute(y, "domain", cross)


def slab_form(psi, potential, projectors, offsets, intersection, dmat):
    n = lax.axis_size("domain")
    nband = lax.axis_size("band")
    cap, nproj = projectors.shape[2], projectors.shape[3]
    foot = projectors.shape[4] // 128
    chunk = cap * nproj
    lanes = n * chunk
    dims = (n, cap, nproj, foot, chunk)
    cells = psi.shape[1] * psi.shape[2]
    y = psi.reshape(cells, 128)
    p = projectors.reshape(lanes, foot * 128)
    off = offsets[0].T
    atom = intersection[0].T
    couplings = dmat.transpose(1, 2, 0).reshape(nproj * nproj, dmat.shape[0])
    info = jnp.stack([lax.axis_index("domain") % 2, lax.axis_index("band")]).astype(jnp.int32)
    params = pltpu.CompilerParams(vmem_limit_bytes=40 * 1024 * 1024)

    start = pl.pallas_call(
        functools.partial(start_kernel, dims),
        out_shape=jax.ShapeDtypeStruct((n, 24, lanes), f32),
        in_specs=[VMEM, VMEM, SMEM, SMEM, VMEM],
        out_specs=VMEM,
        scratch_shapes=[pltpu.VMEM((lanes, 128), f32)],
        compiler_params=params,
        name="first_partials",
    )
    got = lax.all_to_all(
        start(y, p, off, atom, couplings), "domain", split_axis=0, concat_axis=0, tiled=True
    )
    if potential.shape[1] % 8 == 0 and nband <= 8:
        pieces = [potential.reshape(-1, 128)]
        for back in range(1, nband):
            ring = [(i, (i + back) % nband) for i in range(nband)]
            pieces.append(lax.ppermute(pieces[0], "band", ring))
    else:
        pieces = [lax.all_gather(potential, "band", axis=1, tiled=True).reshape(cells, 128)]

    y_shape = jax.ShapeDtypeStruct((cells, 128), f32)
    c_shape = jax.ShapeDtypeStruct((n, lanes), f32)
    scratch = [
        pltpu.VMEM((cells // 32 * 48, 128), f32),
        pltpu.VMEM((cells, 128), f32),
        pltpu.VMEM((cells, 128), f32),
        pltpu.VMEM((lanes, 128), f32),
    ]
    from_a, from_b = beside_slabs(y, n)
    previous = y
    y, c, v, w = pl.pallas_call(
        functools.partial(step_kernel, dims, len(pieces), True, False),
        out_shape=(y_shape, c_shape, y_shape, jax.ShapeDtypeStruct((lanes, lanes), f32)),
        in_specs=[SMEM, SMEM] + [VMEM] * 5 + [SMEM] + [VMEM] * len(pieces),
        out_specs=(VMEM,) * 4,
        scratch_shapes=scratch,
        compiler_params=params,
        name="first_step",
    )(info, off, y, from_a, from_b, got, p, atom, *pieces)
    for degree in range(1, DEGREE):
        last = degree == DEGREE - 1
        got = lax.all_to_all(c, "domain", split_axis=0, concat_axis=0, tiled=True)
        from_a, from_b = beside_slabs(y, n)
        out = pl.pallas_call(
            functools.partial(step_kernel, dims, len(pieces), False, last),
            out_shape=(y_shape,) if last else (y_shape, c_shape),
            in_specs=[SMEM, SMEM] + [VMEM] * 8,
            out_specs=(VMEM,) if last else (VMEM, VMEM),
            scratch_shapes=scratch,
            compiler_params=params,
            name="last_step" if last else "next_step",
        )(info, off, y, from_a, from_b, got, p, previous, v, w)
        previous, y = y, out[0]
        if not last:
            c = out[1]
    return y.reshape(psi.shape)


NY = 32
SLAB = 6 * NY
SMALL = 24


def circulant_z():
    apart = jnp.abs(iota((128, 128), 0) - iota((128, 128), 1))
    apart = jnp.minimum(apart, 128 - apart)
    out = jnp.full((128, 128), 3.0 * stencil_weights[0], f32)
    out = jnp.where(apart > reach, 0.0, out)
    for distance in range(1, reach + 1):
        out = jnp.where(apart == distance, stencil_weights[distance], out)
    return out


def stencil(y_ref, other_ref, v_ref, prev_ref, out_ref, pad_ref, slabs, scale, bases):
    tall = NY + 16
    for plane in range(6 * slabs):
        own = y_ref[plane * NY : (plane + 1) * NY, :]
        base = plane * tall
        pad_ref[base + 8 : base + 8 + NY, :] = own
        pad_ref[base : base + 8, :] = own[NY - 8 :, :]
        pad_ref[base + 8 + NY : base + tall, :] = own[0:8, :]
    along_z = jnp.dot(
        y_ref[0 : slabs * SLAB, :],
        circulant_z(),
        precision=highest,
        preferred_element_type=f32,
    )
    below, above = bases()
    for slab in range(slabs):
        for plane in range(6):
            at = (slab * 6 + plane) * NY
            rows = slice(at, at + NY)
            base = (slab * 6 + plane) * tall + 8
            own = y_ref[rows, :]
            lap = along_z[rows, :]
            for distance in range(1, reach + 1):
                beside = pad_ref[base + distance : base + distance + NY, :]
                beside = beside + pad_ref[base - distance : base - distance + NY, :]
                for index in (plane - distance, plane + distance):
                    if index < 0:
                        spot = pl.multiple_of(below[slab] + (index + 6) * NY, 8)
                        beside = beside + other_ref[pl.ds(spot, NY), :]
                    elif index >= 6:
                        spot = pl.multiple_of(above[slab] + (index - 6) * NY, 8)
                        beside = beside + other_ref[pl.ds(spot, NY), :]
                    else:
                        spot = (slab * 6 + index) * NY
                        beside = beside + y_ref[spot : spot + NY, :]
                lap = lap + stencil_weights[distance] * beside
            if v_ref is None:
                value = scale * (-filter_center * own - 0.5 * lap)
            else:
                value = scale * ((v_ref[rows, :] - filter_center) * own - 0.5 * lap)
            if prev_ref is not None:
                value = value - prev_ref[rows, :]
            out_ref[rows, :] = value


def pack_kernel(dims, *refs):
    n, cap, nproj, foot, chunk = dims
    lanes = n * chunk
    sources, (pack_ref, p_ref), scratch = refs[:6], refs[6:8], refs[8:]
    off_ref, atom_ref, dmat_ref, r_ref, sems = scratch
    small = pack_ref.shape[0] - SMALL
    targets = (
        pack_ref.at[0:SLAB, :],
        p_ref,
        off_ref,
        atom_ref,
        dmat_ref,
        pack_ref.at[SLAB:small, :],
    )
    copies = [
        pltpu.make_async_copy(source, target, sems.at[index])
        for index, (source, target) in enumerate(zip(sources, targets))
    ]
    for copy in copies:
        copy.start()
    for copy in copies[2:]:
        copy.wait()
    lane = iota((1, lanes), 1) // nproj
    atoms = jnp.zeros((1, lanes), f32)
    starts = jnp.zeros((1, lanes), f32)
    for slot in range(n * cap):
        here = lane == slot
        atoms = jnp.where(here, atom_ref[slot % cap, slot // cap].astype(f32), atoms)
        starts = jnp.where(here, off_ref[slot % cap, slot // cap].astype(f32), starts)
    pack_ref[small + 1 : small + 2, :] = atoms
    pack_ref[small + 2 : small + 3, :] = starts
    pack_ref[small + 3 : small + 8, :] = jnp.zeros((5, 128), f32)
    count = dmat_ref.shape[1]
    for group in range(128 // count):
        block = dmat_ref[group * 2 * nproj : (group + 1) * 2 * nproj, :]
        pack_ref[small + 8 :, group * count : (group + 1) * count] = block
    copies[0].wait()
    copies[1].wait()
    pack_ref[small : small + 1, :] = partials(pack_ref, p_ref, off_ref, r_ref, dims)[0:1]


def sort_kernel(*refs):
    packs, (pair_ref, v_ref) = refs[:-4], refs[-3:-1]
    small = packs[0].shape[0] - SMALL
    size = SLAB + SMALL
    for local, pack in enumerate(packs):
        pair_ref[local * size : local * size + SLAB, :] = pack[0:SLAB, :]
        pair_ref[local * size + SLAB : (local + 1) * size, :] = pack[small:, :]
        v_ref[local * (small - SLAB) : (local + 1) * (small - SLAB), :] = pack[SLAB:small, :]


def relay_kernel(x_ref, y_ref, top_ref, bottom_ref):
    rows = top_ref.shape[0]
    top_ref[...] = x_ref[0:rows, :]
    bottom_ref[...] = y_ref[rows:, :]


def begin_kernel(dims, info_ref, own_ref, got_ref, *refs):
    n, cap, nproj, foot, chunk = dims
    half = n // 2
    part_ref, y_ref, w_ref, c_ref, int_ref, other_ref, pad_ref, dmat_ref = refs
    lanes = n * chunk
    size = SLAB + SMALL
    c_rows, atom_rows, start_rows = [], [], []
    for group, source in enumerate((own_ref, got_ref)):
        for local in range(half):
            slab = local * size
            rows = slice(local * SLAB, (local + 1) * SLAB)
            target = other_ref if group else y_ref
            target[rows, :] = source[slab : slab + SLAB, :]
            small = slab + SLAB
            c_rows.append(source[small : small + 1, :])
            atom_rows.append(source[small + 1 : small + 2, :])
            if group == 0:
                start_rows.append(source[small + 2 : small + 3, :])
            dmat_ref[group * half + local] = source[small + 8 : small + SMALL, :]
    other_ref[half * SLAB :, :] = jnp.zeros((SLAB, 128), f32)
    c_ref[...] = by_owner(jnp.concatenate(c_rows, 0), n, chunk)
    atoms = by_owner(jnp.concatenate(atom_rows, 0), n, chunk)
    lane = iota((1, 128), 1)
    table = jnp.zeros((1, 128), jnp.int32)
    for local in range(half):
        int_ref[local : local + 1, :] = start_rows[local].astype(jnp.int32)
        for side in range(2):
            value = info_ref[(2 + side) * half + local]
            table = jnp.where(lane == side * half + local, value, table)
    table = jnp.where(lane == 2 * half, info_ref[4 * half + n], table)
    int_ref[half : half + 1, :] = table
    int_ref[half + 1 :, :] = jnp.zeros((8 - half - 1, 128), jnp.int32)

    def bases():
        return (
            [info_ref[2 * half + local] for local in range(half)],
            [info_ref[3 * half + local] for local in range(half)],
        )

    stencil(
        y_ref, other_ref, None, None, part_ref, pad_ref, half, 1.0 / filter_half_width, bases
    )
    square = (lanes, 128)
    diagonal = iota(square, 0) == iota(square, 1)
    ones = jnp.ones((128, 128), f32)
    column = iota(square, 1).astype(f32)
    count = 128 // (nproj // 2)
    shift = (iota(square, 0) % nproj // 2 * count).astype(f32)
    wide, picks = [], []
    for local in range(half):
        held = jnp.where(diagonal, atom_rows[local], 0.0)
        mine = jnp.dot(held, ones, precision=highest, preferred_element_type=f32)
        mine = jnp.round(mine)
        wide.append(mine)
        picks.append(jnp.where((column == shift + mine) & (mine >= 0.0), 1.0, 0.0))
    tall = half * chunk
    parity = iota((tall, 2 * nproj), 1) // nproj == iota((tall, 2 * nproj), 0) % 2
    spread = iota((2 * nproj, 128), 1) % nproj == iota((2 * nproj, 128), 0) % nproj
    spread = jnp.where(spread, 1.0, 0.0)
    for owner in range(n):
        rows = slice(owner * chunk, (owner + 1) * chunk)
        pick = jnp.concatenate([p[rows, :] for p in picks], 0)
        mine = jnp.concatenate([m[rows, :] for m in wide], 0)
        entries = lax.dot_general(
            pick,
            dmat_ref[info_ref[4 * half + owner]],
            (((1,), (1,)), ((), ())),
            precision=highest,
            preferred_element_type=f32,
        )
        entries = jnp.where(parity, entries, 0.0)
        block = jnp.dot(entries, spread, precision=highest, preferred_element_type=f32)
        same = (atoms[owner : owner + 1, :] == mine) & (mine >= 0.0)
        w_ref[owner * tall : (owner + 1) * tall, :] = jnp.where(same, block, 0.0)


def p_rows(p_refs, slab, slot, nproj, tile):
    ref, at = p_refs[slab], slot * nproj
    if at >= ref.shape[0]:
        ref, at = p_refs[slab + 1], at - ref.shape[0]
    return ref[at : at + nproj, tile * 128 : (tile + 1) * 128]


def couple(dims, slabs, half, coefficients, w_ref, p_refs, start_of, out_ref, scale):
    n, cap, nproj, foot, chunk = dims
    sublane = iota((foot, 128), 0)
    for slab in range(slabs):
        for slot in range(n * cap):
            owner, k = slot // cap, slot % cap
            at = (owner * half + slab) * chunk + k * nproj
            returned = jnp.sum(
                w_ref[at : at + nproj, :] * coefficients[owner : owner + 1, :],
                axis=1,
                keepdims=True,
            )
            returned = jnp.broadcast_to(returned * scale, (nproj, 128))
            contrib = jnp.zeros((foot, 128), f32)
            for tile in range(foot):
                term = jnp.sum(
                    p_rows(p_refs, slab, slot, nproj, tile) * returned,
                    axis=0,
                    keepdims=True,
                )
                contrib = jnp.where(sublane == tile, term, contrib)
            spot = pl.ds(start_of(slab, slot), foot)
            out_ref[spot, :] = out_ref[spot, :] + contrib


def next_partials(dims, half, send_ref, p_refs, start_of, r_ref):
    n, cap, nproj, foot, chunk = dims
    lanes = n * chunk
    for slab in range(half):
        for slot in range(n * cap):
            start = start_of(slab, slot)
            total = None
            for tile in range(foot):
                cells = jnp.broadcast_to(send_ref[pl.ds(start + tile, 1), :], (nproj, 128))
                term = p_rows(p_refs, slab, slot, nproj, tile) * cells
                total = term if total is None else total + term
            r_ref[slab * lanes + slot * nproj : slab * lanes + (slot + 1) * nproj, :] = total
    row = lax.dot_general(
        jnp.ones((8, 128), f32),
        r_ref[...],
        (((1,), (1,)), ((), ())),
        precision=highest,
        preferred_element_type=f32,
    )
    for slab in range(half):
        send_ref[half * SLAB + slab : half * SLAB + slab + 1, :] = row[
            0:1, slab * lanes : (slab + 1) * lanes
        ]
    send_ref[half * SLAB + half :, :] = jnp.zeros((8 - half, 128), f32)


def starts_from(int_s, nproj):
    return lambda slab, slot: slab * SLAB + int_s[slab, slot * nproj]


def potential_kernel(nband, table_ref, part_ref, y_ref, *refs):
    pieces, (out_ref, v_ref, int_s, sem) = refs[:nband], refs[nband:]
    copy = pltpu.make_async_copy(table_ref, int_s, sem)
    copy.start()
    copy.wait()
    scale = 1.0 / filter_half_width
    piece = NY // nband
    for back in range(nband):
        at = lax.rem(int_s[4, 8] - back + nband, nband) * piece
        for plane in range(part_ref.shape[0] // NY):
            spot = pl.ds(pl.multiple_of(plane * NY + at, 8), piece)
            value = pieces[back][plane * piece : (plane + 1) * piece, :]
            v_ref[spot, :] = value
            out_ref[spot, :] = part_ref[spot, :] + scale * (value * y_ref[spot, :])


def first_kernel(dims, *refs):
    n, cap, nproj, foot, chunk = dims
    half = n // 2
    int_ref, part_ref, w_ref, c_ref = refs[:4]
    p_refs, (send_ref, r_ref, int_s, sem) = refs[4 : 5 + half], refs[5 + half :]
    copy = pltpu.make_async_copy(int_ref, int_s, sem)
    copy.start()
    send_ref[0 : half * SLAB, :] = part_ref[...]
    copy.wait()
    start_of = starts_from(int_s, nproj)
    scale = 1.0 / filter_half_width
    couple(dims, half, half, c_ref[...], w_ref, p_refs, start_of, send_ref, scale)
    next_partials(dims, half, send_ref, p_refs, start_of, r_ref)


def chip_kernel(dims, last, *refs):
    n, cap, nproj, foot, chunk = dims
    half = n // 2
    int_ref, y_ref, got_ref, prev_ref, v_ref, w_ref = refs[:6]
    p_refs = refs[6 : 7 + half]
    out_ref, other_ref, pad_ref, int_s, sem = refs[7 + half : 12 + half]
    copy = pltpu.make_async_copy(int_ref, int_s, sem)
    copy.start()
    other_ref[0 : half * SLAB, :] = got_ref[0 : half * SLAB, :]
    other_ref[half * SLAB :, :] = jnp.zeros((SLAB, 128), f32)
    slabs = 1 if last else half
    scale = 2.0 / filter_half_width

    def bases():
        copy.wait()
        return (
            [int_s[half, local] for local in range(half)],
            [int_s[half, half + local] for local in range(half)],
        )

    stencil(y_ref, other_ref, v_ref, prev_ref, out_ref, pad_ref, slabs, scale, bases)
    below = slice(half * SLAB, half * SLAB + half)
    rows = jnp.concatenate([y_ref[below, :], got_ref[below, :]], 0)
    coefficients = by_owner(rows, n, chunk)
    start_of = starts_from(int_s, nproj)
    couple(dims, slabs, half, coefficients, w_ref, p_refs, start_of, out_ref, scale)
    if not last:
        next_partials(dims, half, out_ref, p_refs, start_of, refs[12 + half])


def chip_table(n):
    half = n // 2
    table = np.zeros((n, 4 * half + n), np.int32)
    for device in range(n):
        chip, core = device // 2, device % 2
        for local in range(half):
            there = chip ^ local
            same = local * SLAB
            far = there + (1 if core else -1)
            cross = (far ^ chip) * SLAB if 0 <= far < half else half * SLAB
            table[device, 2 * half + local] = same if core else cross
            table[device, 3 * half + local] = cross if core else same
        for owner in range(n):
            table[device, 4 * half + owner] = owner % 2 * half if core == 0 else (1 - owner % 2) * half
            table[device, 4 * half + owner] += owner // 2 ^ chip
    return table


def chip_form(psi, potential, projectors, offsets, intersection, dmat):
    n = lax.axis_size("domain")
    nband = lax.axis_size("band")
    cap, nproj = projectors.shape[2], projectors.shape[3]
    foot = projectors.shape[4] // 128
    chunk = cap * nproj
    lanes = n * chunk
    half = n // 2
    dims = (n, cap, nproj, foot, chunk)
    p = projectors.reshape(lanes, foot * 128)
    v_piece = potential.reshape(-1, 128)
    couplings = dmat.transpose(1, 2, 0).reshape(nproj * nproj, dmat.shape[0])
    domain = lax.axis_index("domain")
    info = jnp.concatenate(
        [
            lax.dynamic_slice_in_dim(jnp.asarray(chip_table(n)), domain, 1, 0)[0],
            lax.axis_index("band").astype(jnp.int32)[None],
        ]
    )
    params = pltpu.CompilerParams(vmem_limit_bytes=40 * 1024 * 1024)
    HBM = pl.BlockSpec(memory_space=pltpu.HBM)
    small = pl.CostEstimate(flops=1, bytes_accessed=1, transcendentals=0)
    large = pl.CostEstimate(flops=10**10, bytes_accessed=1, transcendentals=0)
    larger = pl.CostEstimate(flops=10**10, bytes_accessed=1, transcendentals=0)

    def shape(rows, dtype=f32):
        return jax.ShapeDtypeStruct((rows, 128), dtype)

    def swap(x, step):
        return lax.ppermute(x, "domain", [(i, i ^ step) for i in range(n)])

    sources = (psi.reshape(SLAB, 128), p, offsets[0].T, intersection[0].T, couplings, v_piece)
    sources = [pltpu.with_memory_space_constraint(x, pltpu.HBM) for x in sources]
    pack, p = pl.pallas_call(
        functools.partial(pack_kernel, dims),
        out_shape=(
            shape(SLAB + v_piece.shape[0] + SMALL),
            jax.ShapeDtypeStruct(p.shape, f32),
        ),
        in_specs=[HBM] * 6,
        out_specs=(VMEM, VMEM),
        scratch_shapes=[
            pltpu.SMEM((cap, n), jnp.int32),
            pltpu.SMEM((cap, n), jnp.int32),
            pltpu.VMEM(couplings.shape, f32),
            pltpu.VMEM((lanes, 128), f32),
            pltpu.SemaphoreType.DMA((6,)),
        ],
        compiler_params=params,
        cost_estimate=small,
        name="pack",
    )(*sources)
    packs = [pack] + [swap(pack, 2 * local) for local in range(1, half)]
    own, v_piece, p = pl.pallas_call(
        sort_kernel,
        out_shape=(
            shape(half * (SLAB + SMALL)),
            shape(half * v_piece.shape[0]),
            jax.ShapeDtypeStruct(p.shape, f32),
        ),
        in_specs=[VMEM] * (half + 1),
        out_specs=(VMEM,) * 3,
        input_output_aliases={half: 2},
        compiler_params=params,
        cost_estimate=small,
        name="sort",
    )(*packs, p)
    got = swap(own, 1)
    pieces = [v_piece]
    for back in range(1, nband):
        ring = [(i, (i + back) % nband) for i in range(nband)]
        pieces.append(lax.ppermute(v_piece, "band", ring))
    p_x, p_y = swap(p, 2), swap(p, 4)
    halves = (jax.ShapeDtypeStruct((lanes // 2, foot * 128), f32),) * 2
    top, bottom = pl.pallas_call(
        relay_kernel,
        out_shape=halves,
        in_specs=[VMEM] * 2,
        out_specs=(VMEM, VMEM),
        compiler_params=params,
        cost_estimate=large,
        name="relay",
    )(p_x, p_y)
    all_p = [p, p_x, p_y, swap(top, 4), swap(bottom, 2)]
    other = pltpu.VMEM(((half + 1) * SLAB, 128), f32)
    padded = pltpu.VMEM((half * 6 * (NY + 16), 128), f32)
    row_scratch = pltpu.VMEM((half * lanes, 128), f32)
    ints = [pltpu.SMEM((8, 128), jnp.int32), pltpu.SemaphoreType.DMA(())]
    part, previous, w, c, table = pl.pallas_call(
        functools.partial(begin_kernel, dims),
        out_shape=(
            shape(half * SLAB),
            shape(half * SLAB),
            shape(half * lanes),
            shape(n),
            shape(8, jnp.int32),
        ),
        in_specs=[SMEM] + [VMEM] * 2,
        out_specs=(VMEM,) * 5,
        scratch_shapes=[other, padded, pltpu.VMEM((n, 2 * nproj, 128), f32)],
        compiler_params=params,
        cost_estimate=small,
        name="begin",
    )(info, own, got)
    sent = shape(half * SLAB + 8)
    part, v = pl.pallas_call(
        functools.partial(potential_kernel, nband),
        out_shape=(shape(half * SLAB), shape(half * SLAB)),
        in_specs=[VMEM] * (3 + nband),
        out_specs=(VMEM, VMEM),
        scratch_shapes=ints,
        compiler_params=params,
        cost_estimate=larger,
        name="potential",
    )(table, part, previous, *pieces)
    y = pl.pallas_call(
        functools.partial(first_kernel, dims),
        out_shape=sent,
        in_specs=[VMEM] * (5 + half),
        out_specs=VMEM,
        scratch_shapes=[row_scratch] + ints,
        compiler_params=params,
        name="first",
    )(table, part, w, c, *all_p)
    for degree in range(1, DEGREE):
        last = degree == DEGREE - 1
        following = pl.pallas_call(
            functools.partial(chip_kernel, dims, last),
            out_shape=shape(SLAB) if last else sent,
            in_specs=[VMEM] * (7 + half),
            out_specs=VMEM,
            scratch_shapes=[other, padded] + ints + ([] if last else [row_scratch]),
            compiler_params=params,
            name="last" if last else "next",
        )(table, y, swap(y, 1), previous, v, w, *all_p)
        previous, y = y, following
    return y.reshape(psi.shape)


def shards(psi, potential, projectors, offsets, intersection, dmat):
    n = lax.axis_size("domain")
    nband = lax.axis_size("band")
    fits = n == 8 and potential.shape[1] % 8 == 0 and nband <= 8
    form = chip_form if fits else slab_form
    return form(psi, potential, projectors, offsets, intersection, dmat)


def solution(mesh):
    return jax.shard_map(
        shards,
        mesh=mesh,
        in_specs=(
            P("band", "domain", None, None),
            P("domain", "band", None),
            P("domain", None, None, None, None),
            P("domain", None, None),
            P("domain", None, None),
            P("domain", None, None),
        ),
        out_specs=P("band", "domain", None, None),
        check_vma=False,
    )
```

```python
import functools

import jax
import jax.numpy as jnp
import numpy as np
from jax import lax
from jax.experimental import pallas as pl
from jax.experimental.pallas import tpu as pltpu
from jax.sharding import PartitionSpec as P

DEGREE = 4

stencil_weights = (
    -5369.0 / 1800.0,
    12.0 / 7.0,
    -15.0 / 56.0,
    10.0 / 189.0,
    -1.0 / 112.0,
    2.0 / 1925.0,
    -1.0 / 16632.0,
)
reach = len(stencil_weights) - 1
filter_center = 6.0
filter_half_width = 4.0
highest = lax.Precision.HIGHEST
f32 = jnp.float32
VMEM = pl.BlockSpec(memory_space=pltpu.VMEM)
SMEM = pl.BlockSpec(memory_space=pltpu.SMEM)


def iota(shape, dim):
    return lax.broadcasted_iota(jnp.int32, shape, dim)


def partials(y_ref, p_ref, off_ref, r_ref, dims):
    n, cap, nproj, foot, chunk = dims
    for slot in range(n * cap):
        start = off_ref[slot % cap, slot // cap]
        rows = pl.ds(slot * nproj, nproj)
        total = None
        for tile in range(foot):
            cells = jnp.broadcast_to(y_ref[pl.ds(start + tile, 1), :], (nproj, 128))
            term = p_ref[rows, tile * 128 : (tile + 1) * 128] * cells
            total = term if total is None else total + term
        r_ref[rows, :] = total
    return lax.dot_general(
        jnp.ones((8, 128), f32),
        r_ref[...],
        (((1,), (1,)), ((), ())),
        precision=highest,
        preferred_element_type=f32,
    )


def by_owner(rows, n, chunk):
    lanes = n * chunk
    shape = (n, lanes)
    ahead = (iota(shape, 1) // chunk - iota(shape, 0) + n) % n
    out = rows
    for step in range(1, n):
        moved = pltpu.roll(rows, n - step, 0)
        moved = pltpu.roll(moved, step * chunk, 1)
        out = jnp.where(ahead == step, moved, out)
    return out


def start_kernel(dims, y_ref, p_ref, off_ref, atom_ref, dmat_ref, out_ref, r_ref):
    n, cap, nproj, foot, chunk = dims
    lanes = n * chunk
    out_ref[:, 0, :] = jnp.broadcast_to(
        partials(y_ref, p_ref, off_ref, r_ref, dims)[0:1], (n, lanes)
    )
    lane = iota((1, lanes), 1) // nproj
    atoms = jnp.zeros((1, lanes), f32)
    for slot in range(n * cap):
        value = atom_ref[slot % cap, slot // cap].astype(f32)
        atoms = jnp.where(lane == slot, value, atoms)
    out_ref[:, 1, :] = jnp.broadcast_to(atoms, (n, lanes))
    count = dmat_ref.shape[1]
    for group in range(128 // count):
        block = dmat_ref[group * 2 * nproj : (group + 1) * 2 * nproj, :]
        for peer in range(n):
            out_ref[peer, 8:, group * count : (group + 1) * count] = block


def step_kernel(dims, nband, first, last, *refs):
    n, cap, nproj, foot, chunk = dims
    refs = list(refs)
    take = lambda: refs.pop(0)
    info_ref, off_ref = take(), take()
    y_ref, a_ref, b_ref, got_ref, p_ref = take(), take(), take(), take(), take()
    if first:
        atom_ref = take()
        v_pieces = [take() for _ in range(nband)]
        prev_ref = None
    else:
        prev_ref, v_ref, w_ref = take(), take(), take()
    out_ref = take()
    if not last:
        c_ref = take()
    if first:
        v_ref, w_ref = take(), take()
    pad_ref, lo_ref, hi_ref, r_ref = take(), take(), take(), take()
    cells = y_ref.shape[0]
    ny = 32
    planes = cells // ny
    lanes = n * chunk
    weights = stencil_weights

    if first:
        if nband > 1:
            piece_rows = ny // nband
            for back, piece in enumerate(v_pieces):
                at = lax.rem(info_ref[1] - back + nband, nband) * piece_rows
                for plane in range(planes):
                    spot = pl.multiple_of(plane * ny + at, 8)
                    v_ref[pl.ds(spot, piece_rows), :] = piece[
                        plane * piece_rows : (plane + 1) * piece_rows, :
                    ]
        else:
            v_ref[...] = v_pieces[0][...]
        atoms = by_owner(got_ref[:, 1, :], n, chunk)
        row = iota((chunk, 128), 0)
        column = iota((chunk, 128), 1)
        count = 128 // (nproj // 2)
        parity = (iota((chunk, 2 * nproj), 1) // nproj) == (iota((chunk, 2 * nproj), 0) % 2)
        spread = (iota((2 * nproj, lanes), 1) % nproj == iota((2 * nproj, lanes), 0) % nproj)
        spread = spread.astype(f32)
        for owner in range(n):
            mine = jnp.zeros((chunk, 128), jnp.int32)
            for k in range(cap):
                mine = jnp.where(row // nproj == k, atom_ref[k, owner], mine)
            pick = (column == (row % nproj) // 2 * count + mine) & (mine >= 0)
            entries = lax.dot_general(
                pick.astype(f32),
                got_ref[owner, 8:, 0:128],
                (((1,), (1,)), ((), ())),
                precision=highest,
                preferred_element_type=f32,
            )
            entries = jnp.where(parity, entries, 0.0)
            block = jnp.dot(entries, spread, precision=highest, preferred_element_type=f32)
            mine_row = jnp.zeros((chunk, lanes), f32)
            row_wide = iota((chunk, lanes), 0) // nproj
            for k in range(cap):
                mine_row = jnp.where(row_wide == k, atom_ref[k, owner].astype(f32), mine_row)
            same = (atoms[owner : owner + 1, :] == mine_row) & (mine_row >= 0.0)
            w_ref[pl.ds(owner * chunk, chunk), :] = jnp.where(same, block, 0.0)
        coefficients = by_owner(got_ref[:, 0, :], n, chunk)
    else:
        coefficients = by_owner(got_ref[...], n, chunk)

    odd = jnp.full((cells, 128), info_ref[0], jnp.int32) == 1
    from_a, from_b = a_ref[...], b_ref[...]
    lo_ref[...] = jnp.where(odd, from_a, from_b)
    hi_ref[...] = jnp.where(odd, from_b, from_a)
    tall = ny + 16
    for plane in range(planes):
        own = y_ref[plane * ny : (plane + 1) * ny, :]
        base = plane * tall
        pad_ref[base + 8 : base + 8 + ny, :] = own
        pad_ref[base : base + 8, :] = own[ny - 8 :, :]
        pad_ref[base + 8 + ny : base + tall, :] = own[0:8, :]

    apart = iota((128, 128), 0) - iota((128, 128), 1)
    apart = jnp.abs(apart)
    apart = jnp.minimum(apart, 128 - apart)
    circulant = jnp.full((128, 128), 3.0 * weights[0], f32)
    circulant = jnp.where(apart > reach, 0.0, circulant)
    for distance in range(1, reach + 1):
        circulant = jnp.where(apart == distance, weights[distance], circulant)
    along_z = jnp.dot(y_ref[...], circulant, precision=highest, preferred_element_type=f32)

    scale = (1.0 if first else 2.0) / filter_half_width

    def plane_of(index):
        if index < 0:
            ref, index = lo_ref, index + planes
        elif index >= planes:
            ref, index = hi_ref, index - planes
        else:
            ref = y_ref
        return ref[index * ny : (index + 1) * ny, :]

    for plane in range(planes):
        rows = slice(plane * ny, (plane + 1) * ny)
        base = plane * tall + 8
        own = y_ref[rows, :]
        lap = along_z[rows, :]
        for distance in range(1, reach + 1):
            beside = plane_of(plane + distance) + plane_of(plane - distance)
            beside = beside + pad_ref[base + distance : base + distance + ny, :]
            beside = beside + pad_ref[base - distance : base - distance + ny, :]
            lap = lap + weights[distance] * beside
        value = scale * ((v_ref[rows, :] - filter_center) * own - 0.5 * lap)
        if prev_ref is not None:
            value = value - prev_ref[rows, :]
        out_ref[rows, :] = value

    sublane = iota((foot, 128), 0)
    for slot in range(n * cap):
        owner = slot // cap
        rows = slice(slot * nproj, (slot + 1) * nproj)
        returned = jnp.sum(
            w_ref[rows, :] * coefficients[owner : owner + 1, :], axis=1, keepdims=True
        )
        returned = jnp.broadcast_to(returned * scale, (nproj, 128))
        contrib = jnp.zeros((foot, 128), f32)
        for tile in range(foot):
            term = jnp.sum(
                p_ref[rows, tile * 128 : (tile + 1) * 128] * returned, axis=0, keepdims=True
            )
            contrib = jnp.where(sublane == tile, term, contrib)
        start = off_ref[slot % cap, slot // cap]
        out_ref[pl.ds(start, foot), :] = out_ref[pl.ds(start, foot), :] + contrib

    if not last:
        c_ref[...] = jnp.broadcast_to(
            partials(out_ref, p_ref, off_ref, r_ref, dims)[0:1], (n, lanes)
        )


def beside_slabs(y, n):
    pairs = [(i, i ^ 1) for i in range(n) if i ^ 1 < n]
    cross = [(i, i + 1) for i in range(1, n - 1, 2)] + [(i + 1, i) for i in range(1, n - 1, 2)]
    return lax.ppermute(y, "domain", pairs), lax.ppermute(y, "domain", cross)


def slab_form(psi, potential, projectors, offsets, intersection, dmat):
    n = lax.axis_size("domain")
    nband = lax.axis_size("band")
    cap, nproj = projectors.shape[2], projectors.shape[3]
    foot = projectors.shape[4] // 128
    chunk = cap * nproj
    lanes = n * chunk
    dims = (n, cap, nproj, foot, chunk)
    cells = psi.shape[1] * psi.shape[2]
    y = psi.reshape(cells, 128)
    p = projectors.reshape(lanes, foot * 128)
    off = offsets[0].T
    atom = intersection[0].T
    couplings = dmat.transpose(1, 2, 0).reshape(nproj * nproj, dmat.shape[0])
    info = jnp.stack([lax.axis_index("domain") % 2, lax.axis_index("band")]).astype(jnp.int32)
    params = pltpu.CompilerParams(vmem_limit_bytes=40 * 1024 * 1024)

    start = pl.pallas_call(
        functools.partial(start_kernel, dims),
        out_shape=jax.ShapeDtypeStruct((n, 24, lanes), f32),
        in_specs=[VMEM, VMEM, SMEM, SMEM, VMEM],
        out_specs=VMEM,
        scratch_shapes=[pltpu.VMEM((lanes, 128), f32)],
        compiler_params=params,
        name="first_partials",
    )
    got = lax.all_to_all(
        start(y, p, off, atom, couplings), "domain", split_axis=0, concat_axis=0, tiled=True
    )
    if potential.shape[1] % 8 == 0 and nband <= 8:
        pieces = [potential.reshape(-1, 128)]
        for back in range(1, nband):
            ring = [(i, (i + back) % nband) for i in range(nband)]
            pieces.append(lax.ppermute(pieces[0], "band", ring))
    else:
        pieces = [lax.all_gather(potential, "band", axis=1, tiled=True).reshape(cells, 128)]

    y_shape = jax.ShapeDtypeStruct((cells, 128), f32)
    c_shape = jax.ShapeDtypeStruct((n, lanes), f32)
    scratch = [
        pltpu.VMEM((cells // 32 * 48, 128), f32),
        pltpu.VMEM((cells, 128), f32),
        pltpu.VMEM((cells, 128), f32),
        pltpu.VMEM((lanes, 128), f32),
    ]
    from_a, from_b = beside_slabs(y, n)
    previous = y
    y, c, v, w = pl.pallas_call(
        functools.partial(step_kernel, dims, len(pieces), True, False),
        out_shape=(y_shape, c_shape, y_shape, jax.ShapeDtypeStruct((lanes, lanes), f32)),
        in_specs=[SMEM, SMEM] + [VMEM] * 5 + [SMEM] + [VMEM] * len(pieces),
        out_specs=(VMEM,) * 4,
        scratch_shapes=scratch,
        compiler_params=params,
        name="first_step",
    )(info, off, y, from_a, from_b, got, p, atom, *pieces)
    for degree in range(1, DEGREE):
        last = degree == DEGREE - 1
        got = lax.all_to_all(c, "domain", split_axis=0, concat_axis=0, tiled=True)
        from_a, from_b = beside_slabs(y, n)
        out = pl.pallas_call(
            functools.partial(step_kernel, dims, len(pieces), False, last),
            out_shape=(y_shape,) if last else (y_shape, c_shape),
            in_specs=[SMEM, SMEM] + [VMEM] * 8,
            out_specs=(VMEM,) if last else (VMEM, VMEM),
            scratch_shapes=scratch,
            compiler_params=params,
            name="last_step" if last else "next_step",
        )(info, off, y, from_a, from_b, got, p, previous, v, w)
        previous, y = y, out[0]
        if not last:
            c = out[1]
    return y.reshape(psi.shape)


NY = 32
SLAB = 6 * NY
SMALL = 24


def circulant_z():
    apart = jnp.abs(iota((128, 128), 0) - iota((128, 128), 1))
    apart = jnp.minimum(apart, 128 - apart)
    out = jnp.full((128, 128), 3.0 * stencil_weights[0], f32)
    out = jnp.where(apart > reach, 0.0, out)
    for distance in range(1, reach + 1):
        out = jnp.where(apart == distance, stencil_weights[distance], out)
    return out


def stencil(y_ref, other_ref, v_ref, prev_ref, out_ref, pad_ref, slabs, scale, bases):
    tall = NY + 16
    for plane in range(6 * slabs):
        own = y_ref[plane * NY : (plane + 1) * NY, :]
        base = plane * tall
        pad_ref[base + 8 : base + 8 + NY, :] = own
        pad_ref[base : base + 8, :] = own[NY - 8 :, :]
        pad_ref[base + 8 + NY : base + tall, :] = own[0:8, :]
    along_z = jnp.dot(
        y_ref[0 : slabs * SLAB, :],
        circulant_z(),
        precision=highest,
        preferred_element_type=f32,
    )
    below, above = bases()
    for slab in range(slabs):
        for plane in range(6):
            at = (slab * 6 + plane) * NY
            rows = slice(at, at + NY)
            base = (slab * 6 + plane) * tall + 8
            own = y_ref[rows, :]
            lap = along_z[rows, :]
            for distance in range(1, reach + 1):
                beside = pad_ref[base + distance : base + distance + NY, :]
                beside = beside + pad_ref[base - distance : base - distance + NY, :]
                for index in (plane - distance, plane + distance):
                    if index < 0:
                        spot = pl.multiple_of(below[slab] + (index + 6) * NY, 8)
                        beside = beside + other_ref[pl.ds(spot, NY), :]
                    elif index >= 6:
                        spot = pl.multiple_of(above[slab] + (index - 6) * NY, 8)
                        beside = beside + other_ref[pl.ds(spot, NY), :]
                    else:
                        spot = (slab * 6 + index) * NY
                        beside = beside + y_ref[spot : spot + NY, :]
                lap = lap + stencil_weights[distance] * beside
            if v_ref is None:
                value = scale * (-filter_center * own - 0.5 * lap)
            else:
                value = scale * ((v_ref[rows, :] - filter_center) * own - 0.5 * lap)
            if prev_ref is not None:
                value = value - prev_ref[rows, :]
            out_ref[rows, :] = value


def pack_kernel(dims, *refs):
    n, cap, nproj, foot, chunk = dims
    lanes = n * chunk
    sources, (pack_ref, top_ref, bottom_ref), scratch = refs[:6], refs[6:9], refs[9:]
    off_ref, atom_ref, dmat_ref, r_ref, sems = scratch
    small = pack_ref.shape[0] - SMALL
    targets = (
        pack_ref.at[0:SLAB, :],
        top_ref,
        bottom_ref,
        off_ref,
        atom_ref,
        dmat_ref,
        pack_ref.at[SLAB:small, :],
    )
    rows = top_ref.shape[0]
    p_ref = sources[1]
    sources = (sources[0], p_ref.at[0:rows, :], p_ref.at[rows:, :], *sources[2:6])
    copies = [
        pltpu.make_async_copy(source, target, sems.at[index])
        for index, (source, target) in enumerate(zip(sources, targets))
    ]
    for copy in copies:
        copy.start()
    for copy in copies[3:]:
        copy.wait()
    lane = iota((1, lanes), 1) // nproj
    atoms = jnp.zeros((1, lanes), f32)
    starts = jnp.zeros((1, lanes), f32)
    for slot in range(n * cap):
        here = lane == slot
        atoms = jnp.where(here, atom_ref[slot % cap, slot // cap].astype(f32), atoms)
        starts = jnp.where(here, off_ref[slot % cap, slot // cap].astype(f32), starts)
    pack_ref[small + 1 : small + 2, :] = atoms
    pack_ref[small + 2 : small + 3, :] = starts
    pack_ref[small + 3 : small + 8, :] = jnp.zeros((5, 128), f32)
    count = dmat_ref.shape[1]
    for group in range(128 // count):
        block = dmat_ref[group * 2 * nproj : (group + 1) * 2 * nproj, :]
        pack_ref[small + 8 :, group * count : (group + 1) * count] = block
    for copy in copies[:3]:
        copy.wait()
    p_refs, at = [top_ref, bottom_ref], lambda slab, slot: off_ref[slot % cap, slot // cap]
    fill_rows(dims, 0, pack_ref, p_refs, at, r_ref)
    pack_ref[small : small + 1, :] = row_sums(r_ref)[0:1, :]


def sort_kernel(*refs):
    packs, (pair_ref, v_ref) = refs[:-2], refs[-2:]
    small = packs[0].shape[0] - SMALL
    size = SLAB + SMALL
    for local, pack in enumerate(packs):
        pair_ref[local * size : local * size + SLAB, :] = pack[0:SLAB, :]
        pair_ref[local * size + SLAB : (local + 1) * size, :] = pack[small:, :]
        v_ref[local * (small - SLAB) : (local + 1) * (small - SLAB), :] = pack[SLAB:small, :]


def relay_kernel(x_ref, out_ref):
    out_ref[...] = x_ref[...]


def begin_kernel(dims, info_ref, own_ref, got_ref, *refs):
    n, cap, nproj, foot, chunk = dims
    half = n // 2
    part_ref, y_ref, w_ref, c_ref, int_ref, other_ref, pad_ref, dmat_ref = refs
    lanes = n * chunk
    size = SLAB + SMALL
    c_rows, atom_rows, start_rows = [], [], []
    for group, source in enumerate((own_ref, got_ref)):
        for local in range(half):
            slab = local * size
            rows = slice(local * SLAB, (local + 1) * SLAB)
            target = other_ref if group else y_ref
            target[rows, :] = source[slab : slab + SLAB, :]
            small = slab + SLAB
            c_rows.append(source[small : small + 1, :])
            atom_rows.append(source[small + 1 : small + 2, :])
            if group == 0:
                start_rows.append(source[small + 2 : small + 3, :])
            dmat_ref[group * half + local] = source[small + 8 : small + SMALL, :]
    other_ref[half * SLAB :, :] = jnp.zeros((SLAB, 128), f32)
    c_ref[...] = by_owner(jnp.concatenate(c_rows, 0), n, chunk)
    atoms = by_owner(jnp.concatenate(atom_rows, 0), n, chunk)
    lane = iota((1, 128), 1)
    table = jnp.zeros((1, 128), jnp.int32)
    for local in range(half):
        int_ref[local : local + 1, :] = start_rows[local].astype(jnp.int32)
        for side in range(2):
            value = info_ref[(2 + side) * half + local]
            table = jnp.where(lane == side * half + local, value, table)
    table = jnp.where(lane == 2 * half, info_ref[4 * half + n], table)
    int_ref[half : half + 1, :] = table
    int_ref[half + 1 :, :] = jnp.zeros((8 - half - 1, 128), jnp.int32)

    def bases():
        return (
            [info_ref[2 * half + local] for local in range(half)],
            [info_ref[3 * half + local] for local in range(half)],
        )

    stencil(
        y_ref, other_ref, None, None, part_ref, pad_ref, half, 1.0 / filter_half_width, bases
    )
    square = (lanes, 128)
    diagonal = iota(square, 0) == iota(square, 1)
    ones = jnp.ones((128, 128), f32)
    column = iota(square, 1).astype(f32)
    count = 128 // (nproj // 2)
    shift = (iota(square, 0) % nproj // 2 * count).astype(f32)
    wide, picks = [], []
    for local in range(half):
        held = jnp.where(diagonal, atom_rows[local], 0.0)
        mine = jnp.dot(held, ones, precision=highest, preferred_element_type=f32)
        mine = jnp.round(mine)
        wide.append(mine)
        picks.append(jnp.where((column == shift + mine) & (mine >= 0.0), 1.0, 0.0))
    tall = half * chunk
    parity = iota((tall, 2 * nproj), 1) // nproj == iota((tall, 2 * nproj), 0) % 2
    spread = iota((2 * nproj, 128), 1) % nproj == iota((2 * nproj, 128), 0) % nproj
    spread = jnp.where(spread, 1.0, 0.0)
    for owner in range(n):
        rows = slice(owner * chunk, (owner + 1) * chunk)
        pick = jnp.concatenate([p[rows, :] for p in picks], 0)
        mine = jnp.concatenate([m[rows, :] for m in wide], 0)
        entries = lax.dot_general(
            pick,
            dmat_ref[info_ref[4 * half + owner]],
            (((1,), (1,)), ((), ())),
            precision=highest,
            preferred_element_type=f32,
        )
        entries = jnp.where(parity, entries, 0.0)
        block = jnp.dot(entries, spread, precision=highest, preferred_element_type=f32)
        same = (atoms[owner : owner + 1, :] == mine) & (mine >= 0.0)
        w_ref[owner * tall : (owner + 1) * tall, :] = jnp.where(same, block, 0.0)


def p_rows(p_refs, slab, slot, nproj, tile):
    at = slot * nproj
    rows = p_refs[2 * slab].shape[0]
    ref = p_refs[2 * slab + at // rows]
    return ref[at % rows : at % rows + nproj, tile * 128 : (tile + 1) * 128]


def couple(dims, slabs, half, coefficients, w_ref, p_refs, start_of, out_ref, scale):
    n, cap, nproj, foot, chunk = dims
    sublane = iota((foot, 128), 0)
    for slab in range(slabs):
        for slot in range(n * cap):
            owner, k = slot // cap, slot % cap
            at = (owner * half + slab) * chunk + k * nproj
            returned = jnp.sum(
                w_ref[at : at + nproj, :] * coefficients[owner : owner + 1, :],
                axis=1,
                keepdims=True,
            )
            returned = jnp.broadcast_to(returned * scale, (nproj, 128))
            contrib = jnp.zeros((foot, 128), f32)
            for tile in range(foot):
                term = jnp.sum(
                    p_rows(p_refs, slab, slot, nproj, tile) * returned,
                    axis=0,
                    keepdims=True,
                )
                contrib = jnp.where(sublane == tile, term, contrib)
            spot = pl.ds(start_of(slab, slot), foot)
            out_ref[spot, :] = out_ref[spot, :] + contrib


def fill_rows(dims, slab, y_ref, p_refs, start_of, r_ref):
    n, cap, nproj, foot, chunk = dims
    for slot in range(n * cap):
        start = start_of(slab, slot)
        total = None
        for tile in range(foot):
            cells = jnp.broadcast_to(y_ref[pl.ds(start + tile, 1), :], (nproj, 128))
            term = p_rows(p_refs, slab, slot, nproj, tile) * cells
            total = term if total is None else total + term
        at = (slab * n * cap + slot) * nproj
        r_ref[at : at + nproj, :] = total


def row_sums(r_ref):
    return lax.dot_general(
        jnp.ones((8, 128), f32),
        r_ref[...],
        (((1,), (1,)), ((), ())),
        precision=highest,
        preferred_element_type=f32,
    )


def next_partials(dims, half, send_ref, p_refs, start_of, r_ref):
    n, cap, nproj, foot, chunk = dims
    lanes = n * chunk
    for slab in range(half):
        fill_rows(dims, slab, send_ref, p_refs, start_of, r_ref)
    row = row_sums(r_ref)
    for slab in range(half):
        send_ref[half * SLAB + slab : half * SLAB + slab + 1, :] = row[
            0:1, slab * lanes : (slab + 1) * lanes
        ]
    send_ref[half * SLAB + half :, :] = jnp.zeros((8 - half, 128), f32)


def starts_from(int_s, nproj):
    return lambda slab, slot: slab * SLAB + int_s[slab, slot * nproj]


def potential_kernel(nband, table_ref, part_ref, y_ref, *refs):
    pieces, (out_ref, v_ref, int_s, sem) = refs[:nband], refs[nband:]
    copy = pltpu.make_async_copy(table_ref, int_s, sem)
    copy.start()
    copy.wait()
    scale = 1.0 / filter_half_width
    piece = NY // nband
    for back in range(nband):
        at = lax.rem(int_s[4, 8] - back + nband, nband) * piece
        for plane in range(part_ref.shape[0] // NY):
            spot = pl.ds(pl.multiple_of(plane * NY + at, 8), piece)
            value = pieces[back][plane * piece : (plane + 1) * piece, :]
            v_ref[spot, :] = value
            out_ref[spot, :] = part_ref[spot, :] + scale * (value * y_ref[spot, :])


def first_kernel(dims, *refs):
    n, cap, nproj, foot, chunk = dims
    half = n // 2
    int_ref, part_ref, w_ref, c_ref = refs[:4]
    p_refs, (send_ref, r_ref, int_s, sem) = refs[4 : 4 + 2 * half], refs[4 + 2 * half :]
    copy = pltpu.make_async_copy(int_ref, int_s, sem)
    copy.start()
    send_ref[0 : half * SLAB, :] = part_ref[...]
    copy.wait()
    start_of = starts_from(int_s, nproj)
    scale = 1.0 / filter_half_width
    couple(dims, half, half, c_ref[...], w_ref, p_refs, start_of, send_ref, scale)
    next_partials(dims, half, send_ref, p_refs, start_of, r_ref)


def chip_kernel(dims, last, *refs):
    n, cap, nproj, foot, chunk = dims
    half = n // 2
    int_ref, y_ref, got_ref, prev_ref, v_ref, w_ref = refs[:6]
    p_refs, refs = refs[6 : 6 + 2 * half], refs[6 + 2 * half :]
    out_ref, other_ref, pad_ref, int_s, sem = refs[:5]
    copy = pltpu.make_async_copy(int_ref, int_s, sem)
    copy.start()
    other_ref[0 : half * SLAB, :] = got_ref[0 : half * SLAB, :]
    other_ref[half * SLAB :, :] = jnp.zeros((SLAB, 128), f32)
    slabs = 1 if last else half
    scale = 2.0 / filter_half_width

    def bases():
        copy.wait()
        return (
            [int_s[half, local] for local in range(half)],
            [int_s[half, half + local] for local in range(half)],
        )

    stencil(y_ref, other_ref, v_ref, prev_ref, out_ref, pad_ref, slabs, scale, bases)
    below = slice(half * SLAB, half * SLAB + half)
    rows = jnp.concatenate([y_ref[below, :], got_ref[below, :]], 0)
    coefficients = by_owner(rows, n, chunk)
    start_of = starts_from(int_s, nproj)
    couple(dims, slabs, half, coefficients, w_ref, p_refs, start_of, out_ref, scale)
    if not last:
        next_partials(dims, half, out_ref, p_refs, start_of, refs[5])


def chip_table(n):
    half = n // 2
    table = np.zeros((n, 4 * half + n), np.int32)
    for device in range(n):
        chip, core = device // 2, device % 2
        for local in range(half):
            there = chip ^ local
            same = local * SLAB
            far = there + (1 if core else -1)
            cross = (far ^ chip) * SLAB if 0 <= far < half else half * SLAB
            table[device, 2 * half + local] = same if core else cross
            table[device, 3 * half + local] = cross if core else same
        for owner in range(n):
            table[device, 4 * half + owner] = owner % 2 * half if core == 0 else (1 - owner % 2) * half
            table[device, 4 * half + owner] += owner // 2 ^ chip
    return table


def chip_form(psi, potential, projectors, offsets, intersection, dmat):
    n = lax.axis_size("domain")
    nband = lax.axis_size("band")
    cap, nproj = projectors.shape[2], projectors.shape[3]
    foot = projectors.shape[4] // 128
    chunk = cap * nproj
    lanes = n * chunk
    half = n // 2
    dims = (n, cap, nproj, foot, chunk)
    p = projectors.reshape(lanes, foot * 128)
    v_piece = potential.reshape(-1, 128)
    couplings = dmat.transpose(1, 2, 0).reshape(nproj * nproj, dmat.shape[0])
    domain = lax.axis_index("domain")
    info = jnp.concatenate(
        [
            lax.dynamic_slice_in_dim(jnp.asarray(chip_table(n)), domain, 1, 0)[0],
            lax.axis_index("band").astype(jnp.int32)[None],
        ]
    )
    params = pltpu.CompilerParams(vmem_limit_bytes=40 * 1024 * 1024)
    HBM = pl.BlockSpec(memory_space=pltpu.HBM)
    small = pl.CostEstimate(flops=1, bytes_accessed=1, transcendentals=0)
    large = pl.CostEstimate(flops=10**10, bytes_accessed=1, transcendentals=0)
    larger = pl.CostEstimate(flops=10**10, bytes_accessed=1, transcendentals=0)

    def shape(rows, dtype=f32):
        return jax.ShapeDtypeStruct((rows, 128), dtype)

    def swap(x, step):
        return lax.ppermute(x, "domain", [(i, i ^ step) for i in range(n)])

    sources = (psi.reshape(SLAB, 128), p, offsets[0].T, intersection[0].T, couplings, v_piece)
    sources = [pltpu.with_memory_space_constraint(x, pltpu.HBM) for x in sources]
    half_p = jax.ShapeDtypeStruct((lanes // 2, foot * 128), f32)
    pack, top, bottom = pl.pallas_call(
        functools.partial(pack_kernel, dims),
        out_shape=(shape(SLAB + v_piece.shape[0] + SMALL), half_p, half_p),
        in_specs=[HBM] * 6,
        out_specs=(VMEM,) * 3,
        scratch_shapes=[
            pltpu.SMEM((cap, n), jnp.int32),
            pltpu.SMEM((cap, n), jnp.int32),
            pltpu.VMEM(couplings.shape, f32),
            pltpu.VMEM((lanes, 128), f32),
            pltpu.SemaphoreType.DMA((7,)),
        ],
        compiler_params=params,
        cost_estimate=small,
        name="pack",
    )(*sources)
    packs = [pack] + [swap(pack, 2 * local) for local in range(1, half)]
    own, v_piece = pl.pallas_call(
        sort_kernel,
        out_shape=(shape(half * (SLAB + SMALL)), shape(half * v_piece.shape[0])),
        in_specs=[VMEM] * half,
        out_specs=(VMEM, VMEM),
        compiler_params=params,
        cost_estimate=small,
        name="sort",
    )(*packs)
    got = swap(own, 1)
    pieces = [v_piece]
    for back in range(1, nband):
        ring = [(i, (i + back) % nband) for i in range(nband)]
        pieces.append(lax.ppermute(v_piece, "band", ring))
    x_top, y_bottom = swap(top, 2), swap(bottom, 4)
    x_bottom, y_top = swap(bottom, 2), swap(top, 4)

    def relay(x, name):
        return pl.pallas_call(
            relay_kernel,
            out_shape=half_p,
            in_specs=[VMEM],
            out_specs=VMEM,
            compiler_params=params,
            cost_estimate=large,
            name=name,
        )(x)

    far_top, far_bottom = swap(relay(x_top, "relay_x"), 4), swap(relay(y_bottom, "relay_y"), 2)
    all_p = [top, bottom, x_top, x_bottom, y_top, y_bottom, far_top, far_bottom]
    other = pltpu.VMEM(((half + 1) * SLAB, 128), f32)
    padded = pltpu.VMEM((half * 6 * (NY + 16), 128), f32)
    row_scratch = pltpu.VMEM((half * lanes, 128), f32)
    ints = [pltpu.SMEM((8, 128), jnp.int32), pltpu.SemaphoreType.DMA(())]
    part, previous, w, c, table = pl.pallas_call(
        functools.partial(begin_kernel, dims),
        out_shape=(
            shape(half * SLAB),
            shape(half * SLAB),
            shape(half * lanes),
            shape(n),
            shape(8, jnp.int32),
        ),
        in_specs=[SMEM] + [VMEM] * 2,
        out_specs=(VMEM,) * 5,
        scratch_shapes=[other, padded, pltpu.VMEM((n, 2 * nproj, 128), f32)],
        compiler_params=params,
        cost_estimate=small,
        name="begin",
    )(info, own, got)
    sent = shape(half * SLAB + 8)
    part, v = pl.pallas_call(
        functools.partial(potential_kernel, nband),
        out_shape=(shape(half * SLAB), shape(half * SLAB)),
        in_specs=[VMEM] * (3 + nband),
        out_specs=(VMEM, VMEM),
        scratch_shapes=ints,
        compiler_params=params,
        cost_estimate=larger,
        name="potential",
    )(table, part, previous, *pieces)
    y = pl.pallas_call(
        functools.partial(first_kernel, dims),
        out_shape=sent,
        in_specs=[VMEM] * (4 + 2 * half),
        out_specs=VMEM,
        scratch_shapes=[row_scratch] + ints,
        compiler_params=params,
        name="first",
    )(table, part, w, c, *all_p)
    for degree in range(1, DEGREE):
        last = degree == DEGREE - 1
        following = pl.pallas_call(
            functools.partial(chip_kernel, dims, last),
            out_shape=shape(SLAB) if last else sent,
            in_specs=[VMEM] * (6 + 2 * half),
            out_specs=VMEM,
            scratch_shapes=[other, padded] + ints + ([] if last else [row_scratch]),
            compiler_params=params,
            name="last" if last else "next",
        )(table, y, swap(y, 1), previous, v, w, *all_p)
        previous, y = y, following
    return y.reshape(psi.shape)


def shards(psi, potential, projectors, offsets, intersection, dmat):
    n = lax.axis_size("domain")
    nband = lax.axis_size("band")
    fits = n == 8 and potential.shape[1] % 8 == 0 and nband <= 8
    form = chip_form if fits else slab_form
    return form(psi, potential, projectors, offsets, intersection, dmat)


def solution(mesh):
    return jax.shard_map(
        shards,
        mesh=mesh,
        in_specs=(
            P("band", "domain", None, None),
            P("domain", "band", None),
            P("domain", None, None, None, None),
            P("domain", None, None),
            P("domain", None, None),
            P("domain", None, None),
        ),
        out_specs=P("band", "domain", None, None),
        check_vma=False,
    )
```

```python
import functools

import jax
import jax.numpy as jnp
import numpy as np
from jax import lax
from jax.experimental import pallas as pl
from jax.experimental.pallas import tpu as pltpu
from jax.sharding import PartitionSpec as P

DEGREE = 4

stencil_weights = (
    -5369.0 / 1800.0,
    12.0 / 7.0,
    -15.0 / 56.0,
    10.0 / 189.0,
    -1.0 / 112.0,
    2.0 / 1925.0,
    -1.0 / 16632.0,
)
reach = len(stencil_weights) - 1
filter_center = 6.0
filter_half_width = 4.0
highest = lax.Precision.HIGHEST
f32 = jnp.float32
VMEM = pl.BlockSpec(memory_space=pltpu.VMEM)
SMEM = pl.BlockSpec(memory_space=pltpu.SMEM)


def iota(shape, dim):
    return lax.broadcasted_iota(jnp.int32, shape, dim)


def partials(y_ref, p_ref, off_ref, r_ref, dims):
    n, cap, nproj, foot, chunk = dims
    for slot in range(n * cap):
        start = off_ref[slot % cap, slot // cap]
        rows = pl.ds(slot * nproj, nproj)
        total = None
        for tile in range(foot):
            cells = jnp.broadcast_to(y_ref[pl.ds(start + tile, 1), :], (nproj, 128))
            term = p_ref[rows, tile * 128 : (tile + 1) * 128] * cells
            total = term if total is None else total + term
        r_ref[rows, :] = total
    return lax.dot_general(
        jnp.ones((8, 128), f32),
        r_ref[...],
        (((1,), (1,)), ((), ())),
        precision=highest,
        preferred_element_type=f32,
    )


def by_owner(rows, n, chunk):
    lanes = n * chunk
    shape = (n, lanes)
    ahead = (iota(shape, 1) // chunk - iota(shape, 0) + n) % n
    out = rows
    for step in range(1, n):
        moved = pltpu.roll(rows, n - step, 0)
        moved = pltpu.roll(moved, step * chunk, 1)
        out = jnp.where(ahead == step, moved, out)
    return out


def start_kernel(dims, y_ref, p_ref, off_ref, atom_ref, dmat_ref, out_ref, r_ref):
    n, cap, nproj, foot, chunk = dims
    lanes = n * chunk
    out_ref[:, 0, :] = jnp.broadcast_to(
        partials(y_ref, p_ref, off_ref, r_ref, dims)[0:1], (n, lanes)
    )
    lane = iota((1, lanes), 1) // nproj
    atoms = jnp.zeros((1, lanes), f32)
    for slot in range(n * cap):
        value = atom_ref[slot % cap, slot // cap].astype(f32)
        atoms = jnp.where(lane == slot, value, atoms)
    out_ref[:, 1, :] = jnp.broadcast_to(atoms, (n, lanes))
    count = dmat_ref.shape[1]
    for group in range(128 // count):
        block = dmat_ref[group * 2 * nproj : (group + 1) * 2 * nproj, :]
        for peer in range(n):
            out_ref[peer, 8:, group * count : (group + 1) * count] = block


def step_kernel(dims, nband, first, last, *refs):
    n, cap, nproj, foot, chunk = dims
    refs = list(refs)
    take = lambda: refs.pop(0)
    info_ref, off_ref = take(), take()
    y_ref, a_ref, b_ref, got_ref, p_ref = take(), take(), take(), take(), take()
    if first:
        atom_ref = take()
        v_pieces = [take() for _ in range(nband)]
        prev_ref = None
    else:
        prev_ref, v_ref, w_ref = take(), take(), take()
    out_ref = take()
    if not last:
        c_ref = take()
    if first:
        v_ref, w_ref = take(), take()
    pad_ref, lo_ref, hi_ref, r_ref = take(), take(), take(), take()
    cells = y_ref.shape[0]
    ny = 32
    planes = cells // ny
    lanes = n * chunk
    weights = stencil_weights

    if first:
        if nband > 1:
            piece_rows = ny // nband
            for back, piece in enumerate(v_pieces):
                at = lax.rem(info_ref[1] - back + nband, nband) * piece_rows
                for plane in range(planes):
                    spot = pl.multiple_of(plane * ny + at, 8)
                    v_ref[pl.ds(spot, piece_rows), :] = piece[
                        plane * piece_rows : (plane + 1) * piece_rows, :
                    ]
        else:
            v_ref[...] = v_pieces[0][...]
        atoms = by_owner(got_ref[:, 1, :], n, chunk)
        row = iota((chunk, 128), 0)
        column = iota((chunk, 128), 1)
        count = 128 // (nproj // 2)
        parity = (iota((chunk, 2 * nproj), 1) // nproj) == (iota((chunk, 2 * nproj), 0) % 2)
        spread = (iota((2 * nproj, lanes), 1) % nproj == iota((2 * nproj, lanes), 0) % nproj)
        spread = spread.astype(f32)
        for owner in range(n):
            mine = jnp.zeros((chunk, 128), jnp.int32)
            for k in range(cap):
                mine = jnp.where(row // nproj == k, atom_ref[k, owner], mine)
            pick = (column == (row % nproj) // 2 * count + mine) & (mine >= 0)
            entries = lax.dot_general(
                pick.astype(f32),
                got_ref[owner, 8:, 0:128],
                (((1,), (1,)), ((), ())),
                precision=highest,
                preferred_element_type=f32,
            )
            entries = jnp.where(parity, entries, 0.0)
            block = jnp.dot(entries, spread, precision=highest, preferred_element_type=f32)
            mine_row = jnp.zeros((chunk, lanes), f32)
            row_wide = iota((chunk, lanes), 0) // nproj
            for k in range(cap):
                mine_row = jnp.where(row_wide == k, atom_ref[k, owner].astype(f32), mine_row)
            same = (atoms[owner : owner + 1, :] == mine_row) & (mine_row >= 0.0)
            w_ref[pl.ds(owner * chunk, chunk), :] = jnp.where(same, block, 0.0)
        coefficients = by_owner(got_ref[:, 0, :], n, chunk)
    else:
        coefficients = by_owner(got_ref[...], n, chunk)

    odd = jnp.full((cells, 128), info_ref[0], jnp.int32) == 1
    from_a, from_b = a_ref[...], b_ref[...]
    lo_ref[...] = jnp.where(odd, from_a, from_b)
    hi_ref[...] = jnp.where(odd, from_b, from_a)
    tall = ny + 16
    for plane in range(planes):
        own = y_ref[plane * ny : (plane + 1) * ny, :]
        base = plane * tall
        pad_ref[base + 8 : base + 8 + ny, :] = own
        pad_ref[base : base + 8, :] = own[ny - 8 :, :]
        pad_ref[base + 8 + ny : base + tall, :] = own[0:8, :]

    apart = iota((128, 128), 0) - iota((128, 128), 1)
    apart = jnp.abs(apart)
    apart = jnp.minimum(apart, 128 - apart)
    circulant = jnp.full((128, 128), 3.0 * weights[0], f32)
    circulant = jnp.where(apart > reach, 0.0, circulant)
    for distance in range(1, reach + 1):
        circulant = jnp.where(apart == distance, weights[distance], circulant)
    along_z = jnp.dot(y_ref[...], circulant, precision=highest, preferred_element_type=f32)

    scale = (1.0 if first else 2.0) / filter_half_width

    def plane_of(index):
        if index < 0:
            ref, index = lo_ref, index + planes
        elif index >= planes:
            ref, index = hi_ref, index - planes
        else:
            ref = y_ref
        return ref[index * ny : (index + 1) * ny, :]

    for plane in range(planes):
        rows = slice(plane * ny, (plane + 1) * ny)
        base = plane * tall + 8
        own = y_ref[rows, :]
        lap = along_z[rows, :]
        for distance in range(1, reach + 1):
            beside = plane_of(plane + distance) + plane_of(plane - distance)
            beside = beside + pad_ref[base + distance : base + distance + ny, :]
            beside = beside + pad_ref[base - distance : base - distance + ny, :]
            lap = lap + weights[distance] * beside
        value = scale * ((v_ref[rows, :] - filter_center) * own - 0.5 * lap)
        if prev_ref is not None:
            value = value - prev_ref[rows, :]
        out_ref[rows, :] = value

    sublane = iota((foot, 128), 0)
    for slot in range(n * cap):
        owner = slot // cap
        rows = slice(slot * nproj, (slot + 1) * nproj)
        returned = jnp.sum(
            w_ref[rows, :] * coefficients[owner : owner + 1, :], axis=1, keepdims=True
        )
        returned = jnp.broadcast_to(returned * scale, (nproj, 128))
        contrib = jnp.zeros((foot, 128), f32)
        for tile in range(foot):
            term = jnp.sum(
                p_ref[rows, tile * 128 : (tile + 1) * 128] * returned, axis=0, keepdims=True
            )
            contrib = jnp.where(sublane == tile, term, contrib)
        start = off_ref[slot % cap, slot // cap]
        out_ref[pl.ds(start, foot), :] = out_ref[pl.ds(start, foot), :] + contrib

    if not last:
        c_ref[...] = jnp.broadcast_to(
            partials(out_ref, p_ref, off_ref, r_ref, dims)[0:1], (n, lanes)
        )


def beside_slabs(y, n):
    pairs = [(i, i ^ 1) for i in range(n) if i ^ 1 < n]
    cross = [(i, i + 1) for i in range(1, n - 1, 2)] + [(i + 1, i) for i in range(1, n - 1, 2)]
    return lax.ppermute(y, "domain", pairs), lax.ppermute(y, "domain", cross)


def slab_form(psi, potential, projectors, offsets, intersection, dmat):
    n = lax.axis_size("domain")
    nband = lax.axis_size("band")
    cap, nproj = projectors.shape[2], projectors.shape[3]
    foot = projectors.shape[4] // 128
    chunk = cap * nproj
    lanes = n * chunk
    dims = (n, cap, nproj, foot, chunk)
    cells = psi.shape[1] * psi.shape[2]
    y = psi.reshape(cells, 128)
    p = projectors.reshape(lanes, foot * 128)
    off = offsets[0].T
    atom = intersection[0].T
    couplings = dmat.transpose(1, 2, 0).reshape(nproj * nproj, dmat.shape[0])
    info = jnp.stack([lax.axis_index("domain") % 2, lax.axis_index("band")]).astype(jnp.int32)
    params = pltpu.CompilerParams(vmem_limit_bytes=40 * 1024 * 1024)

    start = pl.pallas_call(
        functools.partial(start_kernel, dims),
        out_shape=jax.ShapeDtypeStruct((n, 24, lanes), f32),
        in_specs=[VMEM, VMEM, SMEM, SMEM, VMEM],
        out_specs=VMEM,
        scratch_shapes=[pltpu.VMEM((lanes, 128), f32)],
        compiler_params=params,
        name="first_partials",
    )
    got = lax.all_to_all(
        start(y, p, off, atom, couplings), "domain", split_axis=0, concat_axis=0, tiled=True
    )
    if potential.shape[1] % 8 == 0 and nband <= 8:
        pieces = [potential.reshape(-1, 128)]
        for back in range(1, nband):
            ring = [(i, (i + back) % nband) for i in range(nband)]
            pieces.append(lax.ppermute(pieces[0], "band", ring))
    else:
        pieces = [lax.all_gather(potential, "band", axis=1, tiled=True).reshape(cells, 128)]

    y_shape = jax.ShapeDtypeStruct((cells, 128), f32)
    c_shape = jax.ShapeDtypeStruct((n, lanes), f32)
    scratch = [
        pltpu.VMEM((cells // 32 * 48, 128), f32),
        pltpu.VMEM((cells, 128), f32),
        pltpu.VMEM((cells, 128), f32),
        pltpu.VMEM((lanes, 128), f32),
    ]
    from_a, from_b = beside_slabs(y, n)
    previous = y
    y, c, v, w = pl.pallas_call(
        functools.partial(step_kernel, dims, len(pieces), True, False),
        out_shape=(y_shape, c_shape, y_shape, jax.ShapeDtypeStruct((lanes, lanes), f32)),
        in_specs=[SMEM, SMEM] + [VMEM] * 5 + [SMEM] + [VMEM] * len(pieces),
        out_specs=(VMEM,) * 4,
        scratch_shapes=scratch,
        compiler_params=params,
        name="first_step",
    )(info, off, y, from_a, from_b, got, p, atom, *pieces)
    for degree in range(1, DEGREE):
        last = degree == DEGREE - 1
        got = lax.all_to_all(c, "domain", split_axis=0, concat_axis=0, tiled=True)
        from_a, from_b = beside_slabs(y, n)
        out = pl.pallas_call(
            functools.partial(step_kernel, dims, len(pieces), False, last),
            out_shape=(y_shape,) if last else (y_shape, c_shape),
            in_specs=[SMEM, SMEM] + [VMEM] * 8,
            out_specs=(VMEM,) if last else (VMEM, VMEM),
            scratch_shapes=scratch,
            compiler_params=params,
            name="last_step" if last else "next_step",
        )(info, off, y, from_a, from_b, got, p, previous, v, w)
        previous, y = y, out[0]
        if not last:
            c = out[1]
    return y.reshape(psi.shape)


NY = 32
SLAB = 6 * NY
SMALL = 24


def circulant_z():
    apart = jnp.abs(iota((128, 128), 0) - iota((128, 128), 1))
    apart = jnp.minimum(apart, 128 - apart)
    out = jnp.full((128, 128), 3.0 * stencil_weights[0], f32)
    out = jnp.where(apart > reach, 0.0, out)
    for distance in range(1, reach + 1):
        out = jnp.where(apart == distance, stencil_weights[distance], out)
    return out


def stencil(y_ref, other_ref, v_ref, prev_ref, out_ref, pad_ref, slabs, scale, bases):
    tall = NY + 16
    for plane in range(6 * slabs):
        own = y_ref[plane * NY : (plane + 1) * NY, :]
        base = plane * tall
        pad_ref[base + 8 : base + 8 + NY, :] = own
        pad_ref[base : base + 8, :] = own[NY - 8 :, :]
        pad_ref[base + 8 + NY : base + tall, :] = own[0:8, :]
    along_z = jnp.dot(
        y_ref[0 : slabs * SLAB, :],
        circulant_z(),
        precision=highest,
        preferred_element_type=f32,
    )
    below, above = bases()
    for slab in range(slabs):
        for plane in range(6):
            at = (slab * 6 + plane) * NY
            rows = slice(at, at + NY)
            base = (slab * 6 + plane) * tall + 8
            own = y_ref[rows, :]
            lap = along_z[rows, :]
            for distance in range(1, reach + 1):
                beside = pad_ref[base + distance : base + distance + NY, :]
                beside = beside + pad_ref[base - distance : base - distance + NY, :]
                for index in (plane - distance, plane + distance):
                    if index < 0:
                        spot = pl.multiple_of(below[slab] + (index + 6) * NY, 8)
                        beside = beside + other_ref[pl.ds(spot, NY), :]
                    elif index >= 6:
                        spot = pl.multiple_of(above[slab] + (index - 6) * NY, 8)
                        beside = beside + other_ref[pl.ds(spot, NY), :]
                    else:
                        spot = (slab * 6 + index) * NY
                        beside = beside + y_ref[spot : spot + NY, :]
                lap = lap + stencil_weights[distance] * beside
            if v_ref is None:
                value = scale * (-filter_center * own - 0.5 * lap)
            else:
                value = scale * ((v_ref[rows, :] - filter_center) * own - 0.5 * lap)
            if prev_ref is not None:
                value = value - prev_ref[rows, :]
            out_ref[rows, :] = value


def pack_kernel(dims, *refs):
    n, cap, nproj, foot, chunk = dims
    lanes = n * chunk
    sources, (pack_ref, p_ref), scratch = refs[:6], refs[6:8], refs[8:]
    off_ref, atom_ref, dmat_ref, r_ref, sems = scratch
    small = pack_ref.shape[0] - SMALL
    targets = (
        pack_ref.at[0:SLAB, :],
        p_ref,
        off_ref,
        atom_ref,
        dmat_ref,
        pack_ref.at[SLAB:small, :],
    )
    copies = [
        pltpu.make_async_copy(source, target, sems.at[index])
        for index, (source, target) in enumerate(zip(sources, targets))
    ]
    for copy in copies:
        copy.start()
    for copy in copies[2:]:
        copy.wait()
    lane = iota((1, lanes), 1) // nproj
    atoms = jnp.zeros((1, lanes), f32)
    starts = jnp.zeros((1, lanes), f32)
    for slot in range(n * cap):
        here = lane == slot
        atoms = jnp.where(here, atom_ref[slot % cap, slot // cap].astype(f32), atoms)
        starts = jnp.where(here, off_ref[slot % cap, slot // cap].astype(f32), starts)
    pack_ref[small + 1 : small + 2, :] = atoms
    pack_ref[small + 2 : small + 3, :] = starts
    pack_ref[small + 3 : small + 8, :] = jnp.zeros((5, 128), f32)
    count = dmat_ref.shape[1]
    for group in range(128 // count):
        block = dmat_ref[group * 2 * nproj : (group + 1) * 2 * nproj, :]
        pack_ref[small + 8 :, group * count : (group + 1) * count] = block
    copies[0].wait()
    copies[1].wait()
    pack_ref[small : small + 1, :] = partials(pack_ref, p_ref, off_ref, r_ref, dims)[0:1]


def sort_kernel(*refs):
    packs, (pair_ref, v_ref) = refs[:-4], refs[-3:-1]
    small = packs[0].shape[0] - SMALL
    size = SLAB + SMALL
    for local, pack in enumerate(packs):
        pair_ref[local * size : local * size + SLAB, :] = pack[0:SLAB, :]
        pair_ref[local * size + SLAB : (local + 1) * size, :] = pack[small:, :]
        v_ref[local * (small - SLAB) : (local + 1) * (small - SLAB), :] = pack[SLAB:small, :]


def relay_kernel(x_ref, y_ref, top_ref, bottom_ref):
    rows = top_ref.shape[0]
    top_ref[...] = x_ref[0:rows, :]
    bottom_ref[...] = y_ref[rows:, :]


def begin_kernel(dims, info_ref, own_ref, got_ref, *refs):
    n, cap, nproj, foot, chunk = dims
    half = n // 2
    part_ref, y_ref, w_ref, c_ref, int_ref, other_ref, pad_ref, dmat_ref = refs
    lanes = n * chunk
    size = SLAB + SMALL
    c_rows, atom_rows, start_rows = [], [], []
    for group, source in enumerate((own_ref, got_ref)):
        for local in range(half):
            slab = local * size
            rows = slice(local * SLAB, (local + 1) * SLAB)
            target = other_ref if group else y_ref
            target[rows, :] = source[slab : slab + SLAB, :]
            small = slab + SLAB
            c_rows.append(source[small : small + 1, :])
            atom_rows.append(source[small + 1 : small + 2, :])
            if group == 0:
                start_rows.append(source[small + 2 : small + 3, :])
            dmat_ref[group * half + local] = source[small + 8 : small + SMALL, :]
    other_ref[half * SLAB :, :] = jnp.zeros((SLAB, 128), f32)
    c_ref[...] = by_owner(jnp.concatenate(c_rows, 0), n, chunk)
    atoms = by_owner(jnp.concatenate(atom_rows, 0), n, chunk)
    lane = iota((1, 128), 1)
    table = jnp.zeros((1, 128), jnp.int32)
    for local in range(half):
        int_ref[local : local + 1, :] = start_rows[local].astype(jnp.int32)
        for side in range(2):
            value = info_ref[(2 + side) * half + local]
            table = jnp.where(lane == side * half + local, value, table)
    table = jnp.where(lane == 2 * half, info_ref[4 * half + n], table)
    int_ref[half : half + 1, :] = table
    int_ref[half + 1 :, :] = jnp.zeros((8 - half - 1, 128), jnp.int32)

    def bases():
        return (
            [info_ref[2 * half + local] for local in range(half)],
            [info_ref[3 * half + local] for local in range(half)],
        )

    stencil(
        y_ref, other_ref, None, None, part_ref, pad_ref, half, 1.0 / filter_half_width, bases
    )
    square = (lanes, 128)
    diagonal = iota(square, 0) == iota(square, 1)
    ones = jnp.ones((128, 128), f32)
    column = iota(square, 1).astype(f32)
    count = 128 // (nproj // 2)
    shift = (iota(square, 0) % nproj // 2 * count).astype(f32)
    wide, picks = [], []
    for local in range(half):
        held = jnp.where(diagonal, atom_rows[local], 0.0)
        mine = jnp.dot(held, ones, precision=highest, preferred_element_type=f32)
        mine = jnp.round(mine)
        wide.append(mine)
        picks.append(jnp.where((column == shift + mine) & (mine >= 0.0), 1.0, 0.0))
    tall = half * chunk
    parity = iota((tall, 2 * nproj), 1) // nproj == iota((tall, 2 * nproj), 0) % 2
    spread = iota((2 * nproj, 128), 1) % nproj == iota((2 * nproj, 128), 0) % nproj
    spread = jnp.where(spread, 1.0, 0.0)
    for owner in range(n):
        rows = slice(owner * chunk, (owner + 1) * chunk)
        pick = jnp.concatenate([p[rows, :] for p in picks], 0)
        mine = jnp.concatenate([m[rows, :] for m in wide], 0)
        entries = lax.dot_general(
            pick,
            dmat_ref[info_ref[4 * half + owner]],
            (((1,), (1,)), ((), ())),
            precision=highest,
            preferred_element_type=f32,
        )
        entries = jnp.where(parity, entries, 0.0)
        block = jnp.dot(entries, spread, precision=highest, preferred_element_type=f32)
        same = (atoms[owner : owner + 1, :] == mine) & (mine >= 0.0)
        w_ref[owner * tall : (owner + 1) * tall, :] = jnp.where(same, block, 0.0)


def p_rows(p_refs, slab, slot, nproj, tile):
    ref, at = p_refs[slab], slot * nproj
    if at >= ref.shape[0]:
        ref, at = p_refs[slab + 1], at - ref.shape[0]
    return ref[at : at + nproj, tile * 128 : (tile + 1) * 128]


def swap_rows(x, step):
    if step == 4:
        return pltpu.roll(x, 4, 0)
    low = iota(x.shape, 0) // step % 2 == 0
    return jnp.where(low, pltpu.roll(x, 8 - step, 0), pltpu.roll(x, step, 0))


def column_sums(tiles):
    step = 4
    while step:
        low = iota(tiles[0].shape, 0) // step % 2 == 0
        pairs = [(tiles[t], tiles[t + step]) for t in range(step)]
        tiles = [
            jnp.where(low, a, b) + swap_rows(jnp.where(low, b, a), step) for a, b in pairs
        ]
        step //= 2
    return tiles[0]


def couple(dims, slabs, half, coefficients, w_ref, p_refs, start_of, out_ref, scale):
    n, cap, nproj, foot, chunk = dims
    for slab in slabs:
        for slot in range(n * cap):
            owner, k = slot // cap, slot % cap
            at = (owner * half + slab) * chunk + k * nproj
            back = jnp.sum(
                w_ref[at : at + nproj, :] * coefficients[owner : owner + 1, :],
                axis=1,
                keepdims=True,
            )
            back = jnp.broadcast_to(back * scale, (nproj, 128))
            tiles = [p_rows(p_refs, slab, slot, nproj, tile) * back for tile in range(foot)]
            spot = pl.ds(start_of(slab, slot), foot)
            out_ref[spot, :] = out_ref[spot, :] + column_sums(tiles)


def next_partials(dims, slabs, half, send_ref, p_refs, start_of, r_ref):
    n, cap, nproj, foot, chunk = dims
    lanes = n * chunk
    for index, slab in enumerate(slabs):
        for slot in range(n * cap):
            start = start_of(slab, slot)
            total = None
            for tile in range(foot):
                cells = jnp.broadcast_to(send_ref[pl.ds(start + tile, 1), :], (nproj, 128))
                term = p_rows(p_refs, slab, slot, nproj, tile) * cells
                total = term if total is None else total + term
            at = index * lanes + slot * nproj
            r_ref[at : at + nproj, :] = total
    row = lax.dot_general(
        jnp.ones((8, 128), f32),
        r_ref[...],
        (((1,), (1,)), ((), ())),
        precision=highest,
        preferred_element_type=f32,
    )
    for index, slab in enumerate(slabs):
        send_ref[half * SLAB + slab : half * SLAB + slab + 1, :] = row[
            0:1, index * lanes : (index + 1) * lanes
        ]


def starts_from(int_s, nproj):
    return lambda slab, slot: slab * SLAB + int_s[slab, slot * nproj]


def potential_kernel(nband, table_ref, part_ref, y_ref, *refs):
    pieces, (out_ref, v_ref, int_s, sem) = refs[:nband], refs[nband:]
    copy = pltpu.make_async_copy(table_ref, int_s, sem)
    copy.start()
    copy.wait()
    scale = 1.0 / filter_half_width
    piece = NY // nband
    for back in range(nband):
        at = lax.rem(int_s[4, 8] - back + nband, nband) * piece
        for plane in range(part_ref.shape[0] // NY):
            spot = pl.ds(pl.multiple_of(plane * NY + at, 8), piece)
            value = pieces[back][plane * piece : (plane + 1) * piece, :]
            v_ref[spot, :] = value
            out_ref[spot, :] = part_ref[spot, :] + scale * (value * y_ref[spot, :])


def first_kernel(dims, slabs, *refs):
    n, cap, nproj, foot, chunk = dims
    half = n // 2
    int_ref, part_ref, w_ref, c_ref = refs[:4]
    p_refs, (send_ref, r_ref, int_s, sem) = refs[4:-4], refs[-4:]
    p_refs = (None,) * slabs[0] + tuple(p_refs)
    copy = pltpu.make_async_copy(int_ref, int_s, sem)
    copy.start()
    if slabs[0] == 0:
        send_ref[0 : half * SLAB, :] = part_ref[...]
        send_ref[half * SLAB :, :] = jnp.zeros((8, 128), f32)
    copy.wait()
    start_of = starts_from(int_s, nproj)
    scale = 1.0 / filter_half_width
    couple(dims, slabs, half, c_ref[...], w_ref, p_refs, start_of, send_ref, scale)
    next_partials(dims, slabs, half, send_ref, p_refs, start_of, r_ref)


def chip_kernel(dims, last, *refs):
    n, cap, nproj, foot, chunk = dims
    half = n // 2
    int_ref, y_ref, got_ref, prev_ref, v_ref, w_ref = refs[:6]
    p_refs = refs[6 : 7 + half]
    out_ref, other_ref, pad_ref, int_s, sem = refs[7 + half : 12 + half]
    copy = pltpu.make_async_copy(int_ref, int_s, sem)
    copy.start()
    other_ref[0 : half * SLAB, :] = got_ref[0 : half * SLAB, :]
    other_ref[half * SLAB :, :] = jnp.zeros((SLAB, 128), f32)
    slabs = range(1 if last else half)
    scale = 2.0 / filter_half_width

    def bases():
        copy.wait()
        return (
            [int_s[half, local] for local in range(half)],
            [int_s[half, half + local] for local in range(half)],
        )

    stencil(y_ref, other_ref, v_ref, prev_ref, out_ref, pad_ref, len(slabs), scale, bases)
    below = slice(half * SLAB, half * SLAB + half)
    rows = jnp.concatenate([y_ref[below, :], got_ref[below, :]], 0)
    coefficients = by_owner(rows, n, chunk)
    start_of = starts_from(int_s, nproj)
    couple(dims, slabs, half, coefficients, w_ref, p_refs, start_of, out_ref, scale)
    if not last:
        out_ref[half * SLAB :, :] = jnp.zeros((8, 128), f32)
        next_partials(dims, slabs, half, out_ref, p_refs, start_of, refs[12 + half])


def chip_table(n):
    half = n // 2
    table = np.zeros((n, 4 * half + n), np.int32)
    for device in range(n):
        chip, core = device // 2, device % 2
        for local in range(half):
            there = chip ^ local
            same = local * SLAB
            far = there + (1 if core else -1)
            cross = (far ^ chip) * SLAB if 0 <= far < half else half * SLAB
            table[device, 2 * half + local] = same if core else cross
            table[device, 3 * half + local] = cross if core else same
        for owner in range(n):
            table[device, 4 * half + owner] = owner % 2 * half if core == 0 else (1 - owner % 2) * half
            table[device, 4 * half + owner] += owner // 2 ^ chip
    return table


def chip_form(psi, potential, projectors, offsets, intersection, dmat):
    n = lax.axis_size("domain")
    nband = lax.axis_size("band")
    cap, nproj = projectors.shape[2], projectors.shape[3]
    foot = projectors.shape[4] // 128
    chunk = cap * nproj
    lanes = n * chunk
    half = n // 2
    dims = (n, cap, nproj, foot, chunk)
    p = projectors.reshape(lanes, foot * 128)
    v_piece = potential.reshape(-1, 128)
    couplings = dmat.transpose(1, 2, 0).reshape(nproj * nproj, dmat.shape[0])
    domain = lax.axis_index("domain")
    info = jnp.concatenate(
        [
            lax.dynamic_slice_in_dim(jnp.asarray(chip_table(n)), domain, 1, 0)[0],
            lax.axis_index("band").astype(jnp.int32)[None],
        ]
    )
    params = pltpu.CompilerParams(vmem_limit_bytes=40 * 1024 * 1024)
    HBM = pl.BlockSpec(memory_space=pltpu.HBM)
    small = pl.CostEstimate(flops=1, bytes_accessed=1, transcendentals=0)
    large = pl.CostEstimate(flops=10**10, bytes_accessed=1, transcendentals=0)
    larger = pl.CostEstimate(flops=10**10, bytes_accessed=1, transcendentals=0)

    def shape(rows, dtype=f32):
        return jax.ShapeDtypeStruct((rows, 128), dtype)

    def swap(x, step):
        return lax.ppermute(x, "domain", [(i, i ^ step) for i in range(n)])

    sources = (psi.reshape(SLAB, 128), p, offsets[0].T, intersection[0].T, couplings, v_piece)
    sources = [pltpu.with_memory_space_constraint(x, pltpu.HBM) for x in sources]
    pack, p = pl.pallas_call(
        functools.partial(pack_kernel, dims),
        out_shape=(
            shape(SLAB + v_piece.shape[0] + SMALL),
            jax.ShapeDtypeStruct(p.shape, f32),
        ),
        in_specs=[HBM] * 6,
        out_specs=(VMEM, VMEM),
        scratch_shapes=[
            pltpu.SMEM((cap, n), jnp.int32),
            pltpu.SMEM((cap, n), jnp.int32),
            pltpu.VMEM(couplings.shape, f32),
            pltpu.VMEM((lanes, 128), f32),
            pltpu.SemaphoreType.DMA((6,)),
        ],
        compiler_params=params,
        cost_estimate=small,
        name="pack",
    )(*sources)
    packs = [pack] + [swap(pack, 2 * local) for local in range(1, half)]
    own, v_piece, p = pl.pallas_call(
        sort_kernel,
        out_shape=(
            shape(half * (SLAB + SMALL)),
            shape(half * v_piece.shape[0]),
            jax.ShapeDtypeStruct(p.shape, f32),
        ),
        in_specs=[VMEM] * (half + 1),
        out_specs=(VMEM,) * 3,
        input_output_aliases={half: 2},
        compiler_params=params,
        cost_estimate=small,
        name="sort",
    )(*packs, p)
    got = swap(own, 1)
    pieces = [v_piece]
    for back in range(1, nband):
        ring = [(i, (i + back) % nband) for i in range(nband)]
        pieces.append(lax.ppermute(v_piece, "band", ring))
    p_x, p_y = swap(p, 2), swap(p, 4)
    halves = (jax.ShapeDtypeStruct((lanes // 2, foot * 128), f32),) * 2
    top, bottom = pl.pallas_call(
        relay_kernel,
        out_shape=halves,
        in_specs=[VMEM] * 2,
        out_specs=(VMEM, VMEM),
        compiler_params=params,
        cost_estimate=large,
        name="relay",
    )(p_x, p_y)
    all_p = [p, p_x, p_y, swap(top, 4), swap(bottom, 2)]
    other = pltpu.VMEM(((half + 1) * SLAB, 128), f32)
    padded = pltpu.VMEM((half * 6 * (NY + 16), 128), f32)
    row_scratch = pltpu.VMEM((half * lanes, 128), f32)
    ints = [pltpu.SMEM((8, 128), jnp.int32), pltpu.SemaphoreType.DMA(())]
    part, previous, w, c, table = pl.pallas_call(
        functools.partial(begin_kernel, dims),
        out_shape=(
            shape(half * SLAB),
            shape(half * SLAB),
            shape(half * lanes),
            shape(n),
            shape(8, jnp.int32),
        ),
        in_specs=[SMEM] + [VMEM] * 2,
        out_specs=(VMEM,) * 5,
        scratch_shapes=[other, padded, pltpu.VMEM((n, 2 * nproj, 128), f32)],
        compiler_params=params,
        cost_estimate=small,
        name="begin",
    )(info, own, got)
    sent = shape(half * SLAB + 8)
    part, v = pl.pallas_call(
        functools.partial(potential_kernel, nband),
        out_shape=(shape(half * SLAB), shape(half * SLAB)),
        in_specs=[VMEM] * (3 + nband),
        out_specs=(VMEM, VMEM),
        scratch_shapes=ints,
        compiler_params=params,
        cost_estimate=larger,
        name="potential",
    )(table, part, previous, *pieces)
    y = part
    for slabs in (range(half - 1), range(half - 1, half)):
        start, late = slabs[0], slabs[0] > 0
        some_p = all_p[start:] if late else all_p[: half - 1]
        y = pl.pallas_call(
            functools.partial(first_kernel, dims, slabs),
            out_shape=sent,
            in_specs=[VMEM] * (4 + len(some_p)),
            out_specs=VMEM,
            scratch_shapes=[pltpu.VMEM((len(slabs) * lanes, 128), f32)] + ints,
            input_output_aliases={1: 0} if late else {},
            compiler_params=params,
            cost_estimate=small,
            name="first_late" if late else "first",
        )(table, y, w, c, *some_p)
    for degree in range(1, DEGREE):
        last = degree == DEGREE - 1
        following = pl.pallas_call(
            functools.partial(chip_kernel, dims, last),
            out_shape=shape(SLAB) if last else sent,
            in_specs=[VMEM] * (7 + half),
            out_specs=VMEM,
            scratch_shapes=[other, padded] + ints + ([] if last else [row_scratch]),
            compiler_params=params,
            name="last" if last else "next",
        )(table, y, swap(y, 1), previous, v, w, *all_p)
        previous, y = y, following
    return y.reshape(psi.shape)


def shards(psi, potential, projectors, offsets, intersection, dmat):
    n = lax.axis_size("domain")
    nband = lax.axis_size("band")
    fits = n == 8 and potential.shape[1] % 8 == 0 and nband <= 8
    form = chip_form if fits else slab_form
    return form(psi, potential, projectors, offsets, intersection, dmat)


def solution(mesh):
    return jax.shard_map(
        shards,
        mesh=mesh,
        in_specs=(
            P("band", "domain", None, None),
            P("domain", "band", None),
            P("domain", None, None, None, None),
            P("domain", None, None),
            P("domain", None, None),
            P("domain", None, None),
        ),
        out_specs=P("band", "domain", None, None),
        check_vma=False,
    )
```

```python
import functools

import jax
import jax.numpy as jnp
import numpy as np
from jax import lax
from jax.experimental import pallas as pl
from jax.experimental.pallas import tpu as pltpu
from jax.sharding import PartitionSpec as P

DEGREE = 4

stencil_weights = (
    -5369.0 / 1800.0,
    12.0 / 7.0,
    -15.0 / 56.0,
    10.0 / 189.0,
    -1.0 / 112.0,
    2.0 / 1925.0,
    -1.0 / 16632.0,
)
reach = len(stencil_weights) - 1
filter_center = 6.0
filter_half_width = 4.0
highest = lax.Precision.HIGHEST
f32 = jnp.float32
VMEM = pl.BlockSpec(memory_space=pltpu.VMEM)
SMEM = pl.BlockSpec(memory_space=pltpu.SMEM)


def iota(shape, dim):
    return lax.broadcasted_iota(jnp.int32, shape, dim)


def partials(y_ref, p_ref, off_ref, r_ref, dims):
    n, cap, nproj, foot, chunk = dims
    for slot in range(n * cap):
        start = off_ref[slot % cap, slot // cap]
        rows = pl.ds(slot * nproj, nproj)
        total = None
        for tile in range(foot):
            cells = jnp.broadcast_to(y_ref[pl.ds(start + tile, 1), :], (nproj, 128))
            term = p_ref[rows, tile * 128 : (tile + 1) * 128] * cells
            total = term if total is None else total + term
        r_ref[rows, :] = total
    return lax.dot_general(
        jnp.ones((8, 128), f32),
        r_ref[...],
        (((1,), (1,)), ((), ())),
        precision=highest,
        preferred_element_type=f32,
    )


def by_owner(rows, n, chunk):
    lanes = n * chunk
    shape = (n, lanes)
    ahead = (iota(shape, 1) // chunk - iota(shape, 0) + n) % n
    out = rows
    for step in range(1, n):
        moved = pltpu.roll(rows, n - step, 0)
        moved = pltpu.roll(moved, step * chunk, 1)
        out = jnp.where(ahead == step, moved, out)
    return out


def start_kernel(dims, y_ref, p_ref, off_ref, atom_ref, dmat_ref, out_ref, r_ref):
    n, cap, nproj, foot, chunk = dims
    lanes = n * chunk
    out_ref[:, 0, :] = jnp.broadcast_to(
        partials(y_ref, p_ref, off_ref, r_ref, dims)[0:1], (n, lanes)
    )
    lane = iota((1, lanes), 1) // nproj
    atoms = jnp.zeros((1, lanes), f32)
    for slot in range(n * cap):
        value = atom_ref[slot % cap, slot // cap].astype(f32)
        atoms = jnp.where(lane == slot, value, atoms)
    out_ref[:, 1, :] = jnp.broadcast_to(atoms, (n, lanes))
    count = dmat_ref.shape[1]
    for group in range(128 // count):
        block = dmat_ref[group * 2 * nproj : (group + 1) * 2 * nproj, :]
        for peer in range(n):
            out_ref[peer, 8:, group * count : (group + 1) * count] = block


def step_kernel(dims, nband, first, last, *refs):
    n, cap, nproj, foot, chunk = dims
    refs = list(refs)
    take = lambda: refs.pop(0)
    info_ref, off_ref = take(), take()
    y_ref, a_ref, b_ref, got_ref, p_ref = take(), take(), take(), take(), take()
    if first:
        atom_ref = take()
        v_pieces = [take() for _ in range(nband)]
        prev_ref = None
    else:
        prev_ref, v_ref, w_ref = take(), take(), take()
    out_ref = take()
    if not last:
        c_ref = take()
    if first:
        v_ref, w_ref = take(), take()
    pad_ref, lo_ref, hi_ref, r_ref = take(), take(), take(), take()
    cells = y_ref.shape[0]
    ny = 32
    planes = cells // ny
    lanes = n * chunk
    weights = stencil_weights

    if first:
        if nband > 1:
            piece_rows = ny // nband
            for back, piece in enumerate(v_pieces):
                at = lax.rem(info_ref[1] - back + nband, nband) * piece_rows
                for plane in range(planes):
                    spot = pl.multiple_of(plane * ny + at, 8)
                    v_ref[pl.ds(spot, piece_rows), :] = piece[
                        plane * piece_rows : (plane + 1) * piece_rows, :
                    ]
        else:
            v_ref[...] = v_pieces[0][...]
        atoms = by_owner(got_ref[:, 1, :], n, chunk)
        row = iota((chunk, 128), 0)
        column = iota((chunk, 128), 1)
        count = 128 // (nproj // 2)
        parity = (iota((chunk, 2 * nproj), 1) // nproj) == (iota((chunk, 2 * nproj), 0) % 2)
        spread = (iota((2 * nproj, lanes), 1) % nproj == iota((2 * nproj, lanes), 0) % nproj)
        spread = spread.astype(f32)
        for owner in range(n):
            mine = jnp.zeros((chunk, 128), jnp.int32)
            for k in range(cap):
                mine = jnp.where(row // nproj == k, atom_ref[k, owner], mine)
            pick = (column == (row % nproj) // 2 * count + mine) & (mine >= 0)
            entries = lax.dot_general(
                pick.astype(f32),
                got_ref[owner, 8:, 0:128],
                (((1,), (1,)), ((), ())),
                precision=highest,
                preferred_element_type=f32,
            )
            entries = jnp.where(parity, entries, 0.0)
            block = jnp.dot(entries, spread, precision=highest, preferred_element_type=f32)
            mine_row = jnp.zeros((chunk, lanes), f32)
            row_wide = iota((chunk, lanes), 0) // nproj
            for k in range(cap):
                mine_row = jnp.where(row_wide == k, atom_ref[k, owner].astype(f32), mine_row)
            same = (atoms[owner : owner + 1, :] == mine_row) & (mine_row >= 0.0)
            w_ref[pl.ds(owner * chunk, chunk), :] = jnp.where(same, block, 0.0)
        coefficients = by_owner(got_ref[:, 0, :], n, chunk)
    else:
        coefficients = by_owner(got_ref[...], n, chunk)

    odd = jnp.full((cells, 128), info_ref[0], jnp.int32) == 1
    from_a, from_b = a_ref[...], b_ref[...]
    lo_ref[...] = jnp.where(odd, from_a, from_b)
    hi_ref[...] = jnp.where(odd, from_b, from_a)
    tall = ny + 16
    for plane in range(planes):
        own = y_ref[plane * ny : (plane + 1) * ny, :]
        base = plane * tall
        pad_ref[base + 8 : base + 8 + ny, :] = own
        pad_ref[base : base + 8, :] = own[ny - 8 :, :]
        pad_ref[base + 8 + ny : base + tall, :] = own[0:8, :]

    apart = iota((128, 128), 0) - iota((128, 128), 1)
    apart = jnp.abs(apart)
    apart = jnp.minimum(apart, 128 - apart)
    circulant = jnp.full((128, 128), 3.0 * weights[0], f32)
    circulant = jnp.where(apart > reach, 0.0, circulant)
    for distance in range(1, reach + 1):
        circulant = jnp.where(apart == distance, weights[distance], circulant)
    along_z = jnp.dot(y_ref[...], circulant, precision=highest, preferred_element_type=f32)

    scale = (1.0 if first else 2.0) / filter_half_width

    def plane_of(index):
        if index < 0:
            ref, index = lo_ref, index + planes
        elif index >= planes:
            ref, index = hi_ref, index - planes
        else:
            ref = y_ref
        return ref[index * ny : (index + 1) * ny, :]

    for plane in range(planes):
        rows = slice(plane * ny, (plane + 1) * ny)
        base = plane * tall + 8
        own = y_ref[rows, :]
        lap = along_z[rows, :]
        for distance in range(1, reach + 1):
            beside = plane_of(plane + distance) + plane_of(plane - distance)
            beside = beside + pad_ref[base + distance : base + distance + ny, :]
            beside = beside + pad_ref[base - distance : base - distance + ny, :]
            lap = lap + weights[distance] * beside
        value = scale * ((v_ref[rows, :] - filter_center) * own - 0.5 * lap)
        if prev_ref is not None:
            value = value - prev_ref[rows, :]
        out_ref[rows, :] = value

    sublane = iota((foot, 128), 0)
    for slot in range(n * cap):
        owner = slot // cap
        rows = slice(slot * nproj, (slot + 1) * nproj)
        returned = jnp.sum(
            w_ref[rows, :] * coefficients[owner : owner + 1, :], axis=1, keepdims=True
        )
        returned = jnp.broadcast_to(returned * scale, (nproj, 128))
        contrib = jnp.zeros((foot, 128), f32)
        for tile in range(foot):
            term = jnp.sum(
                p_ref[rows, tile * 128 : (tile + 1) * 128] * returned, axis=0, keepdims=True
            )
            contrib = jnp.where(sublane == tile, term, contrib)
        start = off_ref[slot % cap, slot // cap]
        out_ref[pl.ds(start, foot), :] = out_ref[pl.ds(start, foot), :] + contrib

    if not last:
        c_ref[...] = jnp.broadcast_to(
            partials(out_ref, p_ref, off_ref, r_ref, dims)[0:1], (n, lanes)
        )


def beside_slabs(y, n):
    pairs = [(i, i ^ 1) for i in range(n) if i ^ 1 < n]
    cross = [(i, i + 1) for i in range(1, n - 1, 2)] + [(i + 1, i) for i in range(1, n - 1, 2)]
    return lax.ppermute(y, "domain", pairs), lax.ppermute(y, "domain", cross)


def slab_form(psi, potential, projectors, offsets, intersection, dmat):
    n = lax.axis_size("domain")
    nband = lax.axis_size("band")
    cap, nproj = projectors.shape[2], projectors.shape[3]
    foot = projectors.shape[4] // 128
    chunk = cap * nproj
    lanes = n * chunk
    dims = (n, cap, nproj, foot, chunk)
    cells = psi.shape[1] * psi.shape[2]
    y = psi.reshape(cells, 128)
    p = projectors.reshape(lanes, foot * 128)
    off = offsets[0].T
    atom = intersection[0].T
    couplings = dmat.transpose(1, 2, 0).reshape(nproj * nproj, dmat.shape[0])
    info = jnp.stack([lax.axis_index("domain") % 2, lax.axis_index("band")]).astype(jnp.int32)
    params = pltpu.CompilerParams(vmem_limit_bytes=40 * 1024 * 1024)

    start = pl.pallas_call(
        functools.partial(start_kernel, dims),
        out_shape=jax.ShapeDtypeStruct((n, 24, lanes), f32),
        in_specs=[VMEM, VMEM, SMEM, SMEM, VMEM],
        out_specs=VMEM,
        scratch_shapes=[pltpu.VMEM((lanes, 128), f32)],
        compiler_params=params,
        name="first_partials",
    )
    got = lax.all_to_all(
        start(y, p, off, atom, couplings), "domain", split_axis=0, concat_axis=0, tiled=True
    )
    if potential.shape[1] % 8 == 0 and nband <= 8:
        pieces = [potential.reshape(-1, 128)]
        for back in range(1, nband):
            ring = [(i, (i + back) % nband) for i in range(nband)]
            pieces.append(lax.ppermute(pieces[0], "band", ring))
    else:
        pieces = [lax.all_gather(potential, "band", axis=1, tiled=True).reshape(cells, 128)]

    y_shape = jax.ShapeDtypeStruct((cells, 128), f32)
    c_shape = jax.ShapeDtypeStruct((n, lanes), f32)
    scratch = [
        pltpu.VMEM((cells // 32 * 48, 128), f32),
        pltpu.VMEM((cells, 128), f32),
        pltpu.VMEM((cells, 128), f32),
        pltpu.VMEM((lanes, 128), f32),
    ]
    from_a, from_b = beside_slabs(y, n)
    previous = y
    y, c, v, w = pl.pallas_call(
        functools.partial(step_kernel, dims, len(pieces), True, False),
        out_shape=(y_shape, c_shape, y_shape, jax.ShapeDtypeStruct((lanes, lanes), f32)),
        in_specs=[SMEM, SMEM] + [VMEM] * 5 + [SMEM] + [VMEM] * len(pieces),
        out_specs=(VMEM,) * 4,
        scratch_shapes=scratch,
        compiler_params=params,
        name="first_step",
    )(info, off, y, from_a, from_b, got, p, atom, *pieces)
    for degree in range(1, DEGREE):
        last = degree == DEGREE - 1
        got = lax.all_to_all(c, "domain", split_axis=0, concat_axis=0, tiled=True)
        from_a, from_b = beside_slabs(y, n)
        out = pl.pallas_call(
            functools.partial(step_kernel, dims, len(pieces), False, last),
            out_shape=(y_shape,) if last else (y_shape, c_shape),
            in_specs=[SMEM, SMEM] + [VMEM] * 8,
            out_specs=(VMEM,) if last else (VMEM, VMEM),
            scratch_shapes=scratch,
            compiler_params=params,
            name="last_step" if last else "next_step",
        )(info, off, y, from_a, from_b, got, p, previous, v, w)
        previous, y = y, out[0]
        if not last:
            c = out[1]
    return y.reshape(psi.shape)


NY = 32
SLAB = 6 * NY
SMALL = 24


def circulant_z():
    apart = jnp.abs(iota((128, 128), 0) - iota((128, 128), 1))
    apart = jnp.minimum(apart, 128 - apart)
    out = jnp.full((128, 128), 3.0 * stencil_weights[0], f32)
    out = jnp.where(apart > reach, 0.0, out)
    for distance in range(1, reach + 1):
        out = jnp.where(apart == distance, stencil_weights[distance], out)
    return out


def stencil(y_ref, other_ref, v_ref, prev_ref, out_ref, pad_ref, slabs, scale, bases):
    tall = NY + 16
    for plane in range(6 * slabs):
        own = y_ref[plane * NY : (plane + 1) * NY, :]
        base = plane * tall
        pad_ref[base + 8 : base + 8 + NY, :] = own
        pad_ref[base : base + 8, :] = own[NY - 8 :, :]
        pad_ref[base + 8 + NY : base + tall, :] = own[0:8, :]
    along_z = jnp.dot(
        y_ref[0 : slabs * SLAB, :],
        circulant_z(),
        precision=highest,
        preferred_element_type=f32,
    )
    below, above = bases()
    for slab in range(slabs):
        for plane in range(6):
            at = (slab * 6 + plane) * NY
            rows = slice(at, at + NY)
            base = (slab * 6 + plane) * tall + 8
            own = y_ref[rows, :]
            lap = along_z[rows, :]
            for distance in range(1, reach + 1):
                beside = pad_ref[base + distance : base + distance + NY, :]
                beside = beside + pad_ref[base - distance : base - distance + NY, :]
                for index in (plane - distance, plane + distance):
                    if index < 0:
                        spot = pl.multiple_of(below[slab] + (index + 6) * NY, 8)
                        beside = beside + other_ref[pl.ds(spot, NY), :]
                    elif index >= 6:
                        spot = pl.multiple_of(above[slab] + (index - 6) * NY, 8)
                        beside = beside + other_ref[pl.ds(spot, NY), :]
                    else:
                        spot = (slab * 6 + index) * NY
                        beside = beside + y_ref[spot : spot + NY, :]
                lap = lap + stencil_weights[distance] * beside
            if v_ref is None:
                value = scale * (-filter_center * own - 0.5 * lap)
            else:
                value = scale * ((v_ref[rows, :] - filter_center) * own - 0.5 * lap)
            if prev_ref is not None:
                value = value - prev_ref[rows, :]
            out_ref[rows, :] = value


def pack_kernel(dims, *refs):
    n, cap, nproj, foot, chunk = dims
    lanes = n * chunk
    sources, (pack_ref, p_ref), scratch = refs[:6], refs[6:8], refs[8:]
    off_ref, atom_ref, dmat_ref, r_ref, sems = scratch
    small = pack_ref.shape[0] - SMALL
    targets = (
        pack_ref.at[0:SLAB, :],
        p_ref,
        off_ref,
        atom_ref,
        dmat_ref,
        pack_ref.at[SLAB:small, :],
    )
    copies = [
        pltpu.make_async_copy(source, target, sems.at[index])
        for index, (source, target) in enumerate(zip(sources, targets))
    ]
    for copy in copies:
        copy.start()
    for copy in copies[2:]:
        copy.wait()
    lane = iota((1, lanes), 1) // nproj
    atoms = jnp.zeros((1, lanes), f32)
    starts = jnp.zeros((1, lanes), f32)
    for slot in range(n * cap):
        here = lane == slot
        atoms = jnp.where(here, atom_ref[slot % cap, slot // cap].astype(f32), atoms)
        starts = jnp.where(here, off_ref[slot % cap, slot // cap].astype(f32), starts)
    pack_ref[small + 1 : small + 2, :] = atoms
    pack_ref[small + 2 : small + 3, :] = starts
    pack_ref[small + 3 : small + 8, :] = jnp.zeros((5, 128), f32)
    count = dmat_ref.shape[1]
    for group in range(128 // count):
        block = dmat_ref[group * 2 * nproj : (group + 1) * 2 * nproj, :]
        pack_ref[small + 8 :, group * count : (group + 1) * count] = block
    copies[0].wait()
    copies[1].wait()
    pack_ref[small : small + 1, :] = partials(pack_ref, p_ref, off_ref, r_ref, dims)[0:1]


def gate_kernel(*refs):
    pass


def sort_kernel(*refs):
    packs, (pair_ref, v_ref) = refs[:-2], refs[-2:]
    small = packs[0].shape[0] - SMALL
    size = SLAB + SMALL
    for local, pack in enumerate(packs):
        pair_ref[local * size : local * size + SLAB, :] = pack[0:SLAB, :]
        pair_ref[local * size + SLAB : (local + 1) * size, :] = pack[small:, :]
        v_ref[local * (small - SLAB) : (local + 1) * (small - SLAB), :] = pack[SLAB:small, :]


def relay_kernel(x_ref, y_ref, top_ref, bottom_ref):
    rows = top_ref.shape[0]
    top_ref[...] = x_ref[0:rows, :]
    bottom_ref[...] = y_ref[rows:, :]


def begin_kernel(dims, info_ref, own_ref, got_ref, *refs):
    n, cap, nproj, foot, chunk = dims
    half = n // 2
    part_ref, y_ref, w_ref, c_ref, int_ref, other_ref, pad_ref, dmat_ref = refs
    lanes = n * chunk
    size = SLAB + SMALL
    c_rows, atom_rows, start_rows = [], [], []
    for group, source in enumerate((own_ref, got_ref)):
        for local in range(half):
            slab = local * size
            rows = slice(local * SLAB, (local + 1) * SLAB)
            target = other_ref if group else y_ref
            target[rows, :] = source[slab : slab + SLAB, :]
            small = slab + SLAB
            c_rows.append(source[small : small + 1, :])
            atom_rows.append(source[small + 1 : small + 2, :])
            if group == 0:
                start_rows.append(source[small + 2 : small + 3, :])
            dmat_ref[group * half + local] = source[small + 8 : small + SMALL, :]
    other_ref[half * SLAB :, :] = jnp.zeros((SLAB, 128), f32)
    c_ref[...] = by_owner(jnp.concatenate(c_rows, 0), n, chunk)
    atoms = by_owner(jnp.concatenate(atom_rows, 0), n, chunk)
    lane = iota((1, 128), 1)
    table = jnp.zeros((1, 128), jnp.int32)
    for local in range(half):
        int_ref[local : local + 1, :] = start_rows[local].astype(jnp.int32)
        for side in range(2):
            value = info_ref[(2 + side) * half + local]
            table = jnp.where(lane == side * half + local, value, table)
    table = jnp.where(lane == 2 * half, info_ref[4 * half + n], table)
    int_ref[half : half + 1, :] = table
    int_ref[half + 1 :, :] = jnp.zeros((8 - half - 1, 128), jnp.int32)

    def bases():
        return (
            [info_ref[2 * half + local] for local in range(half)],
            [info_ref[3 * half + local] for local in range(half)],
        )

    stencil(
        y_ref, other_ref, None, None, part_ref, pad_ref, half, 1.0 / filter_half_width, bases
    )
    square = (lanes, 128)
    diagonal = iota(square, 0) == iota(square, 1)
    ones = jnp.ones((128, 128), f32)
    column = iota(square, 1).astype(f32)
    count = 128 // (nproj // 2)
    shift = (iota(square, 0) % nproj // 2 * count).astype(f32)
    wide, picks = [], []
    for local in range(half):
        held = jnp.where(diagonal, atom_rows[local], 0.0)
        mine = jnp.dot(held, ones, precision=highest, preferred_element_type=f32)
        mine = jnp.round(mine)
        wide.append(mine)
        picks.append(jnp.where((column == shift + mine) & (mine >= 0.0), 1.0, 0.0))
    tall = half * chunk
    parity = iota((tall, 2 * nproj), 1) // nproj == iota((tall, 2 * nproj), 0) % 2
    spread = iota((2 * nproj, 128), 1) % nproj == iota((2 * nproj, 128), 0) % nproj
    spread = jnp.where(spread, 1.0, 0.0)
    for owner in range(n):
        rows = slice(owner * chunk, (owner + 1) * chunk)
        pick = jnp.concatenate([p[rows, :] for p in picks], 0)
        mine = jnp.concatenate([m[rows, :] for m in wide], 0)
        entries = lax.dot_general(
            pick,
            dmat_ref[info_ref[4 * half + owner]],
            (((1,), (1,)), ((), ())),
            precision=highest,
            preferred_element_type=f32,
        )
        entries = jnp.where(parity, entries, 0.0)
        block = jnp.dot(entries, spread, precision=highest, preferred_element_type=f32)
        same = (atoms[owner : owner + 1, :] == mine) & (mine >= 0.0)
        w_ref[owner * tall : (owner + 1) * tall, :] = jnp.where(same, block, 0.0)


def p_rows(p_refs, slab, slot, nproj, tile):
    ref, at = p_refs[slab], slot * nproj
    if at >= ref.shape[0]:
        ref, at = p_refs[slab + 1], at - ref.shape[0]
    return ref[at : at + nproj, tile * 128 : (tile + 1) * 128]


def swap_rows(x, step):
    if step == 4:
        return pltpu.roll(x, 4, 0)
    low = iota(x.shape, 0) // step % 2 == 0
    return jnp.where(low, pltpu.roll(x, 8 - step, 0), pltpu.roll(x, step, 0))


def column_sums(tiles):
    step = 4
    while step:
        low = iota(tiles[0].shape, 0) // step % 2 == 0
        pairs = [(tiles[t], tiles[t + step]) for t in range(step)]
        tiles = [
            jnp.where(low, a, b) + swap_rows(jnp.where(low, b, a), step) for a, b in pairs
        ]
        step //= 2
    return tiles[0]


def couple(dims, slabs, half, coefficients, w_ref, p_refs, start_of, out_ref, scale):
    n, cap, nproj, foot, chunk = dims
    for slab in slabs:
        for slot in range(n * cap):
            owner, k = slot // cap, slot % cap
            at = (owner * half + slab) * chunk + k * nproj
            back = jnp.sum(
                w_ref[at : at + nproj, :] * coefficients[owner : owner + 1, :],
                axis=1,
                keepdims=True,
            )
            back = jnp.broadcast_to(back * scale, (nproj, 128))
            tiles = [p_rows(p_refs, slab, slot, nproj, tile) * back for tile in range(foot)]
            spot = pl.ds(start_of(slab, slot), foot)
            out_ref[spot, :] = out_ref[spot, :] + column_sums(tiles)


def next_partials(dims, slabs, half, send_ref, p_refs, start_of, r_ref):
    n, cap, nproj, foot, chunk = dims
    lanes = n * chunk
    for index, slab in enumerate(slabs):
        for slot in range(n * cap):
            start = start_of(slab, slot)
            total = None
            for tile in range(foot):
                cells = jnp.broadcast_to(send_ref[pl.ds(start + tile, 1), :], (nproj, 128))
                term = p_rows(p_refs, slab, slot, nproj, tile) * cells
                total = term if total is None else total + term
            at = index * lanes + slot * nproj
            r_ref[at : at + nproj, :] = total
    row = lax.dot_general(
        jnp.ones((8, 128), f32),
        r_ref[...],
        (((1,), (1,)), ((), ())),
        precision=highest,
        preferred_element_type=f32,
    )
    for index, slab in enumerate(slabs):
        send_ref[half * SLAB + slab : half * SLAB + slab + 1, :] = row[
            0:1, index * lanes : (index + 1) * lanes
        ]


def starts_from(int_s, nproj):
    return lambda slab, slot: slab * SLAB + int_s[slab, slot * nproj]


def potential_kernel(nband, table_ref, part_ref, y_ref, *refs):
    pieces, (out_ref, v_ref, int_s, sem) = refs[:nband], refs[nband:]
    copy = pltpu.make_async_copy(table_ref, int_s, sem)
    copy.start()
    copy.wait()
    scale = 1.0 / filter_half_width
    piece = NY // nband
    for back in range(nband):
        at = lax.rem(int_s[4, 8] - back + nband, nband) * piece
        for plane in range(part_ref.shape[0] // NY):
            spot = pl.ds(pl.multiple_of(plane * NY + at, 8), piece)
            value = pieces[back][plane * piece : (plane + 1) * piece, :]
            v_ref[spot, :] = value
            out_ref[spot, :] = part_ref[spot, :] + scale * (value * y_ref[spot, :])


def first_kernel(dims, slabs, *refs):
    n, cap, nproj, foot, chunk = dims
    half = n // 2
    int_ref, part_ref, w_ref, c_ref = refs[:4]
    p_refs, (send_ref, r_ref, int_s, sem) = refs[4:-4], refs[-4:]
    p_refs = (None,) * slabs[0] + tuple(p_refs)
    copy = pltpu.make_async_copy(int_ref, int_s, sem)
    copy.start()
    if slabs[0] == 0:
        send_ref[0 : half * SLAB, :] = part_ref[...]
        send_ref[half * SLAB :, :] = jnp.zeros((8, 128), f32)
    copy.wait()
    start_of = starts_from(int_s, nproj)
    scale = 1.0 / filter_half_width
    couple(dims, slabs, half, c_ref[...], w_ref, p_refs, start_of, send_ref, scale)
    next_partials(dims, slabs, half, send_ref, p_refs, start_of, r_ref)


def chip_kernel(dims, last, *refs):
    n, cap, nproj, foot, chunk = dims
    half = n // 2
    int_ref, y_ref, got_ref, prev_ref, v_ref, w_ref = refs[:6]
    p_refs = refs[6 : 7 + half]
    out_ref, other_ref, pad_ref, int_s, sem = refs[7 + half : 12 + half]
    copy = pltpu.make_async_copy(int_ref, int_s, sem)
    copy.start()
    other_ref[0 : half * SLAB, :] = got_ref[0 : half * SLAB, :]
    other_ref[half * SLAB :, :] = jnp.zeros((SLAB, 128), f32)
    slabs = range(1 if last else half)
    scale = 2.0 / filter_half_width

    def bases():
        copy.wait()
        return (
            [int_s[half, local] for local in range(half)],
            [int_s[half, half + local] for local in range(half)],
        )

    stencil(y_ref, other_ref, v_ref, prev_ref, out_ref, pad_ref, len(slabs), scale, bases)
    below = slice(half * SLAB, half * SLAB + half)
    rows = jnp.concatenate([y_ref[below, :], got_ref[below, :]], 0)
    coefficients = by_owner(rows, n, chunk)
    start_of = starts_from(int_s, nproj)
    couple(dims, slabs, half, coefficients, w_ref, p_refs, start_of, out_ref, scale)
    if not last:
        out_ref[half * SLAB :, :] = jnp.zeros((8, 128), f32)
        next_partials(dims, slabs, half, out_ref, p_refs, start_of, refs[12 + half])


def chip_table(n):
    half = n // 2
    table = np.zeros((n, 4 * half + n), np.int32)
    for device in range(n):
        chip, core = device // 2, device % 2
        for local in range(half):
            there = chip ^ local
            same = local * SLAB
            far = there + (1 if core else -1)
            cross = (far ^ chip) * SLAB if 0 <= far < half else half * SLAB
            table[device, 2 * half + local] = same if core else cross
            table[device, 3 * half + local] = cross if core else same
        for owner in range(n):
            table[device, 4 * half + owner] = owner % 2 * half if core == 0 else (1 - owner % 2) * half
            table[device, 4 * half + owner] += owner // 2 ^ chip
    return table


def chip_form(psi, potential, projectors, offsets, intersection, dmat):
    n = lax.axis_size("domain")
    nband = lax.axis_size("band")
    cap, nproj = projectors.shape[2], projectors.shape[3]
    foot = projectors.shape[4] // 128
    chunk = cap * nproj
    lanes = n * chunk
    half = n // 2
    dims = (n, cap, nproj, foot, chunk)
    p = projectors.reshape(lanes, foot * 128)
    v_piece = potential.reshape(-1, 128)
    couplings = dmat.transpose(1, 2, 0).reshape(nproj * nproj, dmat.shape[0])
    domain = lax.axis_index("domain")
    info = jnp.concatenate(
        [
            lax.dynamic_slice_in_dim(jnp.asarray(chip_table(n)), domain, 1, 0)[0],
            lax.axis_index("band").astype(jnp.int32)[None],
        ]
    )
    params = pltpu.CompilerParams(vmem_limit_bytes=40 * 1024 * 1024)
    HBM = pl.BlockSpec(memory_space=pltpu.HBM)
    small = pl.CostEstimate(flops=1, bytes_accessed=1, transcendentals=0)
    large = pl.CostEstimate(flops=10**10, bytes_accessed=1, transcendentals=0)
    larger = pl.CostEstimate(flops=10**10, bytes_accessed=1, transcendentals=0)

    def shape(rows, dtype=f32):
        return jax.ShapeDtypeStruct((rows, 128), dtype)

    def swap(x, step):
        return lax.ppermute(x, "domain", [(i, i ^ step) for i in range(n)])

    sources = (psi.reshape(SLAB, 128), p, offsets[0].T, intersection[0].T, couplings, v_piece)
    sources = [pltpu.with_memory_space_constraint(x, pltpu.HBM) for x in sources]
    pack, p = pl.pallas_call(
        functools.partial(pack_kernel, dims),
        out_shape=(
            shape(SLAB + v_piece.shape[0] + SMALL),
            jax.ShapeDtypeStruct(p.shape, f32),
        ),
        in_specs=[HBM] * 6,
        out_specs=(VMEM, VMEM),
        scratch_shapes=[
            pltpu.SMEM((cap, n), jnp.int32),
            pltpu.SMEM((cap, n), jnp.int32),
            pltpu.VMEM(couplings.shape, f32),
            pltpu.VMEM((lanes, 128), f32),
            pltpu.SemaphoreType.DMA((6,)),
        ],
        compiler_params=params,
        cost_estimate=small,
        name="pack",
    )(*sources)
    packs = [pack] + [swap(pack, 2 * local) for local in range(1, half)]
    p = pl.pallas_call(
        gate_kernel,
        out_shape=jax.ShapeDtypeStruct(p.shape, f32),
        in_specs=[VMEM, VMEM],
        out_specs=VMEM,
        input_output_aliases={1: 0},
        compiler_params=params,
        cost_estimate=small,
        name="gate",
    )(packs[3], p)
    own, v_piece = pl.pallas_call(
        sort_kernel,
        out_shape=(shape(half * (SLAB + SMALL)), shape(half * v_piece.shape[0])),
        in_specs=[VMEM] * half,
        out_specs=(VMEM, VMEM),
        compiler_params=params,
        cost_estimate=small,
        name="sort",
    )(*packs)
    got = swap(own, 1)
    pieces = [v_piece]
    for back in range(1, nband):
        ring = [(i, (i + back) % nband) for i in range(nband)]
        pieces.append(lax.ppermute(v_piece, "band", ring))
    p_x, p_y = swap(p, 2), swap(p, 4)
    halves = (jax.ShapeDtypeStruct((lanes // 2, foot * 128), f32),) * 2
    top, bottom = pl.pallas_call(
        relay_kernel,
        out_shape=halves,
        in_specs=[VMEM] * 2,
        out_specs=(VMEM, VMEM),
        compiler_params=params,
        cost_estimate=large,
        name="relay",
    )(p_x, p_y)
    all_p = [p, p_x, p_y, swap(top, 4), swap(bottom, 2)]
    other = pltpu.VMEM(((half + 1) * SLAB, 128), f32)
    padded = pltpu.VMEM((half * 6 * (NY + 16), 128), f32)
    row_scratch = pltpu.VMEM((half * lanes, 128), f32)
    ints = [pltpu.SMEM((8, 128), jnp.int32), pltpu.SemaphoreType.DMA(())]
    part, previous, w, c, table = pl.pallas_call(
        functools.partial(begin_kernel, dims),
        out_shape=(
            shape(half * SLAB),
            shape(half * SLAB),
            shape(half * lanes),
            shape(n),
            shape(8, jnp.int32),
        ),
        in_specs=[SMEM] + [VMEM] * 2,
        out_specs=(VMEM,) * 5,
        scratch_shapes=[other, padded, pltpu.VMEM((n, 2 * nproj, 128), f32)],
        compiler_params=params,
        cost_estimate=small,
        name="begin",
    )(info, own, got)
    sent = shape(half * SLAB + 8)
    part, v = pl.pallas_call(
        functools.partial(potential_kernel, nband),
        out_shape=(shape(half * SLAB), shape(half * SLAB)),
        in_specs=[VMEM] * (3 + nband),
        out_specs=(VMEM, VMEM),
        scratch_shapes=ints,
        compiler_params=params,
        cost_estimate=larger,
        name="potential",
    )(table, part, previous, *pieces)
    y = part
    for slabs in (range(half - 1), range(half - 1, half)):
        start, late = slabs[0], slabs[0] > 0
        some_p = all_p[start:] if late else all_p[: half - 1]
        y = pl.pallas_call(
            functools.partial(first_kernel, dims, slabs),
            out_shape=sent,
            in_specs=[VMEM] * (4 + len(some_p)),
            out_specs=VMEM,
            scratch_shapes=[pltpu.VMEM((len(slabs) * lanes, 128), f32)] + ints,
            input_output_aliases={1: 0} if late else {},
            compiler_params=params,
            cost_estimate=small,
            name="first_late" if late else "first",
        )(table, y, w, c, *some_p)
    for degree in range(1, DEGREE):
        last = degree == DEGREE - 1
        following = pl.pallas_call(
            functools.partial(chip_kernel, dims, last),
            out_shape=shape(SLAB) if last else sent,
            in_specs=[VMEM] * (7 + half),
            out_specs=VMEM,
            scratch_shapes=[other, padded] + ints + ([] if last else [row_scratch]),
            compiler_params=params,
            name="last" if last else "next",
        )(table, y, swap(y, 1), previous, v, w, *all_p)
        previous, y = y, following
    return y.reshape(psi.shape)


def shards(psi, potential, projectors, offsets, intersection, dmat):
    n = lax.axis_size("domain")
    nband = lax.axis_size("band")
    fits = n == 8 and potential.shape[1] % 8 == 0 and nband <= 8
    form = chip_form if fits else slab_form
    return form(psi, potential, projectors, offsets, intersection, dmat)


def solution(mesh):
    return jax.shard_map(
        shards,
        mesh=mesh,
        in_specs=(
            P("band", "domain", None, None),
            P("domain", "band", None),
            P("domain", None, None, None, None),
            P("domain", None, None),
            P("domain", None, None),
            P("domain", None, None),
        ),
        out_specs=P("band", "domain", None, None),
        check_vma=False,
    )
```

```python
import functools

import jax
import jax.numpy as jnp
import numpy as np
from jax import lax
from jax.experimental import pallas as pl
from jax.experimental.pallas import tpu as pltpu
from jax.sharding import PartitionSpec as P

DEGREE = 4

stencil_weights = (
    -5369.0 / 1800.0,
    12.0 / 7.0,
    -15.0 / 56.0,
    10.0 / 189.0,
    -1.0 / 112.0,
    2.0 / 1925.0,
    -1.0 / 16632.0,
)
reach = len(stencil_weights) - 1
filter_center = 6.0
filter_half_width = 4.0
highest = lax.Precision.HIGHEST
f32 = jnp.float32
VMEM = pl.BlockSpec(memory_space=pltpu.VMEM)
SMEM = pl.BlockSpec(memory_space=pltpu.SMEM)


def iota(shape, dim):
    return lax.broadcasted_iota(jnp.int32, shape, dim)


def partials(y_ref, p_ref, off_ref, r_ref, dims):
    n, cap, nproj, foot, chunk = dims
    for slot in range(n * cap):
        start = off_ref[slot % cap, slot // cap]
        rows = pl.ds(slot * nproj, nproj)
        total = None
        for tile in range(foot):
            cells = jnp.broadcast_to(y_ref[pl.ds(start + tile, 1), :], (nproj, 128))
            term = p_ref[rows, tile * 128 : (tile + 1) * 128] * cells
            total = term if total is None else total + term
        r_ref[rows, :] = total
    return lax.dot_general(
        jnp.ones((8, 128), f32),
        r_ref[...],
        (((1,), (1,)), ((), ())),
        precision=highest,
        preferred_element_type=f32,
    )


def by_owner(rows, n, chunk):
    lanes = n * chunk
    shape = (n, lanes)
    ahead = (iota(shape, 1) // chunk - iota(shape, 0) + n) % n
    out = rows
    for step in range(1, n):
        moved = pltpu.roll(rows, n - step, 0)
        moved = pltpu.roll(moved, step * chunk, 1)
        out = jnp.where(ahead == step, moved, out)
    return out


def start_kernel(dims, y_ref, p_ref, off_ref, atom_ref, dmat_ref, out_ref, r_ref):
    n, cap, nproj, foot, chunk = dims
    lanes = n * chunk
    out_ref[:, 0, :] = jnp.broadcast_to(
        partials(y_ref, p_ref, off_ref, r_ref, dims)[0:1], (n, lanes)
    )
    lane = iota((1, lanes), 1) // nproj
    atoms = jnp.zeros((1, lanes), f32)
    for slot in range(n * cap):
        value = atom_ref[slot % cap, slot // cap].astype(f32)
        atoms = jnp.where(lane == slot, value, atoms)
    out_ref[:, 1, :] = jnp.broadcast_to(atoms, (n, lanes))
    count = dmat_ref.shape[1]
    for group in range(128 // count):
        block = dmat_ref[group * 2 * nproj : (group + 1) * 2 * nproj, :]
        for peer in range(n):
            out_ref[peer, 8:, group * count : (group + 1) * count] = block


def step_kernel(dims, nband, first, last, *refs):
    n, cap, nproj, foot, chunk = dims
    refs = list(refs)
    take = lambda: refs.pop(0)
    info_ref, off_ref = take(), take()
    y_ref, a_ref, b_ref, got_ref, p_ref = take(), take(), take(), take(), take()
    if first:
        atom_ref = take()
        v_pieces = [take() for _ in range(nband)]
        prev_ref = None
    else:
        prev_ref, v_ref, w_ref = take(), take(), take()
    out_ref = take()
    if not last:
        c_ref = take()
    if first:
        v_ref, w_ref = take(), take()
    pad_ref, lo_ref, hi_ref, r_ref = take(), take(), take(), take()
    cells = y_ref.shape[0]
    ny = 32
    planes = cells // ny
    lanes = n * chunk
    weights = stencil_weights

    if first:
        if nband > 1:
            piece_rows = ny // nband
            for back, piece in enumerate(v_pieces):
                at = lax.rem(info_ref[1] - back + nband, nband) * piece_rows
                for plane in range(planes):
                    spot = pl.multiple_of(plane * ny + at, 8)
                    v_ref[pl.ds(spot, piece_rows), :] = piece[
                        plane * piece_rows : (plane + 1) * piece_rows, :
                    ]
        else:
            v_ref[...] = v_pieces[0][...]
        atoms = by_owner(got_ref[:, 1, :], n, chunk)
        row = iota((chunk, 128), 0)
        column = iota((chunk, 128), 1)
        count = 128 // (nproj // 2)
        parity = (iota((chunk, 2 * nproj), 1) // nproj) == (iota((chunk, 2 * nproj), 0) % 2)
        spread = (iota((2 * nproj, lanes), 1) % nproj == iota((2 * nproj, lanes), 0) % nproj)
        spread = spread.astype(f32)
        for owner in range(n):
            mine = jnp.zeros((chunk, 128), jnp.int32)
            for k in range(cap):
                mine = jnp.where(row // nproj == k, atom_ref[k, owner], mine)
            pick = (column == (row % nproj) // 2 * count + mine) & (mine >= 0)
            entries = lax.dot_general(
                pick.astype(f32),
                got_ref[owner, 8:, 0:128],
                (((1,), (1,)), ((), ())),
                precision=highest,
                preferred_element_type=f32,
            )
            entries = jnp.where(parity, entries, 0.0)
            block = jnp.dot(entries, spread, precision=highest, preferred_element_type=f32)
            mine_row = jnp.zeros((chunk, lanes), f32)
            row_wide = iota((chunk, lanes), 0) // nproj
            for k in range(cap):
                mine_row = jnp.where(row_wide == k, atom_ref[k, owner].astype(f32), mine_row)
            same = (atoms[owner : owner + 1, :] == mine_row) & (mine_row >= 0.0)
            w_ref[pl.ds(owner * chunk, chunk), :] = jnp.where(same, block, 0.0)
        coefficients = by_owner(got_ref[:, 0, :], n, chunk)
    else:
        coefficients = by_owner(got_ref[...], n, chunk)

    odd = jnp.full((cells, 128), info_ref[0], jnp.int32) == 1
    from_a, from_b = a_ref[...], b_ref[...]
    lo_ref[...] = jnp.where(odd, from_a, from_b)
    hi_ref[...] = jnp.where(odd, from_b, from_a)
    tall = ny + 16
    for plane in range(planes):
        own = y_ref[plane * ny : (plane + 1) * ny, :]
        base = plane * tall
        pad_ref[base + 8 : base + 8 + ny, :] = own
        pad_ref[base : base + 8, :] = own[ny - 8 :, :]
        pad_ref[base + 8 + ny : base + tall, :] = own[0:8, :]

    apart = iota((128, 128), 0) - iota((128, 128), 1)
    apart = jnp.abs(apart)
    apart = jnp.minimum(apart, 128 - apart)
    circulant = jnp.full((128, 128), 3.0 * weights[0], f32)
    circulant = jnp.where(apart > reach, 0.0, circulant)
    for distance in range(1, reach + 1):
        circulant = jnp.where(apart == distance, weights[distance], circulant)
    along_z = jnp.dot(y_ref[...], circulant, precision=highest, preferred_element_type=f32)

    scale = (1.0 if first else 2.0) / filter_half_width

    def plane_of(index):
        if index < 0:
            ref, index = lo_ref, index + planes
        elif index >= planes:
            ref, index = hi_ref, index - planes
        else:
            ref = y_ref
        return ref[index * ny : (index + 1) * ny, :]

    for plane in range(planes):
        rows = slice(plane * ny, (plane + 1) * ny)
        base = plane * tall + 8
        own = y_ref[rows, :]
        lap = along_z[rows, :]
        for distance in range(1, reach + 1):
            beside = plane_of(plane + distance) + plane_of(plane - distance)
            beside = beside + pad_ref[base + distance : base + distance + ny, :]
            beside = beside + pad_ref[base - distance : base - distance + ny, :]
            lap = lap + weights[distance] * beside
        value = scale * ((v_ref[rows, :] - filter_center) * own - 0.5 * lap)
        if prev_ref is not None:
            value = value - prev_ref[rows, :]
        out_ref[rows, :] = value

    sublane = iota((foot, 128), 0)
    for slot in range(n * cap):
        owner = slot // cap
        rows = slice(slot * nproj, (slot + 1) * nproj)
        returned = jnp.sum(
            w_ref[rows, :] * coefficients[owner : owner + 1, :], axis=1, keepdims=True
        )
        returned = jnp.broadcast_to(returned * scale, (nproj, 128))
        contrib = jnp.zeros((foot, 128), f32)
        for tile in range(foot):
            term = jnp.sum(
                p_ref[rows, tile * 128 : (tile + 1) * 128] * returned, axis=0, keepdims=True
            )
            contrib = jnp.where(sublane == tile, term, contrib)
        start = off_ref[slot % cap, slot // cap]
        out_ref[pl.ds(start, foot), :] = out_ref[pl.ds(start, foot), :] + contrib

    if not last:
        c_ref[...] = jnp.broadcast_to(
            partials(out_ref, p_ref, off_ref, r_ref, dims)[0:1], (n, lanes)
        )


def beside_slabs(y, n):
    pairs = [(i, i ^ 1) for i in range(n) if i ^ 1 < n]
    cross = [(i, i + 1) for i in range(1, n - 1, 2)] + [(i + 1, i) for i in range(1, n - 1, 2)]
    return lax.ppermute(y, "domain", pairs), lax.ppermute(y, "domain", cross)


def slab_form(psi, potential, projectors, offsets, intersection, dmat):
    n = lax.axis_size("domain")
    nband = lax.axis_size("band")
    cap, nproj = projectors.shape[2], projectors.shape[3]
    foot = projectors.shape[4] // 128
    chunk = cap * nproj
    lanes = n * chunk
    dims = (n, cap, nproj, foot, chunk)
    cells = psi.shape[1] * psi.shape[2]
    y = psi.reshape(cells, 128)
    p = projectors.reshape(lanes, foot * 128)
    off = offsets[0].T
    atom = intersection[0].T
    couplings = dmat.transpose(1, 2, 0).reshape(nproj * nproj, dmat.shape[0])
    info = jnp.stack([lax.axis_index("domain") % 2, lax.axis_index("band")]).astype(jnp.int32)
    params = pltpu.CompilerParams(vmem_limit_bytes=40 * 1024 * 1024)

    start = pl.pallas_call(
        functools.partial(start_kernel, dims),
        out_shape=jax.ShapeDtypeStruct((n, 24, lanes), f32),
        in_specs=[VMEM, VMEM, SMEM, SMEM, VMEM],
        out_specs=VMEM,
        scratch_shapes=[pltpu.VMEM((lanes, 128), f32)],
        compiler_params=params,
        name="first_partials",
    )
    got = lax.all_to_all(
        start(y, p, off, atom, couplings), "domain", split_axis=0, concat_axis=0, tiled=True
    )
    if potential.shape[1] % 8 == 0 and nband <= 8:
        pieces = [potential.reshape(-1, 128)]
        for back in range(1, nband):
            ring = [(i, (i + back) % nband) for i in range(nband)]
            pieces.append(lax.ppermute(pieces[0], "band", ring))
    else:
        pieces = [lax.all_gather(potential, "band", axis=1, tiled=True).reshape(cells, 128)]

    y_shape = jax.ShapeDtypeStruct((cells, 128), f32)
    c_shape = jax.ShapeDtypeStruct((n, lanes), f32)
    scratch = [
        pltpu.VMEM((cells // 32 * 48, 128), f32),
        pltpu.VMEM((cells, 128), f32),
        pltpu.VMEM((cells, 128), f32),
        pltpu.VMEM((lanes, 128), f32),
    ]
    from_a, from_b = beside_slabs(y, n)
    previous = y
    y, c, v, w = pl.pallas_call(
        functools.partial(step_kernel, dims, len(pieces), True, False),
        out_shape=(y_shape, c_shape, y_shape, jax.ShapeDtypeStruct((lanes, lanes), f32)),
        in_specs=[SMEM, SMEM] + [VMEM] * 5 + [SMEM] + [VMEM] * len(pieces),
        out_specs=(VMEM,) * 4,
        scratch_shapes=scratch,
        compiler_params=params,
        name="first_step",
    )(info, off, y, from_a, from_b, got, p, atom, *pieces)
    for degree in range(1, DEGREE):
        last = degree == DEGREE - 1
        got = lax.all_to_all(c, "domain", split_axis=0, concat_axis=0, tiled=True)
        from_a, from_b = beside_slabs(y, n)
        out = pl.pallas_call(
            functools.partial(step_kernel, dims, len(pieces), False, last),
            out_shape=(y_shape,) if last else (y_shape, c_shape),
            in_specs=[SMEM, SMEM] + [VMEM] * 8,
            out_specs=(VMEM,) if last else (VMEM, VMEM),
            scratch_shapes=scratch,
            compiler_params=params,
            name="last_step" if last else "next_step",
        )(info, off, y, from_a, from_b, got, p, previous, v, w)
        previous, y = y, out[0]
        if not last:
            c = out[1]
    return y.reshape(psi.shape)


NY = 32
SLAB = 6 * NY
SMALL = 24


def circulant_z():
    apart = jnp.abs(iota((128, 128), 0) - iota((128, 128), 1))
    apart = jnp.minimum(apart, 128 - apart)
    out = jnp.full((128, 128), 3.0 * stencil_weights[0], f32)
    out = jnp.where(apart > reach, 0.0, out)
    for distance in range(1, reach + 1):
        out = jnp.where(apart == distance, stencil_weights[distance], out)
    return out


def stencil(y_ref, other_ref, v_ref, prev_ref, out_ref, pad_ref, slabs, scale, bases):
    tall = NY + 16
    for plane in range(6 * slabs):
        own = y_ref[plane * NY : (plane + 1) * NY, :]
        base = plane * tall
        pad_ref[base + 8 : base + 8 + NY, :] = own
        pad_ref[base : base + 8, :] = own[NY - 8 :, :]
        pad_ref[base + 8 + NY : base + tall, :] = own[0:8, :]
    along_z = jnp.dot(
        y_ref[0 : slabs * SLAB, :],
        circulant_z(),
        precision=lax.Precision.HIGH,
        preferred_element_type=f32,
    )
    below, above = bases()
    for slab in range(slabs):
        for plane in range(6):
            at = (slab * 6 + plane) * NY
            rows = slice(at, at + NY)
            base = (slab * 6 + plane) * tall + 8
            own = y_ref[rows, :]
            lap = along_z[rows, :]
            for distance in range(1, reach + 1):
                beside = pad_ref[base + distance : base + distance + NY, :]
                beside = beside + pad_ref[base - distance : base - distance + NY, :]
                for index in (plane - distance, plane + distance):
                    if index < 0:
                        spot = pl.multiple_of(below[slab] + (index + 6) * NY, 8)
                        beside = beside + other_ref[pl.ds(spot, NY), :]
                    elif index >= 6:
                        spot = pl.multiple_of(above[slab] + (index - 6) * NY, 8)
                        beside = beside + other_ref[pl.ds(spot, NY), :]
                    else:
                        spot = (slab * 6 + index) * NY
                        beside = beside + y_ref[spot : spot + NY, :]
                lap = lap + stencil_weights[distance] * beside
            if v_ref is None:
                value = scale * (-filter_center * own - 0.5 * lap)
            else:
                value = scale * ((v_ref[rows, :] - filter_center) * own - 0.5 * lap)
            if prev_ref is not None:
                value = value - prev_ref[rows, :]
            out_ref[rows, :] = value


def pack_kernel(dims, *refs):
    n, cap, nproj, foot, chunk = dims
    lanes = n * chunk
    sources, (pack_ref, p_ref), scratch = refs[:6], refs[6:8], refs[8:]
    off_ref, atom_ref, dmat_ref, r_ref, sems = scratch
    small = pack_ref.shape[0] - SMALL
    targets = (
        pack_ref.at[0:SLAB, :],
        p_ref,
        off_ref,
        atom_ref,
        dmat_ref,
        pack_ref.at[SLAB:small, :],
    )
    copies = [
        pltpu.make_async_copy(source, target, sems.at[index])
        for index, (source, target) in enumerate(zip(sources, targets))
    ]
    for copy in copies:
        copy.start()
    for copy in copies[2:]:
        copy.wait()
    lane = iota((1, lanes), 1) // nproj
    atoms = jnp.zeros((1, lanes), f32)
    starts = jnp.zeros((1, lanes), f32)
    for slot in range(n * cap):
        here = lane == slot
        atoms = jnp.where(here, atom_ref[slot % cap, slot // cap].astype(f32), atoms)
        starts = jnp.where(here, off_ref[slot % cap, slot // cap].astype(f32), starts)
    pack_ref[small + 1 : small + 2, :] = atoms
    pack_ref[small + 2 : small + 3, :] = starts
    pack_ref[small + 3 : small + 8, :] = jnp.zeros((5, 128), f32)
    count = dmat_ref.shape[1]
    for group in range(128 // count):
        block = dmat_ref[group * 2 * nproj : (group + 1) * 2 * nproj, :]
        pack_ref[small + 8 :, group * count : (group + 1) * count] = block
    copies[0].wait()
    copies[1].wait()
    pack_ref[small : small + 1, :] = partials(pack_ref, p_ref, off_ref, r_ref, dims)[0:1]


def gate_kernel(*refs):
    pass


def sort_kernel(*refs):
    packs, (pair_ref, v_ref) = refs[:-2], refs[-2:]
    small = packs[0].shape[0] - SMALL
    size = SLAB + SMALL
    for local, pack in enumerate(packs):
        pair_ref[local * size : local * size + SLAB, :] = pack[0:SLAB, :]
        pair_ref[local * size + SLAB : (local + 1) * size, :] = pack[small:, :]
        v_ref[local * (small - SLAB) : (local + 1) * (small - SLAB), :] = pack[SLAB:small, :]


def relay_kernel(x_ref, y_ref, top_ref, bottom_ref):
    rows = top_ref.shape[0]
    top_ref[...] = x_ref[0:rows, :]
    bottom_ref[...] = y_ref[rows:, :]


def begin_kernel(dims, info_ref, own_ref, got_ref, *refs):
    n, cap, nproj, foot, chunk = dims
    half = n // 2
    part_ref, y_ref, w_ref, c_ref, int_ref, other_ref, pad_ref, dmat_ref = refs
    lanes = n * chunk
    size = SLAB + SMALL
    c_rows, atom_rows, start_rows = [], [], []
    for group, source in enumerate((own_ref, got_ref)):
        for local in range(half):
            slab = local * size
            rows = slice(local * SLAB, (local + 1) * SLAB)
            target = other_ref if group else y_ref
            target[rows, :] = source[slab : slab + SLAB, :]
            small = slab + SLAB
            c_rows.append(source[small : small + 1, :])
            atom_rows.append(source[small + 1 : small + 2, :])
            if group == 0:
                start_rows.append(source[small + 2 : small + 3, :])
            dmat_ref[group * half + local] = source[small + 8 : small + SMALL, :]
    other_ref[half * SLAB :, :] = jnp.zeros((SLAB, 128), f32)
    c_ref[...] = by_owner(jnp.concatenate(c_rows, 0), n, chunk)
    atoms = by_owner(jnp.concatenate(atom_rows, 0), n, chunk)
    lane = iota((1, 128), 1)
    table = jnp.zeros((1, 128), jnp.int32)
    for local in range(half):
        int_ref[local : local + 1, :] = start_rows[local].astype(jnp.int32)
        for side in range(2):
            value = info_ref[(2 + side) * half + local]
            table = jnp.where(lane == side * half + local, value, table)
    table = jnp.where(lane == 2 * half, info_ref[4 * half + n], table)
    int_ref[half : half + 1, :] = table
    int_ref[half + 1 :, :] = jnp.zeros((8 - half - 1, 128), jnp.int32)

    def bases():
        return (
            [info_ref[2 * half + local] for local in range(half)],
            [info_ref[3 * half + local] for local in range(half)],
        )

    stencil(
        y_ref, other_ref, None, None, part_ref, pad_ref, half, 1.0 / filter_half_width, bases
    )
    square = (lanes, 128)
    diagonal = iota(square, 0) == iota(square, 1)
    ones = jnp.ones((128, 128), f32)
    column = iota(square, 1).astype(f32)
    count = 128 // (nproj // 2)
    shift = (iota(square, 0) % nproj // 2 * count).astype(f32)
    wide, picks = [], []
    for local in range(half):
        held = jnp.where(diagonal, atom_rows[local], 0.0)
        mine = jnp.dot(held, ones, precision=highest, preferred_element_type=f32)
        mine = jnp.round(mine)
        wide.append(mine)
        picks.append(jnp.where((column == shift + mine) & (mine >= 0.0), 1.0, 0.0))
    tall = half * chunk
    parity = iota((tall, 2 * nproj), 1) // nproj == iota((tall, 2 * nproj), 0) % 2
    spread = iota((2 * nproj, 128), 1) % nproj == iota((2 * nproj, 128), 0) % nproj
    spread = jnp.where(spread, 1.0, 0.0)
    for owner in range(n):
        rows = slice(owner * chunk, (owner + 1) * chunk)
        pick = jnp.concatenate([p[rows, :] for p in picks], 0)
        mine = jnp.concatenate([m[rows, :] for m in wide], 0)
        entries = lax.dot_general(
            pick,
            dmat_ref[info_ref[4 * half + owner]],
            (((1,), (1,)), ((), ())),
            precision=highest,
            preferred_element_type=f32,
        )
        entries = jnp.where(parity, entries, 0.0)
        block = jnp.dot(entries, spread, precision=highest, preferred_element_type=f32)
        same = (atoms[owner : owner + 1, :] == mine) & (mine >= 0.0)
        w_ref[owner * tall : (owner + 1) * tall, :] = jnp.where(same, block, 0.0)


def p_rows(p_refs, slab, slot, nproj, tile):
    ref, at = p_refs[slab], slot * nproj
    if at >= ref.shape[0]:
        ref, at = p_refs[slab + 1], at - ref.shape[0]
    return ref[at : at + nproj, tile * 128 : (tile + 1) * 128]


def swap_rows(x, step):
    if step == 4:
        return pltpu.roll(x, 4, 0)
    low = iota(x.shape, 0) // step % 2 == 0
    return jnp.where(low, pltpu.roll(x, 8 - step, 0), pltpu.roll(x, step, 0))


def column_sums(tiles):
    step = 4
    while step:
        low = iota(tiles[0].shape, 0) // step % 2 == 0
        pairs = [(tiles[t], tiles[t + step]) for t in range(step)]
        tiles = [
            jnp.where(low, a, b) + swap_rows(jnp.where(low, b, a), step) for a, b in pairs
        ]
        step //= 2
    return tiles[0]


def couple(dims, slabs, half, coefficients, w_ref, p_refs, start_of, out_ref, scale):
    n, cap, nproj, foot, chunk = dims
    for slab in slabs:
        for slot in range(n * cap):
            owner, k = slot // cap, slot % cap
            at = (owner * half + slab) * chunk + k * nproj
            back = jnp.sum(
                w_ref[at : at + nproj, :] * coefficients[owner : owner + 1, :],
                axis=1,
                keepdims=True,
            )
            back = jnp.broadcast_to(back * scale, (nproj, 128))
            tiles = [p_rows(p_refs, slab, slot, nproj, tile) * back for tile in range(foot)]
            spot = pl.ds(start_of(slab, slot), foot)
            out_ref[spot, :] = out_ref[spot, :] + column_sums(tiles)


def next_partials(dims, slabs, half, send_ref, p_refs, start_of, r_ref):
    n, cap, nproj, foot, chunk = dims
    lanes = n * chunk
    for index, slab in enumerate(slabs):
        for slot in range(n * cap):
            start = start_of(slab, slot)
            total = None
            for tile in range(foot):
                cells = jnp.broadcast_to(send_ref[pl.ds(start + tile, 1), :], (nproj, 128))
                term = p_rows(p_refs, slab, slot, nproj, tile) * cells
                total = term if total is None else total + term
            at = index * lanes + slot * nproj
            r_ref[at : at + nproj, :] = total
    row = lax.dot_general(
        jnp.ones((8, 128), f32),
        r_ref[...],
        (((1,), (1,)), ((), ())),
        precision=highest,
        preferred_element_type=f32,
    )
    for index, slab in enumerate(slabs):
        send_ref[half * SLAB + slab : half * SLAB + slab + 1, :] = row[
            0:1, index * lanes : (index + 1) * lanes
        ]


def starts_from(int_s, nproj):
    return lambda slab, slot: slab * SLAB + int_s[slab, slot * nproj]


def potential_kernel(nband, table_ref, part_ref, y_ref, *refs):
    pieces, (out_ref, v_ref, int_s, sem) = refs[:nband], refs[nband:]
    copy = pltpu.make_async_copy(table_ref, int_s, sem)
    copy.start()
    copy.wait()
    scale = 1.0 / filter_half_width
    piece = NY // nband
    for back in range(nband):
        at = lax.rem(int_s[4, 8] - back + nband, nband) * piece
        for plane in range(part_ref.shape[0] // NY):
            spot = pl.ds(pl.multiple_of(plane * NY + at, 8), piece)
            value = pieces[back][plane * piece : (plane + 1) * piece, :]
            v_ref[spot, :] = value
            out_ref[spot, :] = part_ref[spot, :] + scale * (value * y_ref[spot, :])


def first_kernel(dims, slabs, *refs):
    n, cap, nproj, foot, chunk = dims
    half = n // 2
    int_ref, part_ref, w_ref, c_ref = refs[:4]
    p_refs, (send_ref, r_ref, int_s, sem) = refs[4:-4], refs[-4:]
    p_refs = (None,) * slabs[0] + tuple(p_refs)
    copy = pltpu.make_async_copy(int_ref, int_s, sem)
    copy.start()
    if slabs[0] == 0:
        send_ref[0 : half * SLAB, :] = part_ref[...]
        send_ref[half * SLAB :, :] = jnp.zeros((8, 128), f32)
    copy.wait()
    start_of = starts_from(int_s, nproj)
    scale = 1.0 / filter_half_width
    couple(dims, slabs, half, c_ref[...], w_ref, p_refs, start_of, send_ref, scale)
    next_partials(dims, slabs, half, send_ref, p_refs, start_of, r_ref)


def chip_kernel(dims, last, *refs):
    n, cap, nproj, foot, chunk = dims
    half = n // 2
    int_ref, y_ref, got_ref, prev_ref, v_ref, w_ref = refs[:6]
    p_refs = refs[6 : 7 + half]
    out_ref, other_ref, pad_ref, int_s, sem = refs[7 + half : 12 + half]
    copy = pltpu.make_async_copy(int_ref, int_s, sem)
    copy.start()
    other_ref[0 : half * SLAB, :] = got_ref[0 : half * SLAB, :]
    other_ref[half * SLAB :, :] = jnp.zeros((SLAB, 128), f32)
    slabs = range(1 if last else half)
    scale = 2.0 / filter_half_width

    def bases():
        copy.wait()
        return (
            [int_s[half, local] for local in range(half)],
            [int_s[half, half + local] for local in range(half)],
        )

    stencil(y_ref, other_ref, v_ref, prev_ref, out_ref, pad_ref, len(slabs), scale, bases)
    below = slice(half * SLAB, half * SLAB + half)
    rows = jnp.concatenate([y_ref[below, :], got_ref[below, :]], 0)
    coefficients = by_owner(rows, n, chunk)
    start_of = starts_from(int_s, nproj)
    couple(dims, slabs, half, coefficients, w_ref, p_refs, start_of, out_ref, scale)
    if not last:
        out_ref[half * SLAB :, :] = jnp.zeros((8, 128), f32)
        next_partials(dims, slabs, half, out_ref, p_refs, start_of, refs[12 + half])


def chip_table(n):
    half = n // 2
    table = np.zeros((n, 4 * half + n), np.int32)
    for device in range(n):
        chip, core = device // 2, device % 2
        for local in range(half):
            there = chip ^ local
            same = local * SLAB
            far = there + (1 if core else -1)
            cross = (far ^ chip) * SLAB if 0 <= far < half else half * SLAB
            table[device, 2 * half + local] = same if core else cross
            table[device, 3 * half + local] = cross if core else same
        for owner in range(n):
            table[device, 4 * half + owner] = owner % 2 * half if core == 0 else (1 - owner % 2) * half
            table[device, 4 * half + owner] += owner // 2 ^ chip
    return table


def chip_form(psi, potential, projectors, offsets, intersection, dmat):
    n = lax.axis_size("domain")
    nband = lax.axis_size("band")
    cap, nproj = projectors.shape[2], projectors.shape[3]
    foot = projectors.shape[4] // 128
    chunk = cap * nproj
    lanes = n * chunk
    half = n // 2
    dims = (n, cap, nproj, foot, chunk)
    p = projectors.reshape(lanes, foot * 128)
    v_piece = potential.reshape(-1, 128)
    couplings = dmat.transpose(1, 2, 0).reshape(nproj * nproj, dmat.shape[0])
    domain = lax.axis_index("domain")
    info = jnp.concatenate(
        [
            lax.dynamic_slice_in_dim(jnp.asarray(chip_table(n)), domain, 1, 0)[0],
            lax.axis_index("band").astype(jnp.int32)[None],
        ]
    )
    params = pltpu.CompilerParams(vmem_limit_bytes=40 * 1024 * 1024)
    HBM = pl.BlockSpec(memory_space=pltpu.HBM)
    small = pl.CostEstimate(flops=1, bytes_accessed=1, transcendentals=0)
    large = pl.CostEstimate(flops=10**10, bytes_accessed=1, transcendentals=0)
    larger = pl.CostEstimate(flops=10**10, bytes_accessed=1, transcendentals=0)

    def shape(rows, dtype=f32):
        return jax.ShapeDtypeStruct((rows, 128), dtype)

    def swap(x, step):
        return lax.ppermute(x, "domain", [(i, i ^ step) for i in range(n)])

    sources = (psi.reshape(SLAB, 128), p, offsets[0].T, intersection[0].T, couplings, v_piece)
    sources = [pltpu.with_memory_space_constraint(x, pltpu.HBM) for x in sources]
    pack, p = pl.pallas_call(
        functools.partial(pack_kernel, dims),
        out_shape=(
            shape(SLAB + v_piece.shape[0] + SMALL),
            jax.ShapeDtypeStruct(p.shape, f32),
        ),
        in_specs=[HBM] * 6,
        out_specs=(VMEM, VMEM),
        scratch_shapes=[
            pltpu.SMEM((cap, n), jnp.int32),
            pltpu.SMEM((cap, n), jnp.int32),
            pltpu.VMEM(couplings.shape, f32),
            pltpu.VMEM((lanes, 128), f32),
            pltpu.SemaphoreType.DMA((6,)),
        ],
        compiler_params=params,
        cost_estimate=small,
        name="pack",
    )(*sources)
    packs = [pack] + [swap(pack, 2 * local) for local in range(1, half)]
    p = pl.pallas_call(
        gate_kernel,
        out_shape=jax.ShapeDtypeStruct(p.shape, f32),
        in_specs=[VMEM, VMEM],
        out_specs=VMEM,
        input_output_aliases={1: 0},
        compiler_params=params,
        cost_estimate=small,
        name="gate",
    )(packs[3], p)
    own, v_piece = pl.pallas_call(
        sort_kernel,
        out_shape=(shape(half * (SLAB + SMALL)), shape(half * v_piece.shape[0])),
        in_specs=[VMEM] * half,
        out_specs=(VMEM, VMEM),
        compiler_params=params,
        cost_estimate=small,
        name="sort",
    )(*packs)
    got = swap(own, 1)
    pieces = [v_piece]
    for back in range(1, nband):
        ring = [(i, (i + back) % nband) for i in range(nband)]
        pieces.append(lax.ppermute(v_piece, "band", ring))
    p_x, p_y = swap(p, 2), swap(p, 4)
    halves = (jax.ShapeDtypeStruct((lanes // 2, foot * 128), f32),) * 2
    top, bottom = pl.pallas_call(
        relay_kernel,
        out_shape=halves,
        in_specs=[VMEM] * 2,
        out_specs=(VMEM, VMEM),
        compiler_params=params,
        cost_estimate=large,
        name="relay",
    )(p_x, p_y)
    all_p = [p, p_x, p_y, swap(top, 4), swap(bottom, 2)]
    other = pltpu.VMEM(((half + 1) * SLAB, 128), f32)
    padded = pltpu.VMEM((half * 6 * (NY + 16), 128), f32)
    row_scratch = pltpu.VMEM((half * lanes, 128), f32)
    ints = [pltpu.SMEM((8, 128), jnp.int32), pltpu.SemaphoreType.DMA(())]
    part, previous, w, c, table = pl.pallas_call(
        functools.partial(begin_kernel, dims),
        out_shape=(
            shape(half * SLAB),
            shape(half * SLAB),
            shape(half * lanes),
            shape(n),
            shape(8, jnp.int32),
        ),
        in_specs=[SMEM] + [VMEM] * 2,
        out_specs=(VMEM,) * 5,
        scratch_shapes=[other, padded, pltpu.VMEM((n, 2 * nproj, 128), f32)],
        compiler_params=params,
        cost_estimate=small,
        name="begin",
    )(info, own, got)
    sent = shape(half * SLAB + 8)
    part, v = pl.pallas_call(
        functools.partial(potential_kernel, nband),
        out_shape=(shape(half * SLAB), shape(half * SLAB)),
        in_specs=[VMEM] * (3 + nband),
        out_specs=(VMEM, VMEM),
        scratch_shapes=ints,
        compiler_params=params,
        cost_estimate=larger,
        name="potential",
    )(table, part, previous, *pieces)
    y = part
    for slabs in (range(half - 1), range(half - 1, half)):
        start, late = slabs[0], slabs[0] > 0
        some_p = all_p[start:] if late else all_p[: half - 1]
        y = pl.pallas_call(
            functools.partial(first_kernel, dims, slabs),
            out_shape=sent,
            in_specs=[VMEM] * (4 + len(some_p)),
            out_specs=VMEM,
            scratch_shapes=[pltpu.VMEM((len(slabs) * lanes, 128), f32)] + ints,
            input_output_aliases={1: 0} if late else {},
            compiler_params=params,
            cost_estimate=small,
            name="first_late" if late else "first",
        )(table, y, w, c, *some_p)
    for degree in range(1, DEGREE):
        last = degree == DEGREE - 1
        following = pl.pallas_call(
            functools.partial(chip_kernel, dims, last),
            out_shape=shape(SLAB) if last else sent,
            in_specs=[VMEM] * (7 + half),
            out_specs=VMEM,
            scratch_shapes=[other, padded] + ints + ([] if last else [row_scratch]),
            compiler_params=params,
            name="last" if last else "next",
        )(table, y, swap(y, 1), previous, v, w, *all_p)
        previous, y = y, following
    return y.reshape(psi.shape)


def shards(psi, potential, projectors, offsets, intersection, dmat):
    n = lax.axis_size("domain")
    nband = lax.axis_size("band")
    fits = n == 8 and potential.shape[1] % 8 == 0 and nband <= 8
    form = chip_form if fits else slab_form
    return form(psi, potential, projectors, offsets, intersection, dmat)


def solution(mesh):
    return jax.shard_map(
        shards,
        mesh=mesh,
        in_specs=(
            P("band", "domain", None, None),
            P("domain", "band", None),
            P("domain", None, None, None, None),
            P("domain", None, None),
            P("domain", None, None),
            P("domain", None, None),
        ),
        out_specs=P("band", "domain", None, None),
        check_vma=False,
    )
```

```python
import functools

import jax
import jax.numpy as jnp
import numpy as np
from jax import lax
from jax.experimental import pallas as pl
from jax.experimental.pallas import tpu as pltpu
from jax.sharding import PartitionSpec as P

DEGREE = 4

stencil_weights = (
    -5369.0 / 1800.0,
    12.0 / 7.0,
    -15.0 / 56.0,
    10.0 / 189.0,
    -1.0 / 112.0,
    2.0 / 1925.0,
    -1.0 / 16632.0,
)
reach = len(stencil_weights) - 1
filter_center = 6.0
filter_half_width = 4.0
highest = lax.Precision.HIGHEST
f32 = jnp.float32
VMEM = pl.BlockSpec(memory_space=pltpu.VMEM)
SMEM = pl.BlockSpec(memory_space=pltpu.SMEM)


def iota(shape, dim):
    return lax.broadcasted_iota(jnp.int32, shape, dim)


def partials(y_ref, p_ref, off_ref, r_ref, dims):
    n, cap, nproj, foot, chunk = dims
    for slot in range(n * cap):
        start = off_ref[slot % cap, slot // cap]
        rows = pl.ds(slot * nproj, nproj)
        total = None
        for tile in range(foot):
            cells = jnp.broadcast_to(y_ref[pl.ds(start + tile, 1), :], (nproj, 128))
            term = p_ref[rows, tile * 128 : (tile + 1) * 128] * cells
            total = term if total is None else total + term
        r_ref[rows, :] = total
    return lax.dot_general(
        jnp.ones((8, 128), f32),
        r_ref[...],
        (((1,), (1,)), ((), ())),
        precision=highest,
        preferred_element_type=f32,
    )


def by_owner(rows, n, chunk):
    lanes = n * chunk
    shape = (n, lanes)
    ahead = (iota(shape, 1) // chunk - iota(shape, 0) + n) % n
    out = rows
    for step in range(1, n):
        moved = pltpu.roll(rows, n - step, 0)
        moved = pltpu.roll(moved, step * chunk, 1)
        out = jnp.where(ahead == step, moved, out)
    return out


def start_kernel(dims, y_ref, p_ref, off_ref, atom_ref, dmat_ref, out_ref, r_ref):
    n, cap, nproj, foot, chunk = dims
    lanes = n * chunk
    out_ref[:, 0, :] = jnp.broadcast_to(
        partials(y_ref, p_ref, off_ref, r_ref, dims)[0:1], (n, lanes)
    )
    lane = iota((1, lanes), 1) // nproj
    atoms = jnp.zeros((1, lanes), f32)
    for slot in range(n * cap):
        value = atom_ref[slot % cap, slot // cap].astype(f32)
        atoms = jnp.where(lane == slot, value, atoms)
    out_ref[:, 1, :] = jnp.broadcast_to(atoms, (n, lanes))
    count = dmat_ref.shape[1]
    for group in range(128 // count):
        block = dmat_ref[group * 2 * nproj : (group + 1) * 2 * nproj, :]
        for peer in range(n):
            out_ref[peer, 8:, group * count : (group + 1) * count] = block


def step_kernel(dims, nband, first, last, *refs):
    n, cap, nproj, foot, chunk = dims
    refs = list(refs)
    take = lambda: refs.pop(0)
    info_ref, off_ref = take(), take()
    y_ref, a_ref, b_ref, got_ref, p_ref = take(), take(), take(), take(), take()
    if first:
        atom_ref = take()
        v_pieces = [take() for _ in range(nband)]
        prev_ref = None
    else:
        prev_ref, v_ref, w_ref = take(), take(), take()
    out_ref = take()
    if not last:
        c_ref = take()
    if first:
        v_ref, w_ref = take(), take()
    pad_ref, lo_ref, hi_ref, r_ref = take(), take(), take(), take()
    cells = y_ref.shape[0]
    ny = 32
    planes = cells // ny
    lanes = n * chunk
    weights = stencil_weights

    if first:
        if nband > 1:
            piece_rows = ny // nband
            for back, piece in enumerate(v_pieces):
                at = lax.rem(info_ref[1] - back + nband, nband) * piece_rows
                for plane in range(planes):
                    spot = pl.multiple_of(plane * ny + at, 8)
                    v_ref[pl.ds(spot, piece_rows), :] = piece[
                        plane * piece_rows : (plane + 1) * piece_rows, :
                    ]
        else:
            v_ref[...] = v_pieces[0][...]
        atoms = by_owner(got_ref[:, 1, :], n, chunk)
        row = iota((chunk, 128), 0)
        column = iota((chunk, 128), 1)
        count = 128 // (nproj // 2)
        parity = (iota((chunk, 2 * nproj), 1) // nproj) == (iota((chunk, 2 * nproj), 0) % 2)
        spread = (iota((2 * nproj, lanes), 1) % nproj == iota((2 * nproj, lanes), 0) % nproj)
        spread = spread.astype(f32)
        for owner in range(n):
            mine = jnp.zeros((chunk, 128), jnp.int32)
            for k in range(cap):
                mine = jnp.where(row // nproj == k, atom_ref[k, owner], mine)
            pick = (column == (row % nproj) // 2 * count + mine) & (mine >= 0)
            entries = lax.dot_general(
                pick.astype(f32),
                got_ref[owner, 8:, 0:128],
                (((1,), (1,)), ((), ())),
                precision=highest,
                preferred_element_type=f32,
            )
            entries = jnp.where(parity, entries, 0.0)
            block = jnp.dot(entries, spread, precision=highest, preferred_element_type=f32)
            mine_row = jnp.zeros((chunk, lanes), f32)
            row_wide = iota((chunk, lanes), 0) // nproj
            for k in range(cap):
                mine_row = jnp.where(row_wide == k, atom_ref[k, owner].astype(f32), mine_row)
            same = (atoms[owner : owner + 1, :] == mine_row) & (mine_row >= 0.0)
            w_ref[pl.ds(owner * chunk, chunk), :] = jnp.where(same, block, 0.0)
        coefficients = by_owner(got_ref[:, 0, :], n, chunk)
    else:
        coefficients = by_owner(got_ref[...], n, chunk)

    odd = jnp.full((cells, 128), info_ref[0], jnp.int32) == 1
    from_a, from_b = a_ref[...], b_ref[...]
    lo_ref[...] = jnp.where(odd, from_a, from_b)
    hi_ref[...] = jnp.where(odd, from_b, from_a)
    tall = ny + 16
    for plane in range(planes):
        own = y_ref[plane * ny : (plane + 1) * ny, :]
        base = plane * tall
        pad_ref[base + 8 : base + 8 + ny, :] = own
        pad_ref[base : base + 8, :] = own[ny - 8 :, :]
        pad_ref[base + 8 + ny : base + tall, :] = own[0:8, :]

    apart = iota((128, 128), 0) - iota((128, 128), 1)
    apart = jnp.abs(apart)
    apart = jnp.minimum(apart, 128 - apart)
    circulant = jnp.full((128, 128), 3.0 * weights[0], f32)
    circulant = jnp.where(apart > reach, 0.0, circulant)
    for distance in range(1, reach + 1):
        circulant = jnp.where(apart == distance, weights[distance], circulant)
    along_z = jnp.dot(y_ref[...], circulant, precision=highest, preferred_element_type=f32)

    scale = (1.0 if first else 2.0) / filter_half_width

    def plane_of(index):
        if index < 0:
            ref, index = lo_ref, index + planes
        elif index >= planes:
            ref, index = hi_ref, index - planes
        else:
            ref = y_ref
        return ref[index * ny : (index + 1) * ny, :]

    for plane in range(planes):
        rows = slice(plane * ny, (plane + 1) * ny)
        base = plane * tall + 8
        own = y_ref[rows, :]
        lap = along_z[rows, :]
        for distance in range(1, reach + 1):
            beside = plane_of(plane + distance) + plane_of(plane - distance)
            beside = beside + pad_ref[base + distance : base + distance + ny, :]
            beside = beside + pad_ref[base - distance : base - distance + ny, :]
            lap = lap + weights[distance] * beside
        value = scale * ((v_ref[rows, :] - filter_center) * own - 0.5 * lap)
        if prev_ref is not None:
            value = value - prev_ref[rows, :]
        out_ref[rows, :] = value

    sublane = iota((foot, 128), 0)
    for slot in range(n * cap):
        owner = slot // cap
        rows = slice(slot * nproj, (slot + 1) * nproj)
        returned = jnp.sum(
            w_ref[rows, :] * coefficients[owner : owner + 1, :], axis=1, keepdims=True
        )
        returned = jnp.broadcast_to(returned * scale, (nproj, 128))
        contrib = jnp.zeros((foot, 128), f32)
        for tile in range(foot):
            term = jnp.sum(
                p_ref[rows, tile * 128 : (tile + 1) * 128] * returned, axis=0, keepdims=True
            )
            contrib = jnp.where(sublane == tile, term, contrib)
        start = off_ref[slot % cap, slot // cap]
        out_ref[pl.ds(start, foot), :] = out_ref[pl.ds(start, foot), :] + contrib

    if not last:
        c_ref[...] = jnp.broadcast_to(
            partials(out_ref, p_ref, off_ref, r_ref, dims)[0:1], (n, lanes)
        )


def beside_slabs(y, n):
    pairs = [(i, i ^ 1) for i in range(n) if i ^ 1 < n]
    cross = [(i, i + 1) for i in range(1, n - 1, 2)] + [(i + 1, i) for i in range(1, n - 1, 2)]
    return lax.ppermute(y, "domain", pairs), lax.ppermute(y, "domain", cross)


def slab_form(psi, potential, projectors, offsets, intersection, dmat):
    n = lax.axis_size("domain")
    nband = lax.axis_size("band")
    cap, nproj = projectors.shape[2], projectors.shape[3]
    foot = projectors.shape[4] // 128
    chunk = cap * nproj
    lanes = n * chunk
    dims = (n, cap, nproj, foot, chunk)
    cells = psi.shape[1] * psi.shape[2]
    y = psi.reshape(cells, 128)
    p = projectors.reshape(lanes, foot * 128)
    off = offsets[0].T
    atom = intersection[0].T
    couplings = dmat.transpose(1, 2, 0).reshape(nproj * nproj, dmat.shape[0])
    info = jnp.stack([lax.axis_index("domain") % 2, lax.axis_index("band")]).astype(jnp.int32)
    params = pltpu.CompilerParams(vmem_limit_bytes=40 * 1024 * 1024)

    start = pl.pallas_call(
        functools.partial(start_kernel, dims),
        out_shape=jax.ShapeDtypeStruct((n, 24, lanes), f32),
        in_specs=[VMEM, VMEM, SMEM, SMEM, VMEM],
        out_specs=VMEM,
        scratch_shapes=[pltpu.VMEM((lanes, 128), f32)],
        compiler_params=params,
        name="first_partials",
    )
    got = lax.all_to_all(
        start(y, p, off, atom, couplings), "domain", split_axis=0, concat_axis=0, tiled=True
    )
    if potential.shape[1] % 8 == 0 and nband <= 8:
        pieces = [potential.reshape(-1, 128)]
        for back in range(1, nband):
            ring = [(i, (i + back) % nband) for i in range(nband)]
            pieces.append(lax.ppermute(pieces[0], "band", ring))
    else:
        pieces = [lax.all_gather(potential, "band", axis=1, tiled=True).reshape(cells, 128)]

    y_shape = jax.ShapeDtypeStruct((cells, 128), f32)
    c_shape = jax.ShapeDtypeStruct((n, lanes), f32)
    scratch = [
        pltpu.VMEM((cells // 32 * 48, 128), f32),
        pltpu.VMEM((cells, 128), f32),
        pltpu.VMEM((cells, 128), f32),
        pltpu.VMEM((lanes, 128), f32),
    ]
    from_a, from_b = beside_slabs(y, n)
    previous = y
    y, c, v, w = pl.pallas_call(
        functools.partial(step_kernel, dims, len(pieces), True, False),
        out_shape=(y_shape, c_shape, y_shape, jax.ShapeDtypeStruct((lanes, lanes), f32)),
        in_specs=[SMEM, SMEM] + [VMEM] * 5 + [SMEM] + [VMEM] * len(pieces),
        out_specs=(VMEM,) * 4,
        scratch_shapes=scratch,
        compiler_params=params,
        name="first_step",
    )(info, off, y, from_a, from_b, got, p, atom, *pieces)
    for degree in range(1, DEGREE):
        last = degree == DEGREE - 1
        got = lax.all_to_all(c, "domain", split_axis=0, concat_axis=0, tiled=True)
        from_a, from_b = beside_slabs(y, n)
        out = pl.pallas_call(
            functools.partial(step_kernel, dims, len(pieces), False, last),
            out_shape=(y_shape,) if last else (y_shape, c_shape),
            in_specs=[SMEM, SMEM] + [VMEM] * 8,
            out_specs=(VMEM,) if last else (VMEM, VMEM),
            scratch_shapes=scratch,
            compiler_params=params,
            name="last_step" if last else "next_step",
        )(info, off, y, from_a, from_b, got, p, previous, v, w)
        previous, y = y, out[0]
        if not last:
            c = out[1]
    return y.reshape(psi.shape)


NY = 32
SLAB = 6 * NY
SMALL = 24


def circulant_z():
    apart = jnp.abs(iota((128, 128), 0) - iota((128, 128), 1))
    apart = jnp.minimum(apart, 128 - apart)
    out = jnp.full((128, 128), 3.0 * stencil_weights[0], f32)
    out = jnp.where(apart > reach, 0.0, out)
    for distance in range(1, reach + 1):
        out = jnp.where(apart == distance, stencil_weights[distance], out)
    return out


def stencil(y_ref, other_ref, v_ref, prev_ref, out_ref, pad_ref, slabs, scale, bases):
    tall = NY + 16
    for plane in range(6 * slabs):
        own = y_ref[plane * NY : (plane + 1) * NY, :]
        base = plane * tall
        pad_ref[base + 8 : base + 8 + NY, :] = own
        pad_ref[base : base + 8, :] = own[NY - 8 :, :]
        pad_ref[base + 8 + NY : base + tall, :] = own[0:8, :]
    along_z = jnp.dot(
        y_ref[0 : slabs * SLAB, :],
        circulant_z(),
        precision=lax.Precision.HIGH,
        preferred_element_type=f32,
    )
    below, above = bases()
    for slab in range(slabs):
        for plane in range(6):
            at = (slab * 6 + plane) * NY
            rows = slice(at, at + NY)
            base = (slab * 6 + plane) * tall + 8
            own = y_ref[rows, :]
            lap = along_z[rows, :]
            for distance in range(1, reach + 1):
                beside = pad_ref[base + distance : base + distance + NY, :]
                beside = beside + pad_ref[base - distance : base - distance + NY, :]
                for index in (plane - distance, plane + distance):
                    if index < 0:
                        spot = pl.multiple_of(below[slab] + (index + 6) * NY, 8)
                        beside = beside + other_ref[pl.ds(spot, NY), :]
                    elif index >= 6:
                        spot = pl.multiple_of(above[slab] + (index - 6) * NY, 8)
                        beside = beside + other_ref[pl.ds(spot, NY), :]
                    else:
                        spot = (slab * 6 + index) * NY
                        beside = beside + y_ref[spot : spot + NY, :]
                lap = lap + stencil_weights[distance] * beside
            if v_ref is None:
                value = scale * (-filter_center * own - 0.5 * lap)
            else:
                value = scale * ((v_ref[rows, :] - filter_center) * own - 0.5 * lap)
            if prev_ref is not None:
                value = value - prev_ref[rows, :]
            out_ref[rows, :] = value


def pack_kernel(dims, *refs):
    n, cap, nproj, foot, chunk = dims
    lanes = n * chunk
    sources, (pack_ref, p_ref), scratch = refs[:6], refs[6:8], refs[8:]
    off_ref, atom_ref, dmat_ref, r_ref, sems = scratch
    small = pack_ref.shape[0] - SMALL
    targets = (
        pack_ref.at[0:SLAB, :],
        p_ref,
        off_ref,
        atom_ref,
        dmat_ref,
        pack_ref.at[SLAB:small, :],
    )
    copies = [
        pltpu.make_async_copy(source, target, sems.at[index])
        for index, (source, target) in enumerate(zip(sources, targets))
    ]
    for copy in copies:
        copy.start()
    for copy in copies[2:]:
        copy.wait()
    lane = iota((1, lanes), 1) // nproj
    atoms = jnp.zeros((1, lanes), f32)
    starts = jnp.zeros((1, lanes), f32)
    for slot in range(n * cap):
        here = lane == slot
        atoms = jnp.where(here, atom_ref[slot % cap, slot // cap].astype(f32), atoms)
        starts = jnp.where(here, off_ref[slot % cap, slot // cap].astype(f32), starts)
    pack_ref[small + 1 : small + 2, :] = atoms
    pack_ref[small + 2 : small + 3, :] = starts
    pack_ref[small + 3 : small + 8, :] = jnp.zeros((5, 128), f32)
    count = dmat_ref.shape[1]
    for group in range(128 // count):
        block = dmat_ref[group * 2 * nproj : (group + 1) * 2 * nproj, :]
        pack_ref[small + 8 :, group * count : (group + 1) * count] = block
    copies[0].wait()
    copies[1].wait()
    pack_ref[small : small + 1, :] = partials(pack_ref, p_ref, off_ref, r_ref, dims)[0:1]


def gate_kernel(*refs):
    pass


def sort_kernel(*refs):
    packs, (pair_ref, v_ref) = refs[:-2], refs[-2:]
    small = packs[0].shape[0] - SMALL
    size = SLAB + SMALL
    for local, pack in enumerate(packs):
        pair_ref[local * size : local * size + SLAB, :] = pack[0:SLAB, :]
        pair_ref[local * size + SLAB : (local + 1) * size, :] = pack[small:, :]
        v_ref[local * (small - SLAB) : (local + 1) * (small - SLAB), :] = pack[SLAB:small, :]


def relay_kernel(x_ref, y_ref, top_ref, bottom_ref):
    rows = top_ref.shape[0]
    top_ref[...] = x_ref[0:rows, :]
    bottom_ref[...] = y_ref[rows:, :]


def begin_kernel(dims, info_ref, own_ref, got_ref, *refs):
    n, cap, nproj, foot, chunk = dims
    half = n // 2
    part_ref, y_ref, w_ref, c_ref, int_ref, other_ref, pad_ref, dmat_ref = refs
    lanes = n * chunk
    size = SLAB + SMALL
    c_rows, atom_rows, start_rows = [], [], []
    for group, source in enumerate((own_ref, got_ref)):
        for local in range(half):
            slab = local * size
            rows = slice(local * SLAB, (local + 1) * SLAB)
            target = other_ref if group else y_ref
            target[rows, :] = source[slab : slab + SLAB, :]
            small = slab + SLAB
            c_rows.append(source[small : small + 1, :])
            atom_rows.append(source[small + 1 : small + 2, :])
            if group == 0:
                start_rows.append(source[small + 2 : small + 3, :])
            dmat_ref[group * half + local] = source[small + 8 : small + SMALL, :]
    other_ref[half * SLAB :, :] = jnp.zeros((SLAB, 128), f32)
    c_ref[...] = by_owner(jnp.concatenate(c_rows, 0), n, chunk)
    atoms = by_owner(jnp.concatenate(atom_rows, 0), n, chunk)
    lane = iota((1, 128), 1)
    table = jnp.zeros((1, 128), jnp.int32)
    for local in range(half):
        int_ref[local : local + 1, :] = start_rows[local].astype(jnp.int32)
        for side in range(2):
            value = info_ref[(2 + side) * half + local]
            table = jnp.where(lane == side * half + local, value, table)
    table = jnp.where(lane == 2 * half, info_ref[4 * half + n], table)
    int_ref[half : half + 1, :] = table
    int_ref[half + 1 :, :] = jnp.zeros((8 - half - 1, 128), jnp.int32)

    def bases():
        return (
            [info_ref[2 * half + local] for local in range(half)],
            [info_ref[3 * half + local] for local in range(half)],
        )

    stencil(
        y_ref, other_ref, None, None, part_ref, pad_ref, half, 1.0 / filter_half_width, bases
    )
    square = (lanes, 128)
    diagonal = iota(square, 0) == iota(square, 1)
    ones = jnp.ones((128, 128), f32)
    column = iota(square, 1).astype(f32)
    count = 128 // (nproj // 2)
    shift = (iota(square, 0) % nproj // 2 * count).astype(f32)
    wide, picks = [], []
    for local in range(half):
        held = jnp.where(diagonal, atom_rows[local], 0.0)
        mine = jnp.dot(held, ones, precision=highest, preferred_element_type=f32)
        mine = jnp.round(mine)
        wide.append(mine)
        picks.append(jnp.where((column == shift + mine) & (mine >= 0.0), 1.0, 0.0))
    tall = half * chunk
    parity = iota((tall, 2 * nproj), 1) // nproj == iota((tall, 2 * nproj), 0) % 2
    spread = iota((2 * nproj, 128), 1) % nproj == iota((2 * nproj, 128), 0) % nproj
    spread = jnp.where(spread, 1.0, 0.0)
    for owner in range(n):
        rows = slice(owner * chunk, (owner + 1) * chunk)
        pick = jnp.concatenate([p[rows, :] for p in picks], 0)
        mine = jnp.concatenate([m[rows, :] for m in wide], 0)
        entries = lax.dot_general(
            pick,
            dmat_ref[info_ref[4 * half + owner]],
            (((1,), (1,)), ((), ())),
            precision=highest,
            preferred_element_type=f32,
        )
        entries = jnp.where(parity, entries, 0.0)
        block = jnp.dot(entries, spread, precision=highest, preferred_element_type=f32)
        same = (atoms[owner : owner + 1, :] == mine) & (mine >= 0.0)
        w_ref[owner * tall : (owner + 1) * tall, :] = jnp.where(same, block, 0.0)


def p_rows(p_refs, slab, slot, nproj, tile):
    ref, at = p_refs[slab], slot * nproj
    if at >= ref.shape[0]:
        ref, at = p_refs[slab + 1], at - ref.shape[0]
    return ref[at : at + nproj, tile * 128 : (tile + 1) * 128]


def swap_rows(x, step):
    if step == 4:
        return pltpu.roll(x, 4, 0)
    low = iota(x.shape, 0) // step % 2 == 0
    return jnp.where(low, pltpu.roll(x, 8 - step, 0), pltpu.roll(x, step, 0))


def column_sums(tiles):
    step = 4
    while step:
        low = iota(tiles[0].shape, 0) // step % 2 == 0
        pairs = [(tiles[t], tiles[t + step]) for t in range(step)]
        tiles = [
            jnp.where(low, a, b) + swap_rows(jnp.where(low, b, a), step) for a, b in pairs
        ]
        step //= 2
    return tiles[0]


def couple(dims, slabs, half, coefficients, w_ref, p_refs, start_of, out_ref, scale):
    n, cap, nproj, foot, chunk = dims
    for slab in slabs:
        for slot in range(n * cap):
            owner, k = slot // cap, slot % cap
            at = (owner * half + slab) * chunk + k * nproj
            back = jnp.sum(
                w_ref[at : at + nproj, :] * coefficients[owner : owner + 1, :],
                axis=1,
                keepdims=True,
            )
            back = jnp.broadcast_to(back * scale, (nproj, 128))
            tiles = [p_rows(p_refs, slab, slot, nproj, tile) * back for tile in range(foot)]
            spot = pl.ds(start_of(slab, slot), foot)
            out_ref[spot, :] = out_ref[spot, :] + column_sums(tiles)


def next_partials(dims, slabs, half, send_ref, p_refs, start_of, r_ref):
    n, cap, nproj, foot, chunk = dims
    lanes = n * chunk
    for index, slab in enumerate(slabs):
        for slot in range(n * cap):
            start = start_of(slab, slot)
            total = None
            for tile in range(foot):
                cells = jnp.broadcast_to(send_ref[pl.ds(start + tile, 1), :], (nproj, 128))
                term = p_rows(p_refs, slab, slot, nproj, tile) * cells
                total = term if total is None else total + term
            at = index * lanes + slot * nproj
            r_ref[at : at + nproj, :] = total
    row = lax.dot_general(
        jnp.ones((8, 128), f32),
        r_ref[...],
        (((1,), (1,)), ((), ())),
        precision=lax.Precision.HIGH,
        preferred_element_type=f32,
    )
    for index, slab in enumerate(slabs):
        send_ref[half * SLAB + slab : half * SLAB + slab + 1, :] = row[
            0:1, index * lanes : (index + 1) * lanes
        ]


def starts_from(int_s, nproj):
    return lambda slab, slot: slab * SLAB + int_s[slab, slot * nproj]


def potential_kernel(nband, table_ref, part_ref, y_ref, *refs):
    pieces, (out_ref, v_ref, int_s, sem) = refs[:nband], refs[nband:]
    copy = pltpu.make_async_copy(table_ref, int_s, sem)
    copy.start()
    copy.wait()
    scale = 1.0 / filter_half_width
    piece = NY // nband
    for back in range(nband):
        at = lax.rem(int_s[4, 8] - back + nband, nband) * piece
        for plane in range(part_ref.shape[0] // NY):
            spot = pl.ds(pl.multiple_of(plane * NY + at, 8), piece)
            value = pieces[back][plane * piece : (plane + 1) * piece, :]
            v_ref[spot, :] = value
            out_ref[spot, :] = part_ref[spot, :] + scale * (value * y_ref[spot, :])


def first_kernel(dims, slabs, *refs):
    n, cap, nproj, foot, chunk = dims
    half = n // 2
    int_ref, part_ref, w_ref, c_ref = refs[:4]
    p_refs, (send_ref, r_ref, int_s, sem) = refs[4:-4], refs[-4:]
    p_refs = (None,) * slabs[0] + tuple(p_refs)
    copy = pltpu.make_async_copy(int_ref, int_s, sem)
    copy.start()
    if slabs[0] == 0:
        send_ref[0 : half * SLAB, :] = part_ref[...]
        send_ref[half * SLAB :, :] = jnp.zeros((8, 128), f32)
    copy.wait()
    start_of = starts_from(int_s, nproj)
    scale = 1.0 / filter_half_width
    couple(dims, slabs, half, c_ref[...], w_ref, p_refs, start_of, send_ref, scale)
    next_partials(dims, slabs, half, send_ref, p_refs, start_of, r_ref)


def chip_kernel(dims, last, *refs):
    n, cap, nproj, foot, chunk = dims
    half = n // 2
    int_ref, y_ref, got_ref, prev_ref, v_ref, w_ref = refs[:6]
    p_refs = refs[6 : 7 + half]
    out_ref, other_ref, pad_ref, int_s, sem = refs[7 + half : 12 + half]
    copy = pltpu.make_async_copy(int_ref, int_s, sem)
    copy.start()
    other_ref[0 : half * SLAB, :] = got_ref[0 : half * SLAB, :]
    other_ref[half * SLAB :, :] = jnp.zeros((SLAB, 128), f32)
    slabs = range(1 if last else half)
    scale = 2.0 / filter_half_width

    def bases():
        copy.wait()
        return (
            [int_s[half, local] for local in range(half)],
            [int_s[half, half + local] for local in range(half)],
        )

    stencil(y_ref, other_ref, v_ref, prev_ref, out_ref, pad_ref, len(slabs), scale, bases)
    below = slice(half * SLAB, half * SLAB + half)
    rows = jnp.concatenate([y_ref[below, :], got_ref[below, :]], 0)
    coefficients = by_owner(rows, n, chunk)
    start_of = starts_from(int_s, nproj)
    couple(dims, slabs, half, coefficients, w_ref, p_refs, start_of, out_ref, scale)
    if not last:
        out_ref[half * SLAB :, :] = jnp.zeros((8, 128), f32)
        next_partials(dims, slabs, half, out_ref, p_refs, start_of, refs[12 + half])


def chip_table(n):
    half = n // 2
    table = np.zeros((n, 4 * half + n), np.int32)
    for device in range(n):
        chip, core = device // 2, device % 2
        for local in range(half):
            there = chip ^ local
            same = local * SLAB
            far = there + (1 if core else -1)
            cross = (far ^ chip) * SLAB if 0 <= far < half else half * SLAB
            table[device, 2 * half + local] = same if core else cross
            table[device, 3 * half + local] = cross if core else same
        for owner in range(n):
            table[device, 4 * half + owner] = owner % 2 * half if core == 0 else (1 - owner % 2) * half
            table[device, 4 * half + owner] += owner // 2 ^ chip
    return table


def chip_form(psi, potential, projectors, offsets, intersection, dmat):
    n = lax.axis_size("domain")
    nband = lax.axis_size("band")
    cap, nproj = projectors.shape[2], projectors.shape[3]
    foot = projectors.shape[4] // 128
    chunk = cap * nproj
    lanes = n * chunk
    half = n // 2
    dims = (n, cap, nproj, foot, chunk)
    p = projectors.reshape(lanes, foot * 128)
    v_piece = potential.reshape(-1, 128)
    couplings = dmat.transpose(1, 2, 0).reshape(nproj * nproj, dmat.shape[0])
    domain = lax.axis_index("domain")
    info = jnp.concatenate(
        [
            lax.dynamic_slice_in_dim(jnp.asarray(chip_table(n)), domain, 1, 0)[0],
            lax.axis_index("band").astype(jnp.int32)[None],
        ]
    )
    params = pltpu.CompilerParams(vmem_limit_bytes=40 * 1024 * 1024)
    HBM = pl.BlockSpec(memory_space=pltpu.HBM)
    small = pl.CostEstimate(flops=1, bytes_accessed=1, transcendentals=0)
    large = pl.CostEstimate(flops=10**10, bytes_accessed=1, transcendentals=0)
    larger = pl.CostEstimate(flops=10**10, bytes_accessed=1, transcendentals=0)

    def shape(rows, dtype=f32):
        return jax.ShapeDtypeStruct((rows, 128), dtype)

    def swap(x, step):
        return lax.ppermute(x, "domain", [(i, i ^ step) for i in range(n)])

    sources = (psi.reshape(SLAB, 128), p, offsets[0].T, intersection[0].T, couplings, v_piece)
    sources = [pltpu.with_memory_space_constraint(x, pltpu.HBM) for x in sources]
    pack, p = pl.pallas_call(
        functools.partial(pack_kernel, dims),
        out_shape=(
            shape(SLAB + v_piece.shape[0] + SMALL),
            jax.ShapeDtypeStruct(p.shape, f32),
        ),
        in_specs=[HBM] * 6,
        out_specs=(VMEM, VMEM),
        scratch_shapes=[
            pltpu.SMEM((cap, n), jnp.int32),
            pltpu.SMEM((cap, n), jnp.int32),
            pltpu.VMEM(couplings.shape, f32),
            pltpu.VMEM((lanes, 128), f32),
            pltpu.SemaphoreType.DMA((6,)),
        ],
        compiler_params=params,
        cost_estimate=small,
        name="pack",
    )(*sources)
    packs = [pack] + [swap(pack, 2 * local) for local in range(1, half)]
    p = pl.pallas_call(
        gate_kernel,
        out_shape=jax.ShapeDtypeStruct(p.shape, f32),
        in_specs=[VMEM, VMEM],
        out_specs=VMEM,
        input_output_aliases={1: 0},
        compiler_params=params,
        cost_estimate=small,
        name="gate",
    )(packs[3], p)
    own, v_piece = pl.pallas_call(
        sort_kernel,
        out_shape=(shape(half * (SLAB + SMALL)), shape(half * v_piece.shape[0])),
        in_specs=[VMEM] * half,
        out_specs=(VMEM, VMEM),
        compiler_params=params,
        cost_estimate=small,
        name="sort",
    )(*packs)
    got = swap(own, 1)
    pieces = [v_piece]
    for back in range(1, nband):
        ring = [(i, (i + back) % nband) for i in range(nband)]
        pieces.append(lax.ppermute(v_piece, "band", ring))
    p_x, p_y = swap(p, 2), swap(p, 4)
    halves = (jax.ShapeDtypeStruct((lanes // 2, foot * 128), f32),) * 2
    top, bottom = pl.pallas_call(
        relay_kernel,
        out_shape=halves,
        in_specs=[VMEM] * 2,
        out_specs=(VMEM, VMEM),
        compiler_params=params,
        cost_estimate=large,
        name="relay",
    )(p_x, p_y)
    all_p = [p, p_x, p_y, swap(top, 4), swap(bottom, 2)]
    other = pltpu.VMEM(((half + 1) * SLAB, 128), f32)
    padded = pltpu.VMEM((half * 6 * (NY + 16), 128), f32)
    row_scratch = pltpu.VMEM((half * lanes, 128), f32)
    ints = [pltpu.SMEM((8, 128), jnp.int32), pltpu.SemaphoreType.DMA(())]
    part, previous, w, c, table = pl.pallas_call(
        functools.partial(begin_kernel, dims),
        out_shape=(
            shape(half * SLAB),
            shape(half * SLAB),
            shape(half * lanes),
            shape(n),
            shape(8, jnp.int32),
        ),
        in_specs=[SMEM] + [VMEM] * 2,
        out_specs=(VMEM,) * 5,
        scratch_shapes=[other, padded, pltpu.VMEM((n, 2 * nproj, 128), f32)],
        compiler_params=params,
        cost_estimate=small,
        name="begin",
    )(info, own, got)
    sent = shape(half * SLAB + 8)
    part, v = pl.pallas_call(
        functools.partial(potential_kernel, nband),
        out_shape=(shape(half * SLAB), shape(half * SLAB)),
        in_specs=[VMEM] * (3 + nband),
        out_specs=(VMEM, VMEM),
        scratch_shapes=ints,
        compiler_params=params,
        cost_estimate=larger,
        name="potential",
    )(table, part, previous, *pieces)
    y = part
    for slabs in (range(half - 1), range(half - 1, half)):
        start, late = slabs[0], slabs[0] > 0
        some_p = all_p[start:] if late else all_p[: half - 1]
        y = pl.pallas_call(
            functools.partial(first_kernel, dims, slabs),
            out_shape=sent,
            in_specs=[VMEM] * (4 + len(some_p)),
            out_specs=VMEM,
            scratch_shapes=[pltpu.VMEM((len(slabs) * lanes, 128), f32)] + ints,
            input_output_aliases={1: 0} if late else {},
            compiler_params=params,
            cost_estimate=small,
            name="first_late" if late else "first",
        )(table, y, w, c, *some_p)
    for degree in range(1, DEGREE):
        last = degree == DEGREE - 1
        following = pl.pallas_call(
            functools.partial(chip_kernel, dims, last),
            out_shape=shape(SLAB) if last else sent,
            in_specs=[VMEM] * (7 + half),
            out_specs=VMEM,
            scratch_shapes=[other, padded] + ints + ([] if last else [row_scratch]),
            compiler_params=params,
            name="last" if last else "next",
        )(table, y, swap(y, 1), previous, v, w, *all_p)
        previous, y = y, following
    return y.reshape(psi.shape)


def shards(psi, potential, projectors, offsets, intersection, dmat):
    n = lax.axis_size("domain")
    nband = lax.axis_size("band")
    fits = n == 8 and potential.shape[1] % 8 == 0 and nband <= 8
    form = chip_form if fits else slab_form
    return form(psi, potential, projectors, offsets, intersection, dmat)


def solution(mesh):
    return jax.shard_map(
        shards,
        mesh=mesh,
        in_specs=(
            P("band", "domain", None, None),
            P("domain", "band", None),
            P("domain", None, None, None, None),
            P("domain", None, None),
            P("domain", None, None),
            P("domain", None, None),
        ),
        out_specs=P("band", "domain", None, None),
        check_vma=False,
    )
```
